32 devices in a mesh: dp: 16 (over z, y, x), fsdp: 2 (over core).
Axes of the slice: x: 2, y: 2, z: 4, core: 2. Of those that a mesh axis runs over, the one named last changes fastest.
Arguments:
- tokens: bfloat16 [32, 1024, 768], P(('dp', 'fsdp')), may hold values from -6 to 6
- cotangent: bfloat16 [32, 1024, 768], P(('dp', 'fsdp')), may hold values from -6 to 6
- segments: int32 [32, 1024], P(('dp', 'fsdp')), may hold values from 0 to 15, never falling along the last dimension, each value on 1 to 128 neighbouring positions
- keep_mask: int32 [32, 1024], P(('dp', 'fsdp')), may hold values 0 or 1
- qkv_weight: float32 [2, 768, 2304], P(None, 'fsdp'), may hold values from -0.21875 to 0.21875
- qkv_first: float32 [2, 768, 2304], P(None, 'fsdp'), may hold values from -512 to 512
- qkv_second: float32 [2, 768, 2304], P(None, 'fsdp'), may hold values from 4096 to 65536
- proj_weight: float32 [2, 768, 768], P(None, 'fsdp'), may hold values from -0.625 to 0.625
- proj_first: float32 [2, 768, 768], P(None, 'fsdp'), may hold values from -512 to 512
- proj_second: float32 [2, 768, 768], P(None, 'fsdp'), may hold values from 4096 to 65536
- up_weight: float32 [2, 768, 3072], P(None, 'fsdp'), may hold values from -0.21875 to 0.21875
- up_first: float32 [2, 768, 3072], P(None, 'fsdp'), may hold values from -512 to 512
- up_second: float32 [2, 768, 3072], P(None, 'fsdp'), may hold values from 4096 to 65536
- down_weight: float32 [2, 3072, 768], P(None, 'fsdp'), may hold values from -0.109375 to 0.109375
- down_first: float32 [2, 3072, 768], P(None, 'fsdp'), may hold values from -512 to 512
- down_second: float32 [2, 3072, 768], P(None, 'fsdp'), may hold values from 4096 to 65536
- norm_gains: float32 [2, 768, 4], P(None, 'fsdp'), may hold values from 0.5 to 1.5
- gains_first: float32 [2, 768, 4], P(None, 'fsdp'), may hold values from -512 to 512
- gains_second: float32 [2, 768, 4], P(None, 'fsdp'), may hold values from 4096 to 65536
Outputs:
- output: bfloat16 [32, 1024, 768], P(('dp', 'fsdp'))
- input_grad: float32 [32, 1024, 768], P(('dp', 'fsdp'))
- new_qkv_weight: float32 [2, 768, 2304], P(None, 'fsdp')
- new_qkv_first: float32 [2, 768, 2304], P(None, 'fsdp')
- new_qkv_second: float32 [2, 768, 2304], P(None, 'fsdp')
- new_proj_weight: float32 [2, 768, 768], P(None, 'fsdp')
- new_proj_first: float32 [2, 768, 768], P(None, 'fsdp')
- new_proj_second: float32 [2, 768, 768], P(None, 'fsdp')
- new_up_weight: float32 [2, 768, 3072], P(None, 'fsdp')
- new_up_first: float32 [2, 768, 3072], P(None, 'fsdp')
- new_up_second: float32 [2, 768, 3072], P(None, 'fsdp')
- new_down_weight: float32 [2, 3072, 768], P(None, 'fsdp')
- new_down_first: float32 [2, 3072, 768], P(None, 'fsdp')
- new_down_second: float32 [2, 3072, 768], P(None, 'fsdp')
- new_norm_gains: float32 [2, 768, 4], P(None, 'fsdp')
- new_gains_first: float32 [2, 768, 4], P(None, 'fsdp')
- new_gains_second: float32 [2, 768, 4], P(None, 'fsdp')
The draws below stay inside these ranges and needn't reach their ends.
Inputs may be any that keep to these rules, and one draw needn't show every extreme that they name: `segments`: in each packed sequence the ids never fall, and each image holds 1 to 128 positions.
All inputs are finite; a program needn't handle non-finite values. No bound on the sum of `keep_mask` on one device may be relied on, other than what follows from the above.
Results may differ from the reference program's by a relative error of at most 0.035.
Values may be sent and summed in bfloat16 or wider, within the bound.
A program may use at most 512 MiB of HBM per device.

```python
import math
import jax
import jax.numpy as jnp
import numpy as np
from jax import lax

D = 768
HEADS = 12
HEAD_DIM = 64
FF = 3072
LAYERS = 2
SEQ = 1024
STEP = 5
ROWS = 32
TOKENS = 32768


def place_ends(values, rng, least, high):
    longest = values.shape.index(max(values.shape))
    spots = []
    for shift in (0, 1):
        where = [jax.random.randint(jax.random.fold_in(rng, axis), (), 0, length) for axis, length in enumerate(values.shape)]
        where[longest] = (where[longest] + shift) % values.shape[longest]
        spots.append(tuple(where))
    return values.at[spots[0]].set(least).at[spots[1]].set(high)


def level_of(stream_key, extent, cuts, smallest, high):
    level = 1.0
    for axis_at, blocks in cuts:
        draws = jax.random.uniform(jax.random.fold_in(jax.random.fold_in(stream_key, 6), axis_at), (blocks,), jnp.float32, smallest / len(cuts), high / len(cuts))
        level = level * jnp.repeat(jnp.exp(draws), extent[axis_at] // blocks).reshape((-1,) + (1,) * (len(extent) - 1 - axis_at))
    return level


def length_profile(amount, total, reach, skew):
    loads = [(1 << 20) // math.isqrt(standing ** skew) + 1 for standing in range(2, amount + 1)]
    spare, counts = total - reach - (amount - 1), [1] * (amount - 1)
    while spare > 0:
        free = [i for i in range(amount - 1) if counts[i] < reach]
        pool, budget = sum([loads[i] for i in free]), spare
        for i in free:
            more = min(reach - counts[i], max(1, budget * loads[i] // pool), spare)
            counts[i] = counts[i] + more
            spare = spare - more
    return np.array([reach] + counts)


def ragged_sizes(rng, amount, total, limit, slope):
    if amount == 2:
        one = jax.random.randint(rng, (), max(1, total - limit), min(limit, total - 1) + 1)
        return jnp.stack([one, total - one])
    tallies = jnp.asarray(length_profile(amount, total, limit, slope), jnp.int32)
    couples = (amount - 1) // 2
    source_of, receiver = tallies[1:1 + 2 * couples:2], tallies[2:2 + 2 * couples:2]
    slack = jnp.minimum(source_of - 1, limit - receiver)
    moved = jax.random.randint(jax.random.fold_in(rng, 1), (couples,), 0, 1 << 20) % (slack + 1)
    tallies = tallies.at[1:1 + 2 * couples:2].set(source_of - moved).at[2:2 + 2 * couples:2].set(receiver + moved)
    return tallies[jax.random.permutation(jax.random.fold_in(rng, 2), amount)]


def bell_draw(rng, shape, scale, bound, split=(), held_as=jnp.bfloat16):
    values = jax.random.normal(rng, shape, jnp.float32) * scale
    if len(split) > 0:
        values = level_of(rng, shape, split, -0.22, 0.18) * values
    return jnp.clip(values, min=-bound, max=bound).astype(held_as)


def setup_inputs(seed: int = 0) -> dict:
    key_of = jax.random.split(jax.random.key(seed), 20)
    tokens = bell_draw(key_of[0], (ROWS, SEQ, D), 1.0, 6.0, ((0, 32),))
    cotangent = bell_draw(key_of[1], (ROWS, SEQ, D), 1.0, 6.0, ((0, 32),))
    segments = jax.vmap(lambda own: jnp.searchsorted(jnp.cumsum(ragged_sizes(own, 16, SEQ, SEQ // 8, 0)), jnp.arange(SEQ), side="right"))(jax.random.split(key_of[2], ROWS)).reshape((ROWS, SEQ)).astype(jnp.int32)
    keep_mask = place_ends((jax.random.randint(key_of[3], (ROWS, SEQ), 0, 4) < 3).astype(jnp.int32), jax.random.fold_in(key_of[3], 1), 0, 1)
    qkv_weight = bell_draw(key_of[4], (LAYERS, D, 3 * D), D ** -0.5, 0.21875, ((1, 2),), jnp.float32)
    qkv_first = bell_draw(key_of[5], (LAYERS, D, 3 * D), (0.5 * TOKENS ** 0.5), 512.0, ((1, 2),), jnp.float32)
    qkv_second = jnp.clip(jnp.exp(math.log(65536.0) - 2.7725887 * jax.random.uniform(key_of[6], (LAYERS, D, 3 * D), jnp.float32) ** level_of(key_of[6], (LAYERS, D, 3 * D), ((1, 2),), -0.2, 0.2)), 4096.0, 65536.0)
    proj_weight = bell_draw(key_of[7], (LAYERS, D, D), (D // 8) ** -0.5, 0.625, ((1, 2),), jnp.float32)
    proj_first = bell_draw(key_of[8], (LAYERS, D, D), (0.5 * TOKENS ** 0.5), 512.0, ((1, 2),), jnp.float32)
    proj_second = jnp.clip(jnp.exp(math.log(65536.0) - 2.7725887 * jax.random.uniform(key_of[9], (LAYERS, D, D), jnp.float32) ** level_of(key_of[9], (LAYERS, D, D), ((1, 2),), -0.2, 0.2)), 4096.0, 65536.0)
    up_weight = bell_draw(key_of[10], (LAYERS, D, FF), D ** -0.5, 0.21875, ((1, 2),), jnp.float32)
    up_first = bell_draw(key_of[11], (LAYERS, D, FF), (0.5 * TOKENS ** 0.5), 512.0, ((1, 2),), jnp.float32)
    up_second = jnp.clip(jnp.exp(math.log(65536.0) - 2.7725887 * jax.random.uniform(key_of[12], (LAYERS, D, FF), jnp.float32) ** level_of(key_of[12], (LAYERS, D, FF), ((1, 2),), -0.2, 0.2)), 4096.0, 65536.0)
    down_weight = bell_draw(key_of[13], (LAYERS, FF, D), FF ** -0.5, 0.109375, ((1, 2),), jnp.float32)
    down_first = bell_draw(key_of[14], (LAYERS, FF, D), (0.5 * TOKENS ** 0.5), 512.0, ((1, 2),), jnp.float32)
    down_second = jnp.clip(jnp.exp(math.log(65536.0) - 2.7725887 * jax.random.uniform(key_of[15], (LAYERS, FF, D), jnp.float32) ** level_of(key_of[15], (LAYERS, FF, D), ((1, 2),), -0.2, 0.2)), 4096.0, 65536.0)
    norm_gains = jnp.clip(1.0 + 0.1 * jax.random.normal(key_of[16], (LAYERS, D, 4), jnp.float32), 0.5, 1.5)
    gains_first = bell_draw(key_of[17], (LAYERS, D, 4), (0.5 * TOKENS ** 0.5), 512.0, ((1, 2),), jnp.float32)
    gains_second = jnp.clip(jnp.exp(math.log(65536.0) - 2.7725887 * jax.random.uniform(key_of[18], (LAYERS, D, 4), jnp.float32) ** level_of(key_of[18], (LAYERS, D, 4), ((1, 2),), -0.2, 0.2)), 4096.0, 65536.0)
    return {"tokens": tokens, "cotangent": cotangent, "segments": segments, "keep_mask": keep_mask, "qkv_weight": qkv_weight, "qkv_first": qkv_first, "qkv_second": qkv_second, "proj_weight": proj_weight, "proj_first": proj_first, "proj_second": proj_second, "up_weight": up_weight, "up_first": up_first, "up_second": up_second, "down_weight": down_weight, "down_first": down_first, "down_second": down_second, "norm_gains": norm_gains, "gains_first": gains_first, "gains_second": gains_second}


@jax.custom_vjp
def low(v):
    return lax.optimization_barrier(v.astype(jnp.bfloat16)).astype(jnp.float32)

@jax.custom_vjp
def low_back(v):
    return v

def low_keep(v):
    return (low(v), None)

def low_pass(kept, grad):
    return (grad,)

def back_keep(v):
    return (v, None)

def back_low(kept, grad):
    return (low(grad),)
low.defvjp(low_keep, low_pass)
low_back.defvjp(back_keep, back_low)
highest = lax.Precision.HIGHEST
norm_eps = 1e-06
adam_eps = 1e-08

def layer_norm(values, gain):
    average = lax.optimization_barrier(jnp.mean(values, axis=-1, keepdims=True))
    centred = values - average
    spread = lax.optimization_barrier(jnp.mean(centred * centred, axis=-1, keepdims=True))
    return centred * lax.rsqrt(spread + norm_eps) * gain

def gelu_tanh(values):
    return jax.nn.gelu(values, approximate=True)

def attend_row(packed):
    queries, keys_all, values, seg_row, keep_row = packed
    scores = low_back(jnp.einsum('qhd,khd->hqk', queries, keys_all, precision=highest) * HEAD_DIM ** (-0.5))
    positions = jnp.arange(SEQ)
    diagonal = positions[:, None] == positions[None, :]
    allowed = (seg_row[:, None] == seg_row[None, :]) & ((keep_row[None, :] == 1) | diagonal)
    masked = jnp.where(allowed[None], scores, -1e+30)
    probs = low(jax.nn.softmax(masked, axis=-1))
    return low(low_back(jnp.einsum('hqk,khd->qhd', probs, values, precision=highest)))

def residual_block(hidden, weight_set, seg_part, keep_part):
    joint_mat, proj_mat, upper_mat, lower_mat, gain_set = [low(weight_arr) for weight_arr in weight_set]
    count_rows = hidden.shape[0]
    normed = low(layer_norm(hidden, gain_set[:, 0]))
    mixed = low_back(jnp.einsum('rsd,de->rse', normed, joint_mat, precision=highest))
    mixed = mixed.reshape(count_rows, SEQ, 3, HEADS, HEAD_DIM)
    queries = low(layer_norm(mixed[:, :, 0], gain_set[:, 2].reshape(HEADS, HEAD_DIM)))
    keys_all = low(layer_norm(mixed[:, :, 1], gain_set[:, 3].reshape(HEADS, HEAD_DIM)))
    values = low(mixed[:, :, 2])
    attended = lax.map(jax.checkpoint(attend_row), (queries, keys_all, values, seg_part, keep_part))
    attended = attended.reshape(count_rows, SEQ, D)
    middle = hidden + low_back(jnp.einsum('rsd,de->rse', attended, proj_mat, precision=highest))
    normed_two = low(layer_norm(middle, gain_set[:, 1]))
    before = low_back(jnp.einsum('rsd,df->rsf', normed_two, upper_mat, precision=highest))
    active = low(gelu_tanh(before))
    return middle + low_back(jnp.einsum('rsf,fd->rsd', active, lower_mat, precision=highest))

def forward(hidden, weight_sets, segments, keep_mask):
    count_rows = hidden.shape[0]
    per_group = 4 if count_rows % 4 == 0 else 1

    def run_group(packed):
        inputs_part, seg_part, keep_part = packed
        for layer_index in range(LAYERS):
            layer_set = [weight_arr[layer_index] for weight_arr in weight_sets]
            inputs_part = residual_block(inputs_part, layer_set, seg_part, keep_part)
        return inputs_part
    shaped = (hidden.reshape(count_rows // per_group, per_group, SEQ, D), segments.reshape(count_rows // per_group, per_group, SEQ), keep_mask.reshape(count_rows // per_group, per_group, SEQ))
    result = lax.map(jax.checkpoint(run_group), shaped)
    return result.reshape(count_rows, SEQ, D)

def reference(tokens, cotangent, segments, keep_mask, qkv_weight, qkv_first, qkv_second, proj_weight, proj_first, proj_second, up_weight, up_first, up_second, down_weight, down_first, down_second, norm_gains, gains_first, gains_second):
    masters = (qkv_weight, proj_weight, up_weight, down_weight, norm_gains)
    firsts = (qkv_first, proj_first, up_first, down_first, gains_first)
    seconds = (qkv_second, proj_second, up_second, down_second, gains_second)

    def run_forward(inputs, weight_sets):
        return forward(inputs, weight_sets, segments, keep_mask)
    hidden_out, pullback = jax.vjp(run_forward, tokens.astype(jnp.float32), masters)
    input_grad, gradients = pullback(cotangent.astype(jnp.float32))
    output = hidden_out.astype(jnp.bfloat16)
    corr_one = 1.0 - 0.5 ** STEP
    corr_two = 1.0 - 0.5 ** STEP
    updated = []
    for kind_index in range(5):
        grad_now = gradients[kind_index]
        first_new = 0.5 * firsts[kind_index] + 0.5 * grad_now
        second_new = 0.5 * seconds[kind_index] + 0.5 * grad_now * grad_now
        rate_now = 0.5 if kind_index == 4 else D ** (-0.5)
        decay_now = 0.0 if kind_index == 4 else 0.1
        weight_old = masters[kind_index]
        weight_new = weight_old - rate_now * (first_new / corr_one / (jnp.sqrt(second_new / corr_two) + adam_eps) + decay_now * weight_old)
        updated.append((weight_new, first_new, second_new))
    return (output, input_grad, updated[0][0], updated[0][1], updated[0][2], updated[1][0], updated[1][1], updated[1][2], updated[2][0], updated[2][1], updated[2][2], updated[3][0], updated[3][1], updated[3][2], updated[4][0], updated[4][1], updated[4][2])
```

```python
import functools
import math

import jax
import jax.numpy as jnp
from jax import lax
from jax.experimental import pallas as pl
from jax.experimental.pallas import tpu as pltpu
from jax.sharding import PartitionSpec as P

D = 768
HEADS = 12
HEAD_DIM = 64
STEP = 5
BF = jnp.bfloat16
F32 = jnp.float32
norm_eps = 1e-06
adam_eps = 1e-08
VMEM_LIMIT = 60 * 1024 * 1024
LOG2E = 1.4426950408889634
MASKED = -1e30


def dot(a, b):
    return lax.dot_general(a, b, (((1,), (0,)), ((), ())), preferred_element_type=F32)


def dot_nt(a, b):
    return lax.dot_general(a, b, (((1,), (1,)), ((), ())), preferred_element_type=F32)


def dot_tn(a, b):
    return lax.dot_general(a, b, (((0,), (0,)), ((), ())), preferred_element_type=F32)


def split_dot(x, mat):
    high = x.astype(BF)
    low = (x - high.astype(F32)).astype(BF)
    return dot(high, mat) + dot(low, mat)


def normalise(values):
    average = jnp.mean(values, axis=-1, keepdims=True)
    centred = values - average
    spread = jnp.mean(centred * centred, axis=-1, keepdims=True)
    scale = lax.rsqrt(spread + norm_eps)
    return centred * scale, scale


def norm_back(grad, gain, unit, scale):
    scaled = grad * gain
    first = jnp.mean(scaled, axis=-1, keepdims=True)
    second = jnp.mean(scaled * unit, axis=-1, keepdims=True)
    return scale * (scaled - first - unit * second)


def column_sum(x):
    return jnp.sum(x.reshape(x.shape[0] // 8, 8, x.shape[1]), axis=0)


def load_halves(own, mine_ref, other_ref, full_ref, sems):
    half = full_ref.shape[0] // 2
    here = pl.multiple_of(own * half, half)
    there = pl.multiple_of((1 - own) * half, half)
    return (
        pltpu.make_async_copy(mine_ref, full_ref.at[pl.ds(here, half)], sems.at[0]),
        pltpu.make_async_copy(other_ref, full_ref.at[pl.ds(there, half)], sems.at[1]),
    )


def start_all(copies):
    for copy in copies:
        copy.start()


def wait_all(copies):
    for copy in copies:
        copy.wait()


def whole(shape):
    zeros = (0,) * len(shape)
    return pl.BlockSpec(shape, lambda *_: zeros, pipeline_mode=pl.Buffered(1))


ANY = pl.BlockSpec(memory_space=pl.ANY)
SMEM = pl.BlockSpec(memory_space=pltpu.SMEM)


def params(steps=1):
    return pltpu.CompilerParams(
        dimension_semantics=("arbitrary",) * steps, vmem_limit_bytes=VMEM_LIMIT
    )


def qkv_kernel(
    own_ref, h_ref, gain_ref, heads_ref, spread_ref, mine_ref, other_ref,
    normed_ref, unit_q_ref, unit_k_ref, q_ref, k_ref, v_ref, scale_q_ref, scale_k_ref,
    weight, sems,
):
    copies = load_halves(own_ref[0], mine_ref, other_ref, weight, sems)

    @pl.when(pl.program_id(0) == 0)
    def _():
        start_all(copies)

    unit, _ = normalise(h_ref[...].astype(F32))
    normed = (unit * gain_ref[0:1, :]).astype(BF)
    normed_ref[...] = normed

    @pl.when(pl.program_id(0) == 0)
    def _():
        wait_all(copies)

    v_ref[...] = dot(normed, weight[:, 2 * D :]).astype(BF)
    for part, unit_ref, out_ref, scale_ref in (
        (0, unit_q_ref, q_ref, scale_q_ref),
        (1, unit_k_ref, k_ref, scale_k_ref),
    ):
        raw = dot(normed, weight[:, part * D : (part + 1) * D])
        average = split_dot(raw, heads_ref[...]) * (1.0 / HEAD_DIM)
        centred = raw - split_dot(average, spread_ref[...])
        spread = split_dot(centred * centred, heads_ref[...]) * (1.0 / HEAD_DIM)
        scale = lax.rsqrt(spread + norm_eps)
        unit = centred * split_dot(scale, spread_ref[...])
        unit_ref[...] = unit.astype(BF)
        out_ref[...] = (unit * gain_ref[2 + part : 3 + part, :]).astype(BF)
        scale_ref[...] = scale


def qkv_forward(own, h, gains, heads, spread, mine, other):
    rows = h.shape[0]
    block = min(512, rows)
    row = lambda width: pl.BlockSpec((block, width), lambda i: (i, 0))
    outs = [(D, BF)] * 6 + [(128, F32)] * 2
    return pl.pallas_call(
        qkv_kernel,
        name="qkv_forward",
        grid=(rows // block,),
        in_specs=[SMEM, row(D), whole(gains.shape), whole(heads.shape), whole(spread.shape), ANY, ANY],
        out_specs=[row(w) for w, _ in outs],
        out_shape=[jax.ShapeDtypeStruct((rows, w), t) for w, t in outs],
        scratch_shapes=[pltpu.VMEM((D, 3 * D), BF), pltpu.SemaphoreType.DMA((2,))],
        compiler_params=params(),
    )(own, h, gains, heads, spread, mine, other)


def window_start(block, count, reach):
    return jnp.clip(block - 1, 0, count - reach)


def pair_stack(x, low_lanes):
    zero = jnp.zeros_like(x)
    return jnp.concatenate([jnp.where(low_lanes, x, zero), jnp.where(low_lanes, zero, x)], axis=0)


def mix_kernel(
    tile, reach,
    own_ref, h_ref, q_ref, k_ref, v_ref, seg_ref, code_ref, gain_ref,
    proj_mine, proj_other, up_mine, up_other, down_mine, down_other,
    attended_ref, middle_ref, before_ref, out_ref,
    proj, up, down, sems,
):
    step = pl.program_id(0)
    own = own_ref[0]
    proj_copies = load_halves(own, proj_mine, proj_other, proj, sems.at[0])
    up_copies = load_halves(own, up_mine, up_other, up, sems.at[1])
    down_copies = load_halves(own, down_mine, down_other, down, sems.at[2])

    @pl.when(step == 0)
    def _():
        start_all(proj_copies)
        start_all(up_copies)
        start_all(down_copies)

    rows = h_ref.shape[0]
    count = k_ref.shape[0] // tile
    keys = reach * tile
    factor = LOG2E * HEAD_DIM ** (-0.5)
    low_lanes = lax.broadcasted_iota(jnp.int32, (tile, 128), 1) < HEAD_DIM

    def attend(inner, carry):
        block = step * (rows // tile) + inner
        first = pl.multiple_of(window_start(block, count, reach) * tile, tile)
        here = pl.multiple_of(inner * tile, tile)
        seg = seg_ref[pl.ds(here, tile), :]
        code = code_ref[:, pl.ds(first, keys)]
        query_at = block * tile + lax.broadcasted_iota(jnp.int32, (tile, keys), 0)
        key_at = first + lax.broadcasted_iota(jnp.int32, (tile, keys), 1)
        bias = jnp.where((seg == code) | (query_at == key_at), 0.0, MASKED)
        bias = jnp.concatenate([bias, bias], axis=0)
        for pair in range(HEADS // 2):
            lanes = slice(pair * 128, (pair + 1) * 128)
            queries = pair_stack(q_ref[pl.ds(here, tile), lanes], low_lanes)
            scores = dot_nt(queries, k_ref[pl.ds(first, keys), lanes])
            expo = jnp.exp2(scores * factor + bias)
            total = jnp.sum(expo, axis=-1, keepdims=True)
            mixed = dot(expo.astype(BF), v_ref[pl.ds(first, keys), lanes]) / total
            attended_ref[pl.ds(here, tile), lanes] = jnp.where(
                low_lanes, mixed[:tile], mixed[tile:]
            ).astype(BF)
        return carry

    lax.fori_loop(0, rows // tile, attend, 0)

    @pl.when(step == 0)
    def _():
        wait_all(proj_copies)

    middle = h_ref[...].astype(F32) + dot(attended_ref[...], proj[...])
    middle_ref[...] = middle
    unit, _ = normalise(middle)
    normed = (unit * gain_ref[1:2, :]).astype(BF)

    @pl.when(step == 0)
    def _():
        wait_all(up_copies)
        wait_all(down_copies)

    result = middle
    for part in range(up.shape[1] // D):
        lanes = slice(part * D, (part + 1) * D)
        before = dot(normed, up[:, lanes])
        before_ref[:, lanes] = before.astype(BF)
        active = jax.nn.gelu(before, approximate=True).astype(BF)
        result = result + dot(active, down[lanes, :])
    out_ref[...] = result.astype(out_ref.dtype)


def mix_forward(own, h, q, k, v, seg, code, gains, shards, out_type):
    rows = h.shape[0]
    block = min(512, rows)
    tile = min(128, rows)
    reach = min(3, rows // tile)
    width = shards[2].shape[1]
    row = lambda w: pl.BlockSpec((block, w), lambda i: (i, 0))
    outs = [(D, BF), (D, F32), (width, BF), (D, out_type)]
    return pl.pallas_call(
        functools.partial(mix_kernel, tile, reach),
        name="mix_forward",
        grid=(rows // block,),
        in_specs=[SMEM, row(D), row(D), whole(k.shape), whole(v.shape), row(1), whole(code.shape), whole(gains.shape)]
        + [ANY] * 6,
        out_specs=[row(w) for w, _ in outs],
        out_shape=[jax.ShapeDtypeStruct((rows, w), t) for w, t in outs],
        scratch_shapes=[
            pltpu.VMEM((D, D), BF),
            pltpu.VMEM((D, width), BF),
            pltpu.VMEM((width, D), BF),
            pltpu.SemaphoreType.DMA((3, 2)),
        ],
        compiler_params=params(),
    )(own, h, q, k, v, seg, code, gains, *shards)


def ffn_back_kernel(
    blocks, aliased,
    own_ref, dh_ref, before_ref, middle_ref, gain_ref, up_mine, up_other, down_mine, down_other,
    *rest,
):
    dmid_ref, dweight_ref, dgain_ref, up, down, active, dbefore, dbranch, normed, sems = rest[aliased:]
    step = pl.program_id(0)
    own = own_ref[0]
    up_copies = load_halves(own, up_mine, up_other, up, sems.at[0])
    down_copies = load_halves(own, down_mine, down_other, down, sems.at[1])

    @pl.when(step == 0)
    def _():
        start_all(down_copies)
        start_all(up_copies)
        dgain_ref[...] = jnp.zeros_like(dgain_ref)

    rows = dh_ref.shape[0]

    @pl.when(step < blocks)
    def _():
        here = pl.ds(pl.multiple_of(step * rows, rows), rows)
        dh = dh_ref[...].astype(F32)
        branch = dh.astype(BF)
        dbranch[here, :] = branch
        gain = gain_ref[1:2, :]
        unit, scale = normalise(middle_ref[...])
        normed[here, :] = (unit * gain).astype(BF)

        @pl.when(step == 0)
        def _():
            wait_all(down_copies)
            wait_all(up_copies)

        dnormed = jnp.zeros((rows, D), F32)
        for part in range(up.shape[1] // D):
            lanes = slice(part * D, (part + 1) * D)
            dactive = dot_nt(branch, down[lanes, :])
            value = before_ref[:, lanes].astype(F32)
            root = math.sqrt(2.0 / math.pi)
            square = value * value
            curve = jnp.tanh(value * (root + (root * 0.044715) * square))
            half = 0.5 * (1.0 + curve)
            active[here, lanes] = (value * half).astype(BF)
            slope = half + (0.5 * value) * (1.0 - curve * curve) * (
                root + (3.0 * 0.044715 * root) * square
            )
            dpart = (dactive * slope).astype(BF)
            dbefore[here, lanes] = dpart
            dnormed = dnormed + dot_nt(dpart, up[:, lanes])
        dmid_ref[...] = dh + norm_back(dnormed, gain, unit, scale)
        dgain_ref[...] += column_sum(dnormed * unit)

    parts = up.shape[1] // D

    @pl.when((step >= blocks) & (step < blocks + parts))
    def _():
        lanes = pl.ds(pl.multiple_of((step - blocks) * D, D), D)
        dweight_ref[0] = dot_tn(normed[...], dbefore[:, lanes]).astype(BF)

    @pl.when(step >= blocks + parts)
    def _():
        part = step - blocks - parts
        half = D // 2
        base = down.shape[0] // 2
        for side in range(2):
            lanes = pl.ds(pl.multiple_of(side * base + part * half, half), half)
            dweight_ref[0, side * half : (side + 1) * half, :] = dot_tn(
                active[:, lanes], dbranch[...]
            ).astype(BF)


def ffn_backward(own, dh, before, middle, gains, shards, grads, first, slots):
    rows, width = before.shape
    block = min(512, rows)
    blocks = rows // block
    parts = width // D
    aliased = grads is not None
    row = lambda w: pl.BlockSpec((block, w), lambda i: (jnp.minimum(i, blocks - 1), 0))
    ins = [own, dh, before, middle, gains, *shards] + [grads] * aliased
    return pl.pallas_call(
        functools.partial(ffn_back_kernel, blocks, aliased),
        name="ffn_backward",
        grid=(blocks + 2 * parts,),
        in_specs=[SMEM, row(D), row(width), row(D), whole(gains.shape)] + [ANY] * (4 + aliased),
        out_specs=[
            row(D),
            pl.BlockSpec((1, D, D), lambda i: (first + jnp.maximum(i - blocks, 0), 0, 0)),
            pl.BlockSpec((8, D), lambda i: (0, 0)),
        ],
        out_shape=[
            jax.ShapeDtypeStruct((rows, D), F32),
            jax.ShapeDtypeStruct((slots, D, D), BF),
            jax.ShapeDtypeStruct((8, D), F32),
        ],
        scratch_shapes=[
            pltpu.VMEM((D, width), BF),
            pltpu.VMEM((width, D), BF),
            pltpu.VMEM((rows, width), BF),
            pltpu.VMEM((rows, width), BF),
            pltpu.VMEM((rows, D), BF),
            pltpu.VMEM((rows, D), BF),
            pltpu.SemaphoreType.DMA((2, 2)),
        ],
        input_output_aliases={len(ins) - 1: 1} if aliased else {},
        compiler_params=params(),
    )(*ins)


def attn_back_kernel(
    tile, reach, rows,
    own_ref, dmid_ref, h_ref, normed_ref, unit_q_ref, unit_k_ref, q_ref, k_ref, v_ref,
    scale_q_ref, scale_k_ref, attended_ref, seg_ref, code_ref, gain_ref, heads_ref, spread_ref,
    qkv_mine, qkv_other, proj_mine, proj_other, grads_ref,
    dh_ref, dweight_ref, dgain_ref,
    qkv, proj, dattn, dattended, inner, dk, dv, dmixed, sems,
):
    step = pl.program_id(0)
    own = own_ref[0]
    total_rows = k_ref.shape[0]
    count = total_rows // tile
    keys = reach * tile
    blocks = total_rows // rows
    proj_copies = load_halves(own, proj_mine, proj_other, proj, sems.at[0])
    qkv_copies = load_halves(own, qkv_mine, qkv_other, qkv, sems.at[1])
    root = HEAD_DIM ** (-0.5)

    def head_norm_back(grad, gain, unit, scale):
        scaled = grad * gain
        first = split_dot(scaled, heads_ref[...]) * (1.0 / HEAD_DIM)
        second = split_dot(scaled * unit, heads_ref[...]) * (1.0 / HEAD_DIM)
        return split_dot(scale, spread_ref[...]) * (
            scaled - split_dot(first, spread_ref[...]) - unit * split_dot(second, spread_ref[...])
        )

    @pl.when(step == 0)
    def _():
        start_all(proj_copies)
        start_all(qkv_copies)
        dgain_ref[...] = jnp.zeros_like(dgain_ref)
        dk[...] = jnp.zeros_like(dk)
        dv[...] = jnp.zeros_like(dv)
        wait_all(proj_copies)
        for block in range(blocks):
            here = slice(block * rows, (block + 1) * rows)
            grad = dmid_ref[here, :].astype(BF)
            dattn[here, :] = grad
            back = dot_nt(grad, proj[...]).astype(BF)
            dattended[here, :] = back
            product = back.astype(F32) * attended_ref[here, :].astype(F32)
            high = product.astype(BF)
            low = (product - high.astype(F32)).astype(BF)
            turn = (((0,), (1,)), ((), ()))
            inner[:, here] = lax.dot_general(
                heads_ref[...], high, turn, preferred_element_type=F32
            ) + lax.dot_general(heads_ref[...], low, turn, preferred_element_type=F32)

    @pl.when(step < count)
    def _():
        first = pl.multiple_of(window_start(step, count, reach) * tile, tile)
        window = pl.ds(first, keys)
        here = pl.ds(pl.multiple_of(step * tile, tile), tile)
        low_lanes = lax.broadcasted_iota(jnp.int32, (tile, 128), 1) < HEAD_DIM
        seg = seg_ref[:, here]
        code = code_ref[window, :]
        key_at = first + lax.broadcasted_iota(jnp.int32, (keys, tile), 0)
        query_at = step * tile + lax.broadcasted_iota(jnp.int32, (keys, tile), 1)
        bias = jnp.where((seg == code) | (query_at == key_at), 0.0, MASKED)
        bias = jnp.concatenate([bias, bias], axis=1)
        dq_parts = []
        for pair in range(HEADS // 2):
            lanes = slice(pair * 128, (pair + 1) * 128)
            queries = pair_stack(q_ref[here, lanes], low_lanes)
            grads = pair_stack(dattended[here, lanes], low_lanes)
            keys_part = k_ref[window, lanes]
            scores = dot_nt(keys_part, queries)
            expo = jnp.exp2(scores * (LOG2E * root) + bias)
            probs = expo * (1.0 / jnp.sum(expo, axis=0, keepdims=True))
            dprobs = dot_nt(v_ref[window, lanes], grads)
            less = jnp.concatenate(
                [inner[2 * pair : 2 * pair + 1, here], inner[2 * pair + 1 : 2 * pair + 2, here]],
                axis=1,
            )
            dscores = (probs * (dprobs - less)).astype(BF)
            dv[window, lanes] += dot(probs.astype(BF), grads)
            dk[window, lanes] += dot(dscores, queries)
            dq = dot_tn(dscores, keys_part)
            dq_parts.append(jnp.where(low_lanes, dq[:tile], dq[tile:]))
        dq = jnp.concatenate(dq_parts, axis=1) * root
        unit = unit_q_ref[here, :].astype(F32)
        dmixed[here, 0:D] = head_norm_back(dq, gain_ref[2:3, :], unit, scale_q_ref[here, :]).astype(BF)
        dgain_ref[8:16, :] += column_sum(dq * unit)

    @pl.when(step == count)
    def _():
        wait_all(qkv_copies)

    @pl.when((step >= count) & (step < count + blocks))
    def _():
        here = pl.ds(pl.multiple_of((step - count) * rows, rows), rows)
        grad = dk[here, :] * root
        unit = unit_k_ref[here, :].astype(F32)
        dmixed[here, D : 2 * D] = head_norm_back(
            grad, gain_ref[3:4, :], unit, scale_k_ref[here, :]
        ).astype(BF)
        dgain_ref[16:24, :] += column_sum(grad * unit)
        dmixed[here, 2 * D :] = dv[here, :].astype(BF)
        dnormed = dot_nt(dmixed[here, :], qkv[...])
        unit, scale = normalise(h_ref[here, :].astype(F32))
        dh_ref[...] = dmid_ref[here, :] + norm_back(dnormed, gain_ref[0:1, :], unit, scale)
        dgain_ref[0:8, :] += column_sum(dnormed * unit)

    for part in range(4):

        @pl.when(step == count + blocks + part)
        def _():
            if part < 3:
                grad = dot_tn(normed_ref[...], dmixed[:, part * D : (part + 1) * D])
            else:
                grad = dot_tn(attended_ref[...], dattn[...])
            dweight_ref[0] = grad.astype(BF)


def attn_backward(own, dmid, h, saved, attended, segs, gains, heads, spread, shards, grads, offset):
    total = h.shape[0]
    rows = min(512, total)
    tile = min(128, total)
    reach = min(3, total // tile)
    count, blocks = total // tile, total // rows
    normed, unit_q, unit_k, q, k, v, scale_q, scale_k = saved
    ins = [dmid, h, normed, unit_q, unit_k, q, k, v, scale_q, scale_k, attended, *segs, gains, heads, spread]
    return pl.pallas_call(
        functools.partial(attn_back_kernel, tile, reach, rows),
        name="attn_backward",
        grid=(count + blocks + 4,),
        in_specs=[SMEM] + [whole(x.shape) for x in ins] + [ANY] * 5,
        out_specs=[
            pl.BlockSpec((rows, D), lambda i: (jnp.clip(i - count, 0, blocks - 1), 0)),
            pl.BlockSpec((1, D, D), lambda i: (offset + jnp.maximum(i - count - blocks, 0), 0, 0)),
            pl.BlockSpec((24, D), lambda i: (0, 0)),
        ],
        out_shape=[
            jax.ShapeDtypeStruct((total, D), F32),
            jax.ShapeDtypeStruct(grads.shape, BF),
            jax.ShapeDtypeStruct((24, D), F32),
        ],
        scratch_shapes=[
            pltpu.VMEM((D, 3 * D), BF),
            pltpu.VMEM((D, D), BF),
            pltpu.VMEM((total, D), BF),
            pltpu.VMEM((total, D), BF),
            pltpu.VMEM((128, total), F32),
            pltpu.VMEM((total, D), F32),
            pltpu.VMEM((total, D), F32),
            pltpu.VMEM((total, 3 * D), BF),
            pltpu.SemaphoreType.DMA((2, 2)),
        ],
        input_output_aliases={len(ins) + 5: 1},
        compiler_params=params(),
    )(own, *ins, *shards, grads)


MESH = pl.DeviceIdType.MESH

ORDERS = ((0, 1, 2, 3), (1, 0, 2, 3), (2, 0, 1, 3))


def flip(index, bit):
    size = 1 << bit
    return index + size * (1 - 2 * ((index // size) % 2))


def add_rows(target, source, at, other, other_at, rows):
    chunk = 48

    def body(i, carry):
        here = pl.ds(pl.multiple_of(at + i * chunk, chunk), chunk)
        there = pl.ds(pl.multiple_of(other_at + i * chunk, chunk), chunk)
        target[here, :] = (source[here, :].astype(F32) + other[there, :].astype(F32)).astype(BF)
        return carry

    lax.fori_loop(0, rows // chunk, body, 0)


def reduce_kernel(
    waves, delta, orders,
    grads, small, total, small_total,
    held, sibling, arrived, small_held, small_arrived,
    local_sems, send_sems, recv_sems, small_send, small_recv,
):
    kinds = len(orders)
    me = lax.axis_index("dp")
    core = lax.axis_index("fsdp")
    rows = held.shape[1]
    half = rows // 2
    bits = 4

    barrier = pltpu.get_barrier_semaphore()
    pl.semaphore_signal(barrier, inc=1, device_id=(me, 1 - core), device_id_type=MESH)
    for bit in range(bits):
        pl.semaphore_signal(barrier, inc=1, device_id=(flip(me, bit), core), device_id_type=MESH)
    pl.semaphore_wait(barrier, bits + 1)

    mine = pl.ds(pl.multiple_of(core * half, half), half)
    theirs = pl.ds(pl.multiple_of((1 - core) * half, half), half)

    def locals_of(unit):
        return [
            pltpu.make_async_copy(
                grads.at[2 * unit + side, mine], held.at[unit, pl.ds(side * half, half)], local_sems.at[unit, side]
            )
            for side in range(2)
        ]

    def siblings_of(unit):
        return [
            pltpu.make_async_remote_copy(
                src_ref=grads.at[2 * unit + side, theirs],
                dst_ref=sibling.at[unit, pl.ds(side * half, half)],
                send_sem=send_sems.at[unit, side], recv_sem=recv_sems.at[unit, side],
                device_id=(me, 1 - core), device_id_type=MESH,
            )
            for side in range(2)
        ]

    def outs_of(unit):
        return [
            pltpu.make_async_copy(
                sibling.at[unit, pl.ds(side * half, half)], total.at[2 * unit + side], local_sems.at[unit, side]
            )
            for side in range(2)
        ]

    def spans(order):
        found, base, size = [], 0, rows
        for bit in order:
            size = size // 2
            side = (me // (1 << bit)) % 2
            found.append((base + side * size, base + (1 - side) * size, size))
            base = base + side * size
        return found

    def scatter_copy(unit, order, step):
        _, give, size = spans(order)[step]
        landing = rows - 2 * size
        return pltpu.make_async_remote_copy(
            src_ref=held.at[unit, pl.ds(pl.multiple_of(give, size), size)],
            dst_ref=arrived.at[unit, pl.ds(landing, size)],
            send_sem=send_sems.at[unit, 2 + step], recv_sem=recv_sems.at[unit, 2 + step],
            device_id=(flip(me, order[step]), core), device_id_type=MESH,
        )

    def gather_copy(unit, order, step):
        keep, _, size = spans(order)[step]
        place = pl.ds(pl.multiple_of(keep, size), size)
        return pltpu.make_async_remote_copy(
            src_ref=sibling.at[unit, place], dst_ref=sibling.at[unit, place],
            send_sem=send_sems.at[unit, 6 + step], recv_sem=recv_sems.at[unit, 6 + step],
            device_id=(flip(me, order[step]), core), device_id_type=MESH,
        )

    def stage(unit, order, s):
        if s == 0:
            for copy in locals_of(unit) + siblings_of(unit):
                copy.start()
        elif s == 1:
            for copy in locals_of(unit) + siblings_of(unit):
                copy.wait()
            add_rows(held.at[unit], held.at[unit], 0, sibling.at[unit], 0, rows)
            scatter_copy(unit, order, 0).start()
        elif s <= 5:
            step = s - 2
            scatter_copy(unit, order, step).wait()
            keep, _, size = spans(order)[step]
            target = sibling if step == 3 else held
            add_rows(target.at[unit], held.at[unit], keep, arrived.at[unit], rows - 2 * size, size)
            if step < 3:
                scatter_copy(unit, order, step + 1).start()
            else:
                gather_copy(unit, order, 3).start()
        elif s <= 9:
            step = 9 - s
            gather_copy(unit, order, step).wait()
            if step > 0:
                gather_copy(unit, order, step - 1).start()
            else:
                for copy in outs_of(unit):
                    copy.start()
        else:
            for copy in outs_of(unit):
                copy.wait()

    def small_copy(step):
        to = (me, 1 - core) if step == 0 else (flip(me, step - 1), core)
        return pltpu.make_async_remote_copy(
            src_ref=small_held.at[step], dst_ref=small_arrived.at[step],
            send_sem=small_send.at[step], recv_sem=small_recv.at[step],
            device_id=to, device_id_type=MESH,
        )

    small_held[0] = small[...]
    small_copy(0).start()

    def slot(t, carry):
        for s in reversed(range(11)):
            off = t - s
            wave = off // delta
            @pl.when((off >= 0) & (off % delta == 0) & (wave < waves))
            def _():
                for kind, order in enumerate(orders):
                    stage(wave * kinds + kind, order, s)
        return carry

    lax.fori_loop(0, (waves - 1) * delta + 11, slot, 0)
    for step in range(bits + 1):
        small_copy(step).wait()
        value = small_held[step] + small_arrived[step]
        if step < bits:
            small_held[step + 1] = value
            small_copy(step + 1).start()
        else:
            small_total[...] = value


def reduce_all(grads, small, delta=2, orders=ORDERS):
    units = grads.shape[0] // 2
    rows = D
    waves = units // len(orders)
    return pl.pallas_call(
        functools.partial(reduce_kernel, waves, delta, orders),
        name="reduce_all",
        in_specs=[pl.BlockSpec(memory_space=pl.ANY), pl.BlockSpec(memory_space=pltpu.VMEM)],
        out_specs=[pl.BlockSpec(memory_space=pl.ANY), pl.BlockSpec(memory_space=pltpu.VMEM)],
        out_shape=[
            jax.ShapeDtypeStruct((grads.shape[0], rows // 2, D), BF),
            jax.ShapeDtypeStruct(small.shape, F32),
        ],
        scratch_shapes=[
            pltpu.VMEM((units, rows, D), BF),
            pltpu.VMEM((units, rows, D), BF),
            pltpu.VMEM((units, rows - 48, D), BF),
            pltpu.VMEM((5, *small.shape), F32),
            pltpu.VMEM((5, *small.shape), F32),
            pltpu.SemaphoreType.DMA((units, 2)),
            pltpu.SemaphoreType.DMA((units, 10)),
            pltpu.SemaphoreType.DMA((units, 10)),
            pltpu.SemaphoreType.DMA((5,)),
            pltpu.SemaphoreType.DMA((5,)),
        ],
        compiler_params=pltpu.CompilerParams(collective_id=0, has_side_effects=True, vmem_limit_bytes=60 << 20),
    )(grads, small)


CORRECTION = 1.0 - 0.5**STEP


def adam(weight, first, second, grad, rate, decay):
    first = 0.5 * first + 0.5 * grad
    second = 0.5 * second + 0.5 * grad * grad
    step = first / CORRECTION / (jnp.sqrt(second / CORRECTION) + adam_eps)
    return weight - rate * (step + decay * weight), first, second


def adam_kernel(weight_ref, first_ref, second_ref, grad_ref, *outs):
    results = adam(
        weight_ref[0], first_ref[0], second_ref[0], grad_ref[0].astype(F32), D ** (-0.5), 0.1
    )
    for out, result in zip(outs, results):
        out[0] = result


def adam_step(weight, first, second, total, base, per_layer):
    layers, rows, width = weight.shape
    half = D // 2
    down, across = rows // half, width // D
    part = pl.BlockSpec((1, half, D), lambda l, i, j: (l, i, j))
    return pl.pallas_call(
        adam_kernel,
        name="adam_step",
        grid=(layers, down, across),
        in_specs=[part] * 3
        + [pl.BlockSpec((1, half, D), lambda l, i, j: (l * per_layer + base + i + j, 0, 0))],
        out_specs=[part] * 3,
        out_shape=[jax.ShapeDtypeStruct(weight.shape, F32)] * 3,
        compiler_params=params(3),
    )(weight, first, second, total)


def per_device(dp, fsdp, *args):
    tokens, cotangent, segments, keep_mask = args[:4]
    masters, firsts, seconds = args[4::3], args[5::3], args[6::3]
    packs, length, width = tokens.shape
    layers = masters[0].shape[0]
    paired = (dp, fsdp) == (16, 2)
    me = lax.axis_index("fsdp")
    own = jnp.zeros((1,), jnp.int32) + (me if fsdp == 2 else 0)

    def halves(shard):
        if fsdp == 2:
            return shard, lax.ppermute(shard, "fsdp", [(0, 1), (1, 0)])
        full = lax.all_gather(shard, "fsdp", axis=0, tiled=True)
        return full[: full.shape[0] // 2], full[full.shape[0] // 2 :]

    gathered = [
        [halves(masters[kind][layer].astype(BF)) for kind in range(4)] for layer in range(layers)
    ]
    gains_all = lax.all_gather(masters[4].astype(BF), "fsdp", axis=1, tiled=True).astype(F32)
    gains_all = jnp.pad(gains_all.transpose(0, 2, 1), ((0, 0), (0, 4), (0, 0)))
    heads = (
        lax.broadcasted_iota(jnp.int32, (D, 128), 0) // HEAD_DIM
        == lax.broadcasted_iota(jnp.int32, (D, 128), 1)
    ).astype(BF)
    spread = heads.T
    seg = segments[0]
    code = jnp.where(keep_mask[0] == 1, seg, -1)

    hidden = tokens[0]
    stored = []
    for layer in range(layers):
        qkv, proj, up, down = gathered[layer]
        gains = gains_all[layer]
        saved = qkv_forward(own, hidden, gains, heads, spread, *qkv)
        q, k, v = saved[3:6]
        last = layer == layers - 1
        attended, middle, before, result = mix_forward(
            own, hidden, q, k, v, seg[:, None], code[None, :], gains,
            (*proj, *up, *down), BF if last else F32,
        )
        stored.append((hidden, saved, attended, middle, before))
        hidden = result
    output = hidden.reshape(tokens.shape)

    parts = 4 + 2 * (stored[0][4].shape[1] // D)
    slots = layers * parts
    grads, small = None, [None] * layers
    d_hidden = cotangent[0]
    for layer in reversed(range(layers)):
        qkv, proj, up, down = gathered[layer]
        gains = gains_all[layer]
        h, saved, attended, middle, before = stored[layer]
        d_middle, grads, gain_two = ffn_backward(
            own, d_hidden, before, middle, gains, (*up, *down), grads, layer * parts + 4, slots
        )
        d_hidden, grads, gain_rest = attn_backward(
            own, d_middle, h, saved, attended, (seg[None, :], code[:, None]), gains, heads, spread,
            (*qkv, *proj), grads, layer * parts,
        )
        gain_rest = gain_rest.reshape(3, 8, D).sum(1)
        small[layer] = jnp.stack([gain_rest[0], gain_two.sum(0), gain_rest[1], gain_rest[2]])
    small = jnp.concatenate(small)
    input_grad = d_hidden.reshape(tokens.shape)

    updated = []
    if paired:
        total, small = reduce_all(grads, small)
        for kind, base in enumerate((0, 3, 4, 4 + (parts - 4) // 2)):
            updated.append(adam_step(masters[kind], firsts[kind], seconds[kind], total, base, parts))
    else:
        small = lax.psum(small, ("dp", "fsdp"))
        blocks = grads.reshape(layers, parts, D, D)
        wide = (parts - 4) // 2
        across = lambda x: x.transpose(0, 2, 1, 3).reshape(layers, D, -1)
        full = (
            across(blocks[:, :3]),
            blocks[:, 3],
            across(blocks[:, 4 : 4 + wide]),
            blocks[:, 4 + wide :].reshape(layers, wide, 2, D // 2, D).transpose(0, 2, 1, 3, 4)
            .reshape(layers, wide * D, D),
        )
        for kind in range(4):
            grad = lax.psum_scatter(full[kind], "fsdp", scatter_dimension=1, tiled=True)
            grad = lax.psum(grad, "dp").astype(F32)
            updated.append(adam(masters[kind], firsts[kind], seconds[kind], grad, D ** (-0.5), 0.1))
    small = small.reshape(layers, 4, D).transpose(0, 2, 1)
    share = masters[4].shape[1]
    small = lax.dynamic_slice_in_dim(small, me * share, share, 1)
    updated.append(adam(masters[4], firsts[4], seconds[4], small, 0.5, 0.0))
    return (output, input_grad, *[x for group in updated for x in group])


def solution(mesh):
    rows = P(("dp", "fsdp"), None, None)
    weight = P(None, "fsdp", None)
    flat = P(("dp", "fsdp"), None)
    return jax.shard_map(
        functools.partial(per_device, mesh.shape["dp"], mesh.shape["fsdp"]),
        mesh=mesh,
        in_specs=(rows, rows, flat, flat) + (weight,) * 15,
        out_specs=(rows, rows) + (weight,) * 15,
        check_vma=False,
    )
```

```python
import functools
import math

import jax
import jax.numpy as jnp
from jax import lax
from jax.experimental import pallas as pl
from jax.experimental.pallas import tpu as pltpu
from jax.sharding import PartitionSpec as P

D = 768
HEADS = 12
HEAD_DIM = 64
STEP = 5
BF = jnp.bfloat16
F32 = jnp.float32
norm_eps = 1e-06
adam_eps = 1e-08
VMEM_LIMIT = 62 * 1024 * 1024
LOG2E = 1.4426950408889634
MASKED = -1e30


def dot(a, b):
    return lax.dot_general(a, b, (((1,), (0,)), ((), ())), preferred_element_type=F32)


def dot_nt(a, b):
    return lax.dot_general(a, b, (((1,), (1,)), ((), ())), preferred_element_type=F32)


def dot_tn(a, b):
    return lax.dot_general(a, b, (((0,), (0,)), ((), ())), preferred_element_type=F32)


def split_dot(x, mat):
    high = x.astype(BF)
    low = (x - high.astype(F32)).astype(BF)
    return dot(high, mat) + dot(low, mat)


def normalise(values):
    average = jnp.mean(values, axis=-1, keepdims=True)
    centred = values - average
    spread = jnp.mean(centred * centred, axis=-1, keepdims=True)
    scale = lax.rsqrt(spread + norm_eps)
    return centred * scale, scale


def norm_back(grad, gain, unit, scale):
    scaled = grad * gain
    first = jnp.mean(scaled, axis=-1, keepdims=True)
    second = jnp.mean(scaled * unit, axis=-1, keepdims=True)
    return scale * (scaled - first - unit * second)


def column_sum(x):
    return jnp.sum(x.reshape(x.shape[0] // 8, 8, x.shape[1]), axis=0)


def load_halves(own, mine_ref, other_ref, full_ref, sems):
    half = full_ref.shape[0] // 2
    here = pl.multiple_of(own * half, half)
    there = pl.multiple_of((1 - own) * half, half)
    return (
        pltpu.make_async_copy(mine_ref, full_ref.at[pl.ds(here, half)], sems.at[0]),
        pltpu.make_async_copy(other_ref, full_ref.at[pl.ds(there, half)], sems.at[1]),
    )


def start_all(copies):
    for copy in copies:
        copy.start()


def wait_all(copies):
    for copy in copies:
        copy.wait()


def whole(shape):
    zeros = (0,) * len(shape)
    return pl.BlockSpec(shape, lambda *_: zeros, pipeline_mode=pl.Buffered(1))


ANY = pl.BlockSpec(memory_space=pl.ANY)
SMEM = pl.BlockSpec(memory_space=pltpu.SMEM)


def params(steps=1):
    return pltpu.CompilerParams(
        dimension_semantics=("arbitrary",) * steps, vmem_limit_bytes=VMEM_LIMIT
    )


def qkv_kernel(
    own_ref, h_ref, gain_ref, heads_ref, spread_ref, mine_ref, other_ref,
    normed_ref, q_ref, k_ref, v_ref, scale_q_ref, scale_k_ref,
    weight, sems,
):
    copies = load_halves(own_ref[0], mine_ref, other_ref, weight, sems)

    @pl.when(pl.program_id(0) == 0)
    def _():
        start_all(copies)

    unit, _ = normalise(h_ref[...].astype(F32))
    normed = (unit * gain_ref[0:1, :]).astype(BF)
    normed_ref[...] = normed

    @pl.when(pl.program_id(0) == 0)
    def _():
        wait_all(copies)

    v_ref[...] = dot(normed, weight[:, 2 * D :]).astype(BF)
    for part, out_ref, scale_ref in ((0, q_ref, scale_q_ref), (1, k_ref, scale_k_ref)):
        raw = dot(normed, weight[:, part * D : (part + 1) * D])
        average = split_dot(raw, heads_ref[...]) * (1.0 / HEAD_DIM)
        centred = raw - split_dot(average, spread_ref[...])
        spread = split_dot(centred * centred, heads_ref[...]) * (1.0 / HEAD_DIM)
        scale = lax.rsqrt(spread + norm_eps)
        unit = centred * split_dot(scale, spread_ref[...])
        out_ref[...] = (unit * gain_ref[2 + part : 3 + part, :]).astype(BF)
        scale_ref[...] = scale


def qkv_forward(own, h, gains, heads, spread, mine, other):
    rows = h.shape[0]
    block = min(512, rows)
    row = lambda width: pl.BlockSpec((block, width), lambda i: (i, 0))
    outs = [(D, BF)] * 4 + [(128, F32)] * 2
    return pl.pallas_call(
        qkv_kernel,
        name="qkv_forward",
        grid=(rows // block,),
        in_specs=[SMEM, row(D), whole(gains.shape), whole(heads.shape), whole(spread.shape), ANY, ANY],
        out_specs=[row(w) for w, _ in outs],
        out_shape=[jax.ShapeDtypeStruct((rows, w), t) for w, t in outs],
        scratch_shapes=[pltpu.VMEM((D, 3 * D), BF), pltpu.SemaphoreType.DMA((2,))],
        compiler_params=params(),
    )(own, h, gains, heads, spread, mine, other)


def window_start(block, count, reach):
    return jnp.clip(block - 1, 0, count - reach)


def pair_stack(x, low_lanes):
    zero = jnp.zeros_like(x)
    return jnp.concatenate([jnp.where(low_lanes, x, zero), jnp.where(low_lanes, zero, x)], axis=0)


def mix_kernel(
    tile, reach,
    own_ref, h_ref, q_ref, k_ref, v_ref, seg_ref, code_ref, gain_ref,
    proj_mine, proj_other, up_mine, up_other, down_mine, down_other,
    attended_ref, middle_ref, before_ref, out_ref,
    proj, up, down, sems,
):
    step = pl.program_id(0)
    own = own_ref[0]
    proj_copies = load_halves(own, proj_mine, proj_other, proj, sems.at[0])
    up_copies = load_halves(own, up_mine, up_other, up, sems.at[1])
    down_copies = load_halves(own, down_mine, down_other, down, sems.at[2])

    @pl.when(step == 0)
    def _():
        start_all(proj_copies)
        start_all(up_copies)
        start_all(down_copies)

    rows = h_ref.shape[0]
    count = k_ref.shape[0] // tile
    keys = reach * tile
    factor = LOG2E * HEAD_DIM ** (-0.5)
    low_lanes = lax.broadcasted_iota(jnp.int32, (tile, 128), 1) < HEAD_DIM

    def attend(inner, carry):
        block = step * (rows // tile) + inner
        first = pl.multiple_of(window_start(block, count, reach) * tile, tile)
        here = pl.multiple_of(inner * tile, tile)
        seg = seg_ref[pl.ds(here, tile), :]
        code = code_ref[:, pl.ds(first, keys)]
        query_at = block * tile + lax.broadcasted_iota(jnp.int32, (tile, keys), 0)
        key_at = first + lax.broadcasted_iota(jnp.int32, (tile, keys), 1)
        bias = jnp.where((seg == code) | (query_at == key_at), 0.0, MASKED)
        bias = jnp.concatenate([bias, bias], axis=0)
        for pair in range(HEADS // 2):
            lanes = slice(pair * 128, (pair + 1) * 128)
            queries = pair_stack(q_ref[pl.ds(here, tile), lanes], low_lanes)
            scores = dot_nt(queries, k_ref[pl.ds(first, keys), lanes])
            expo = jnp.exp2(scores * factor + bias)
            total = jnp.sum(expo, axis=-1, keepdims=True)
            mixed = dot(expo.astype(BF), v_ref[pl.ds(first, keys), lanes]) / total
            attended_ref[pl.ds(here, tile), lanes] = jnp.where(
                low_lanes, mixed[:tile], mixed[tile:]
            ).astype(BF)
        return carry

    lax.fori_loop(0, rows // tile, attend, 0)

    @pl.when(step == 0)
    def _():
        wait_all(proj_copies)

    middle = h_ref[...].astype(F32) + dot(attended_ref[...], proj[...])
    middle_ref[...] = middle
    unit, _ = normalise(middle)
    normed = (unit * gain_ref[1:2, :]).astype(BF)

    @pl.when(step == 0)
    def _():
        wait_all(up_copies)
        wait_all(down_copies)

    result = middle
    for part in range(up.shape[1] // D):
        lanes = slice(part * D, (part + 1) * D)
        before = dot(normed, up[:, lanes])
        before_ref[:, lanes] = before.astype(BF)
        active = jax.nn.gelu(before, approximate=True).astype(BF)
        result = result + dot(active, down[lanes, :])
    out_ref[...] = result.astype(out_ref.dtype)


def mix_forward(own, h, q, k, v, seg, code, gains, shards, out_type):
    rows = h.shape[0]
    block = min(512, rows)
    tile = min(128, rows)
    reach = min(3, rows // tile)
    width = shards[2].shape[1]
    row = lambda w: pl.BlockSpec((block, w), lambda i: (i, 0))
    outs = [(D, BF), (D, F32), (width, BF), (D, out_type)]
    return pl.pallas_call(
        functools.partial(mix_kernel, tile, reach),
        name="mix_forward",
        grid=(rows // block,),
        in_specs=[SMEM, row(D), row(D), whole(k.shape), whole(v.shape), row(1), whole(code.shape), whole(gains.shape)]
        + [ANY] * 6,
        out_specs=[row(w) for w, _ in outs],
        out_shape=[jax.ShapeDtypeStruct((rows, w), t) for w, t in outs],
        scratch_shapes=[
            pltpu.VMEM((D, D), BF),
            pltpu.VMEM((D, width), BF),
            pltpu.VMEM((width, D), BF),
            pltpu.SemaphoreType.DMA((3, 2)),
        ],
        compiler_params=params(),
    )(own, h, q, k, v, seg, code, gains, *shards)


MESH = pl.DeviceIdType.MESH

BITS = 4
XYZ, YXZ, ZXY, YZX, XZY, ZYX = (
    (0, 1, 2, 3), (1, 0, 2, 3), (2, 0, 1, 3), (1, 2, 0, 3), (0, 2, 1, 3), (2, 1, 0, 3),
)
GROUP, SPLIT = 4, 3
UNIT = GROUP * D // 2
WIDTH = D // SPLIT
FINAL = UNIT >> BITS


def flip(index, bit):
    size = 1 << bit
    return index + size * (1 - 2 * ((index // size) % 2))


def meet(partners):
    me, core = lax.axis_index("dp"), lax.axis_index("fsdp")
    barrier = pltpu.get_barrier_semaphore()
    pl.semaphore_signal(barrier, inc=1, device_id=(me, 1 - core), device_id_type=MESH)
    for bit in range(partners):
        pl.semaphore_signal(barrier, inc=1, device_id=(flip(me, bit), core), device_id_type=MESH)
    pl.semaphore_wait(barrier, 1 + partners)


def add_rows(target, source, at, other, other_at, rows):
    chunk = FINAL

    def body(i, carry):
        here = pl.ds(pl.multiple_of(at + i * chunk, chunk), chunk)
        there = pl.ds(pl.multiple_of(other_at + i * chunk, chunk), chunk)
        target[here, :] = (source[here, :].astype(F32) + other[there, :].astype(F32)).astype(BF)
        return carry

    lax.fori_loop(0, rows // chunk, body, 0)


class Sum:
    def __init__(self, kind, orders):
        self.kind, self.orders, self.count = kind, orders, len(orders)
        self.scatters = kind != "gather"
        self.gathers = kind != "scatter"

    def blocks(self):
        return GROUP * self.count // SPLIT

    def out_shapes(self):
        if self.gathers:
            return [jax.ShapeDtypeStruct((self.blocks(), D // 2, D), BF)]
        return [jax.ShapeDtypeStruct((self.count, FINAL, WIDTH), BF)]

    def inputs(self):
        return 2 if self.scatters else 1

    def scratch(self):
        n = self.count
        found = []
        if self.scatters:
            found += [
                pltpu.VMEM((n, UNIT, WIDTH), BF),
                pltpu.VMEM((n, UNIT - FINAL, WIDTH), BF),
                pltpu.VMEM((2, UNIT, WIDTH), BF),
                pltpu.SemaphoreType.DMA((n, 2 * GROUP)),
                pltpu.SemaphoreType.DMA((n, BITS)),
                pltpu.SemaphoreType.DMA((n, BITS)),
            ]
        if self.gathers:
            found += [
                pltpu.VMEM((n, UNIT, WIDTH), BF),
                pltpu.SemaphoreType.DMA((n, GROUP)),
                pltpu.SemaphoreType.DMA((n, BITS)),
                pltpu.SemaphoreType.DMA((n, BITS)),
            ]
        else:
            found += [pltpu.SemaphoreType.DMA((n,))]
        return found

    def bind(self, ins, outs, scratch):
        self.me, self.core = lax.axis_index("dp"), lax.axis_index("fsdp")
        self.ins, self.out = ins, outs[0]
        scratch = list(scratch)
        if self.scatters:
            self.held, self.arrived, self.stage, self.load, self.send, self.recv = scratch[:6]
            scratch = scratch[6:]
        if self.gathers:
            self.final, self.local, self.gsend, self.grecv = scratch
        else:
            self.local = scratch[0]

    def spans(self, unit):
        found, base, size = [], 0, UNIT
        for bit in self.orders[unit]:
            size = size // 2
            side = (self.me // (1 << bit)) % 2
            found.append((base + side * size, base + (1 - side) * size, size))
            base = base + side * size
        return found

    def window(self, ref, unit, side):
        block = GROUP * (unit // SPLIT) + side
        return ref.at[block, :, pl.ds((unit % SPLIT) * WIDTH, WIDTH)]

    def loads(self, unit):
        return [
            pltpu.make_async_copy(
                self.window(source, unit, side),
                target.at[pl.ds(side * (D // 2), D // 2)],
                self.load.at[unit, GROUP * which + side],
            )
            for which, (source, target) in enumerate(
                ((self.ins[0], self.held.at[unit]), (self.ins[1], self.stage.at[unit % 2]))
            )
            for side in range(GROUP)
        ]

    def scatter_copy(self, unit, step):
        _, give, size = self.spans(unit)[step]
        return pltpu.make_async_remote_copy(
            src_ref=self.held.at[unit, pl.ds(pl.multiple_of(give, size), size)],
            dst_ref=self.arrived.at[unit, pl.ds(UNIT - 2 * size, size)],
            send_sem=self.send.at[unit, step], recv_sem=self.recv.at[unit, step],
            device_id=(flip(self.me, self.orders[unit][step]), self.core), device_id_type=MESH,
        )

    def gather_copy(self, unit, step):
        keep, _, size = self.spans(unit)[step]
        place = pl.ds(pl.multiple_of(keep, size), size)
        return pltpu.make_async_remote_copy(
            src_ref=self.final.at[unit, place], dst_ref=self.final.at[unit, place],
            send_sem=self.gsend.at[unit, step], recv_sem=self.grecv.at[unit, step],
            device_id=(flip(self.me, self.orders[unit][step]), self.core), device_id_type=MESH,
        )

    def share_copy(self, unit):
        keep, _, size = self.spans(unit)[BITS - 1]
        place = pl.ds(pl.multiple_of(keep, size), size)
        if self.scatters:
            return pltpu.make_async_copy(self.held.at[unit, place], self.out.at[unit], self.local.at[unit])
        return pltpu.make_async_copy(self.ins[0].at[unit], self.final.at[unit, place], self.local.at[unit, 0])

    def outs(self, unit):
        return [
            pltpu.make_async_copy(
                self.final.at[unit, pl.ds(side * (D // 2), D // 2)],
                self.window(self.out, unit, side),
                self.local.at[unit, side],
            )
            for side in range(GROUP)
        ]

    def begin(self):
        if not self.scatters:
            for unit in range(self.count):
                self.share_copy(unit).start()
            for unit in range(self.count):
                self.share_copy(unit).wait()
                self.gather_copy(unit, BITS - 1).start()
            return
        for unit in range(min(2, self.count)):
            start_all(self.loads(unit))
        for unit in range(self.count):
            wait_all(self.loads(unit))
            add_rows(self.held.at[unit], self.held.at[unit], 0, self.stage.at[unit % 2], 0, UNIT)
            self.scatter_copy(unit, 0).start()
            if unit + 2 < self.count:
                start_all(self.loads(unit + 2))

    def stages(self):
        return BITS * (self.scatters + self.gathers)

    def advance(self, unit, stage):
        if self.scatters and stage < BITS:
            self.scatter_copy(unit, stage).wait()
            keep, _, size = self.spans(unit)[stage]
            landing = UNIT - 2 * size
            target = self.final if self.gathers and stage == BITS - 1 else self.held
            add_rows(target.at[unit], self.held.at[unit], keep, self.arrived.at[unit], landing, size)
            if stage < BITS - 1:
                self.scatter_copy(unit, stage + 1).start()
            elif self.gathers:
                self.gather_copy(unit, BITS - 1).start()
            else:
                self.share_copy(unit).start()
            return
        step = BITS - 1 - (stage - BITS * self.scatters)
        self.gather_copy(unit, step).wait()
        if step:
            self.gather_copy(unit, step - 1).start()
        else:
            start_all(self.outs(unit))

    def finish(self):
        for unit in range(self.count):
            if self.gathers:
                wait_all(self.outs(unit))
            else:
                self.share_copy(unit).wait()


def bind_sums(sums, ins, outs, scratch):
    ins, outs, scratch = list(ins), list(outs), list(scratch)
    for one in sums:
        a, b, c = one.inputs(), 1, len(one.scratch())
        one.bind(ins[:a], outs[:b], scratch[:c])
        ins, outs, scratch = ins[a:], outs[b:], scratch[c:]


def run_steps(sums, steps):
    owners = [(one, unit) for one in sums for unit in range(one.count)]
    for unit, stage in steps:
        one, own = owners[unit]
        one.advance(own, stage)


class Blocks:
    def __init__(self, count, paired):
        self.count, self.paired = count, paired

    def out_shapes(self):
        rows = D // 2 if self.paired else D
        return [jax.ShapeDtypeStruct((self.count, rows, D), BF)] * (1 + self.paired)

    def scratch(self):
        return [pltpu.SemaphoreType.DMA((self.count,))] * (1 + 2 * self.paired)

    def bind(self, outs, sems):
        self.outs, self.sems = outs, sems

    def copies(self, block, lanes, ref, first_row):
        if not self.paired:
            return [
                pltpu.make_async_copy(
                    ref.at[pl.ds(first_row, D), lanes], self.outs[0].at[block], self.sems[0].at[block]
                )
            ]
        core = lax.axis_index("fsdp")
        half = D // 2
        mine = pl.multiple_of(first_row + core * half, half)
        theirs = pl.multiple_of(first_row + (1 - core) * half, half)
        return [
            pltpu.make_async_copy(
                ref.at[pl.ds(mine, half), lanes], self.outs[0].at[block], self.sems[0].at[block]
            ),
            pltpu.make_async_remote_copy(
                src_ref=ref.at[pl.ds(theirs, half), lanes], dst_ref=self.outs[1].at[block],
                send_sem=self.sems[1].at[block], recv_sem=self.sems[2].at[block],
                device_id=(lax.axis_index("dp"), 1 - core), device_id_type=MESH,
            ),
        ]


def my_half(paired):
    return lax.axis_index("fsdp") if paired else 0


def carve(refs, *sizes):
    found, at = [], 0
    for size in sizes:
        found.append(refs[at : at + size])
        at += size
    return found


def sums_in(sums):
    return sum(one.inputs() for one in sums)


def sums_scratch(sums):
    return [shape for one in sums for shape in one.scratch()]


def sums_outs(sums):
    return [shape for one in sums for shape in one.out_shapes()]


def remote_params(paired, collective_id):
    if not paired:
        return params()
    return pltpu.CompilerParams(
        dimension_semantics=("arbitrary",), vmem_limit_bytes=VMEM_LIMIT,
        collective_id=collective_id, has_side_effects=True,
    )


def ffn_back_kernel(blocks, store, sums, plan, dh_ref, before_ref, middle_ref, gain_ref, *refs):
    weights, ins, outs, store_outs, sum_outs, own_scratch, store_sems, sum_scratch = carve(
        refs, 4, sums_in(sums), 2, 1 + store.paired, len(sums), 7, 1 + 2 * store.paired,
        len(sums_scratch(sums)),
    )
    up_mine, up_other, down_mine, down_other = weights
    dmid_ref, dgain_ref = outs
    up, down, active, dbefore, dbranch, normed, sems = own_scratch
    store.bind(store_outs, store_sems)
    bind_sums(sums, ins, sum_outs, sum_scratch)
    step = pl.program_id(0)
    own = my_half(store.paired)
    up_copies = load_halves(own, up_mine, up_other, up, sems.at[0])
    down_copies = load_halves(own, down_mine, down_other, down, sems.at[1])
    parts = up.shape[1] // D
    rows = dh_ref.shape[0]

    @pl.when(step == 0)
    def _():
        start_all(down_copies)
        start_all(up_copies)
        dgain_ref[...] = jnp.zeros_like(dgain_ref)
        if store.paired:
            meet(BITS if sums else 0)
        for one in sums:
            one.begin()

    @pl.when(step < blocks)
    def _():
        here = pl.ds(pl.multiple_of(step * rows, rows), rows)
        dh = dh_ref[...].astype(F32)
        branch = dh.astype(BF)
        dbranch[here, :] = branch
        gain = gain_ref[1:2, :]
        unit, scale = normalise(middle_ref[...])
        normed[here, :] = (unit * gain).astype(BF)

        @pl.when(step == 0)
        def _():
            wait_all(down_copies)
            wait_all(up_copies)

        dnormed = jnp.zeros((rows, D), F32)
        for part in range(parts):
            lanes = slice(part * D, (part + 1) * D)
            dactive = dot_nt(branch, down[lanes, :])
            value = before_ref[:, lanes].astype(F32)
            root = math.sqrt(2.0 / math.pi)
            square = value * value
            curve = jnp.tanh(value * (root + (root * 0.044715) * square))
            half = 0.5 * (1.0 + curve)
            active[here, lanes] = (value * half).astype(BF)
            slope = half + (0.5 * value) * (1.0 - curve * curve) * (
                root + (3.0 * 0.044715 * root) * square
            )
            dpart = (dactive * slope).astype(BF)
            dbefore[here, lanes] = dpart
            dnormed = dnormed + dot_nt(dpart, up[:, lanes])
            for block in range(blocks):
                if block * parts + part in plan:

                    @pl.when(step == block)
                    def _():
                        run_steps(sums, plan[block * parts + part])

        dmid_ref[...] = dh + norm_back(dnormed, gain, unit, scale)
        dgain_ref[...] += column_sum(dnormed * unit)

    late = blocks * parts - blocks
    for tick in sorted(plan):
        if tick >= blocks * parts:

            @pl.when(step == tick - late)
            def _():
                run_steps(sums, plan[tick])

    every = slice(0, D)

    @pl.when((step >= blocks) & (step < blocks + parts))
    def _():
        part = step - blocks
        lanes = pl.ds(pl.multiple_of(part * D, D), D)
        up[:, lanes] = dot_tn(normed[...], dbefore[:, lanes]).astype(BF)
        start_all(store.copies(part, lanes, up, 0))

    @pl.when(step >= blocks + parts)
    def _():
        part = step - blocks - parts
        half = D // 2
        base = down.shape[0] // 2
        first_row = pl.multiple_of(part * D, D)
        for side in range(2):
            lanes = pl.ds(pl.multiple_of(side * base + part * half, half), half)
            here = pl.ds(pl.multiple_of(first_row + side * half, half), half)
            down[here, :] = dot_tn(active[:, lanes], dbranch[...]).astype(BF)
        start_all(store.copies(parts + part, every, down, first_row))

    @pl.when(step == blocks + 2 * parts - 1)
    def _():
        for part in range(parts):
            wait_all(store.copies(part, slice(part * D, (part + 1) * D), up, 0))
        for part in range(parts):
            wait_all(store.copies(parts + part, every, down, part * D))
        for one in sums:
            one.finish()


def ffn_backward(dh, before, middle, gains, shards, paired, sums, plan, sum_ins, collective_id):
    rows, width = before.shape
    block = min(512, rows)
    blocks = rows // block
    parts = width // D
    store = Blocks(2 * parts, paired)
    row = lambda w, **mode: pl.BlockSpec((block, w), lambda i: (jnp.minimum(i, blocks - 1), 0), **mode)
    once = {"pipeline_mode": pl.Buffered(1)}
    outs = store.out_shapes() + sums_outs(sums)
    return pl.pallas_call(
        functools.partial(ffn_back_kernel, blocks, store, sums, plan),
        name="ffn_backward",
        grid=(blocks + 2 * parts,),
        in_specs=[row(D, **once), row(width), row(D, **once), whole(gains.shape)] + [ANY] * (4 + len(sum_ins)),
        out_specs=[row(D), pl.BlockSpec((8, D), lambda i: (0, 0))] + [ANY] * len(outs),
        out_shape=[jax.ShapeDtypeStruct((rows, D), F32), jax.ShapeDtypeStruct((8, D), F32)] + outs,
        scratch_shapes=[
            pltpu.VMEM((D, width), BF),
            pltpu.VMEM((width, D), BF),
            pltpu.VMEM((rows, width), BF),
            pltpu.VMEM((rows, width), BF),
            pltpu.VMEM((rows, D), BF),
            pltpu.VMEM((rows, D), BF),
            pltpu.SemaphoreType.DMA((2, 2)),
        ]
        + store.scratch()
        + sums_scratch(sums),
        compiler_params=remote_params(paired, collective_id),
    )(dh, before, middle, gains, *shards, *sum_ins)


def window_at(block, count):
    return block - 1 + (count - 1 - block) // (count - 1) - block // (count - 1)


def attn_back_kernel(
    tile, reach, rows, store, sums, plan,
    dmid_ref, h_ref, q_ref, k_ref, v_ref, scale_q_ref, scale_k_ref,
    attended_ref, seg_ref, code_ref, gain_ref, heads_ref, spread_ref, *refs,
):
    weights, ins, outs, store_outs, sum_outs, own_scratch, store_sems, sum_scratch = carve(
        refs, 5, sums_in(sums), 2, 1 + store.paired, len(sums), 9, 1 + 2 * store.paired,
        len(sums_scratch(sums)),
    )
    normed_ref, qkv_mine, qkv_other, proj_mine, proj_other = weights
    dh_ref, dgain_ref = outs
    qkv, proj, dattended, inner, dk, dv, dmixed, sems, normed_sem = own_scratch
    store.bind(store_outs, store_sems)
    bind_sums(sums, ins, sum_outs, sum_scratch)
    step = pl.program_id(0)
    own = my_half(store.paired)
    total_rows = k_ref.shape[0]
    count = total_rows // tile
    keys = reach * tile
    blocks = total_rows // rows
    proj_copies = load_halves(own, proj_mine, proj_other, proj, sems.at[0])
    qkv_copies = load_halves(own, qkv_mine, qkv_other, qkv, sems.at[1])
    normed_copy = pltpu.make_async_copy(normed_ref, dattended, normed_sem)
    root = HEAD_DIM ** (-0.5)

    def head_norm_back(grad, gain, unit, scale):
        scaled = grad * gain
        first = split_dot(scaled, heads_ref[...]) * (1.0 / HEAD_DIM)
        second = split_dot(scaled * unit, heads_ref[...]) * (1.0 / HEAD_DIM)
        return split_dot(scale, spread_ref[...]) * (
            scaled - split_dot(first, spread_ref[...]) - unit * split_dot(second, spread_ref[...])
        )

    @pl.when(step == 0)
    def _():
        start_all(proj_copies)
        start_all(qkv_copies)
        dgain_ref[...] = jnp.zeros_like(dgain_ref)
        dk[...] = jnp.zeros_like(dk)
        dv[...] = jnp.zeros_like(dv)
        if store.paired:
            meet(BITS if sums else 0)
        for one in sums:
            one.begin()
        wait_all(proj_copies)
        for block in range(blocks):
            here = slice(block * rows, (block + 1) * rows)
            back = dot_nt(dmid_ref[here, :].astype(BF), proj[...]).astype(BF)
            dattended[here, :] = back
            product = back.astype(F32) * attended_ref[here, :].astype(F32)
            high = product.astype(BF)
            low = (product - high.astype(F32)).astype(BF)
            turn = (((0,), (1,)), ((), ()))
            inner[:, here] = lax.dot_general(
                heads_ref[...], high, turn, preferred_element_type=F32
            ) + lax.dot_general(heads_ref[...], low, turn, preferred_element_type=F32)

    for tick in sorted(plan):

        @pl.when(step == tick)
        def _():
            run_steps(sums, plan[tick])

    @pl.when(step < count)
    def _():
        first = pl.multiple_of(window_at(step, count) * tile if count > reach else 0, tile)
        window = pl.ds(first, keys)
        here = pl.ds(pl.multiple_of(step * tile, tile), tile)
        low_lanes = lax.broadcasted_iota(jnp.int32, (tile, 128), 1) < HEAD_DIM
        seg = seg_ref[:, here]
        code = code_ref[window, :]
        key_at = first + lax.broadcasted_iota(jnp.int32, (keys, tile), 0)
        query_at = step * tile + lax.broadcasted_iota(jnp.int32, (keys, tile), 1)
        bias = jnp.where((seg == code) | (query_at == key_at), 0.0, MASKED)
        bias = jnp.concatenate([bias, bias], axis=1)
        dq_parts = []
        for pair in range(HEADS // 2):
            lanes = slice(pair * 128, (pair + 1) * 128)
            queries = pair_stack(q_ref[here, lanes], low_lanes)
            grads = pair_stack(dattended[here, lanes], low_lanes)
            keys_part = k_ref[window, lanes]
            scores = dot_nt(keys_part, queries)
            expo = jnp.exp2(scores * (LOG2E * root) + bias)
            probs = expo * (1.0 / jnp.sum(expo, axis=0, keepdims=True))
            dprobs = dot_nt(v_ref[window, lanes], grads)
            less = jnp.concatenate(
                [inner[2 * pair : 2 * pair + 1, here], inner[2 * pair + 1 : 2 * pair + 2, here]],
                axis=1,
            )
            dscores = (probs * (dprobs - less)).astype(BF)
            dv[window, lanes] += dot(probs.astype(BF), grads)
            dk[window, lanes] += dot(dscores, queries)
            dq = dot_tn(dscores, keys_part)
            dq_parts.append(jnp.where(low_lanes, dq[:tile], dq[tile:]))
        dq = jnp.concatenate(dq_parts, axis=1) * root
        gain = gain_ref[2:3, :]
        unit = q_ref[here, :].astype(F32) * (1.0 / gain)
        dmixed[here, 0:D] = head_norm_back(dq, gain, unit, scale_q_ref[here, :]).astype(BF)
        dgain_ref[8:16, :] += column_sum(dq * unit)

    @pl.when(step == count)
    def _():
        normed_copy.start()
        wait_all(qkv_copies)

    @pl.when((step >= count) & (step < count + blocks))
    def _():
        here = pl.ds(pl.multiple_of((step - count) * rows, rows), rows)
        grad = dk[here, :] * root
        gain = gain_ref[3:4, :]
        unit = k_ref[here, :].astype(F32) * (1.0 / gain)
        dmixed[here, D : 2 * D] = head_norm_back(grad, gain, unit, scale_k_ref[here, :]).astype(BF)
        dgain_ref[16:24, :] += column_sum(grad * unit)
        dmixed[here, 2 * D :] = dv[here, :].astype(BF)
        dnormed = dot_nt(dmixed[here, :], qkv[...])
        unit, scale = normalise(h_ref[here, :].astype(F32))
        dh_ref[...] = dmid_ref[here, :] + norm_back(dnormed, gain_ref[0:1, :], unit, scale)
        dgain_ref[0:8, :] += column_sum(dnormed * unit)

    @pl.when(step == count + blocks)
    def _():
        normed_copy.wait()

    @pl.when((step >= count + blocks) & (step < count + blocks + 3))
    def _():
        part = step - count - blocks
        lanes = pl.ds(pl.multiple_of(part * D, D), D)
        qkv[:, lanes] = dot_tn(dattended[...], dmixed[:, lanes]).astype(BF)
        start_all(store.copies(part, lanes, qkv, 0))

    every = slice(0, D)

    @pl.when(step == count + blocks + 3)
    def _():
        proj[...] = dot_tn(attended_ref[...], dmid_ref[...].astype(BF)).astype(BF)
        start_all(store.copies(3, every, proj, 0))
        for part in range(3):
            wait_all(store.copies(part, slice(part * D, (part + 1) * D), qkv, 0))
        wait_all(store.copies(3, every, proj, 0))
        for one in sums:
            one.finish()


def attn_backward(
    dmid, h, saved, attended, segs, gains, heads, spread, shards, paired, sums, plan, sum_ins, collective_id
):
    total = h.shape[0]
    rows = min(512, total)
    tile = min(128, total)
    reach = min(3, total // tile)
    count, blocks = total // tile, total // rows
    normed, q, k, v, scale_q, scale_k = saved
    ins = [dmid, h, q, k, v, scale_q, scale_k, attended, *segs, gains, heads, spread]
    store = Blocks(4, paired)
    outs = store.out_shapes() + sums_outs(sums)
    return pl.pallas_call(
        functools.partial(attn_back_kernel, tile, reach, rows, store, sums, plan),
        name="attn_backward",
        grid=(count + blocks + 4,),
        in_specs=[whole(x.shape) for x in ins] + [ANY] * (5 + len(sum_ins)),
        out_specs=[
            pl.BlockSpec((rows, D), lambda i: (jnp.clip(i - count, 0, blocks - 1), 0)),
            pl.BlockSpec((24, D), lambda i: (0, 0)),
        ]
        + [ANY] * len(outs),
        out_shape=[jax.ShapeDtypeStruct((total, D), F32), jax.ShapeDtypeStruct((24, D), F32)] + outs,
        scratch_shapes=[
            pltpu.VMEM((D, 3 * D), BF),
            pltpu.VMEM((D, D), BF),
            pltpu.VMEM((total, D), BF),
            pltpu.VMEM((128, total), F32),
            pltpu.VMEM((total, D), F32),
            pltpu.VMEM((total, D), F32),
            pltpu.VMEM((total, 3 * D), BF),
            pltpu.SemaphoreType.DMA((2, 2)),
            pltpu.SemaphoreType.DMA,
        ]
        + store.scratch()
        + sums_scratch(sums),
        compiler_params=remote_params(paired, collective_id),
    )(*ins, normed, *shards, *sum_ins)


def last_sums_kernel(sums, steps, counts, *refs):
    n_in, n_out = counts
    small, ins = refs[0], refs[1 : 1 + n_in]
    small_total, outs = refs[1 + n_in], refs[2 + n_in : 2 + n_in + n_out]
    small_held, small_arrived, small_send, small_recv = refs[2 + n_in + n_out : 6 + n_in + n_out]
    bind_sums(sums, ins, outs, refs[6 + n_in + n_out :])
    me, core = lax.axis_index("dp"), lax.axis_index("fsdp")
    meet(BITS)

    def small_copy(step):
        to = (me, 1 - core) if step == 0 else (flip(me, step - 1), core)
        return pltpu.make_async_remote_copy(
            src_ref=small_held.at[step], dst_ref=small_arrived.at[step],
            send_sem=small_send.at[step], recv_sem=small_recv.at[step],
            device_id=to, device_id_type=MESH,
        )

    small_held[0] = small[...]
    small_copy(0).start()
    for one in sums:
        one.begin()
    each = -(-len(steps) // (BITS + 1))
    for stage in range(BITS + 1):
        run_steps(sums, steps[stage * each : (stage + 1) * each])
        small_copy(stage).wait()
        value = small_held[stage] + small_arrived[stage]
        if stage < BITS:
            small_held[stage + 1] = value
            small_copy(stage + 1).start()
        else:
            small_total[...] = value
    for one in sums:
        one.finish()


def last_sums(sums, steps, small, ins, collective_id):
    vmem = pl.BlockSpec(memory_space=pltpu.VMEM)
    outs = [shape for one in sums for shape in one.out_shapes()]
    return pl.pallas_call(
        functools.partial(last_sums_kernel, sums, steps, (len(ins), len(outs))),
        name="last_sums",
        in_specs=[vmem] + [ANY] * len(ins),
        out_specs=[vmem] + [ANY] * len(outs),
        out_shape=[jax.ShapeDtypeStruct(small.shape, F32)] + outs,
        scratch_shapes=[
            pltpu.VMEM((BITS + 1, *small.shape), F32),
            pltpu.VMEM((BITS + 1, *small.shape), F32),
            pltpu.SemaphoreType.DMA((BITS + 1,)),
            pltpu.SemaphoreType.DMA((BITS + 1,)),
        ]
        + [shape for one in sums for shape in one.scratch()],
        compiler_params=pltpu.CompilerParams(
            collective_id=collective_id, has_side_effects=True, vmem_limit_bytes=VMEM_LIMIT
        ),
    )(small, *ins)


CORRECTION = 1.0 - 0.5**STEP


def adam(weight, first, second, grad, rate, decay):
    first = 0.5 * first + 0.5 * grad
    second = 0.5 * second + 0.5 * grad * grad
    step = first / CORRECTION / (jnp.sqrt(second / CORRECTION) + adam_eps)
    return weight - rate * (step + decay * weight), first, second


def adam_kernel(weight_ref, first_ref, second_ref, *refs):
    grad_refs, outs = refs[:-3], refs[-3:]
    for layer, grad_ref in enumerate(grad_refs):

        @pl.when(pl.program_id(0) == layer)
        def _():
            results = adam(
                weight_ref[0], first_ref[0], second_ref[0], grad_ref[0].astype(F32), D ** (-0.5), 0.1
            )
            for out, result in zip(outs, results):
                out[0] = result


def adam_step(weight, first, second, totals, base):
    layers, rows, width = weight.shape
    half = D // 2
    down, across = rows // half, width // D
    last = down * across - 1
    part = pl.BlockSpec((1, half, D), lambda l, i, j: (l, i, j))

    def grad_spec(layer):
        def at(l, i, j):
            inside = jnp.where(l < layer, 0, last)
            return (base + jnp.where(l == layer, i * across + j, inside), 0, 0)

        return pl.BlockSpec((1, half, D), at)

    return pl.pallas_call(
        adam_kernel,
        name="adam_step",
        grid=(layers, down, across),
        in_specs=[part] * 3 + [grad_spec(layer) for layer in range(layers)],
        out_specs=[part] * 3,
        out_shape=[jax.ShapeDtypeStruct(weight.shape, F32)] * 3,
        compiler_params=params(3),
    )(weight, first, second, *totals)


def per_device(dp, fsdp, *args):
    tokens, cotangent, segments, keep_mask = args[:4]
    masters, firsts, seconds = args[4::3], args[5::3], args[6::3]
    packs, length, width = tokens.shape
    layers = masters[0].shape[0]
    paired = (dp, fsdp) == (1 << BITS, 2)
    me = lax.axis_index("fsdp")
    own = jnp.zeros((1,), jnp.int32) + (me if paired else 0)

    def halves(shard):
        if paired:
            return shard, lax.ppermute(shard, "fsdp", [(0, 1), (1, 0)])
        full = lax.all_gather(shard, "fsdp", axis=0, tiled=True)
        return full[: full.shape[0] // 2], full[full.shape[0] // 2 :]

    gathered = [
        [halves(masters[kind][layer].astype(BF)) for kind in range(4)] for layer in range(layers)
    ]
    gains_all = lax.all_gather(masters[4].astype(BF), "fsdp", axis=1, tiled=True).astype(F32)
    gains_all = jnp.pad(gains_all.transpose(0, 2, 1), ((0, 0), (0, 4), (0, 0)))
    heads = (
        lax.broadcasted_iota(jnp.int32, (D, 128), 0) // HEAD_DIM
        == lax.broadcasted_iota(jnp.int32, (D, 128), 1)
    ).astype(BF)
    spread = heads.T
    seg = segments[0]
    code = jnp.where(keep_mask[0] == 1, seg, -1)

    hidden = tokens[0]
    stored = []
    for layer in range(layers):
        qkv, proj, up, down = gathered[layer]
        gains = gains_all[layer]
        saved = qkv_forward(own, hidden, gains, heads, spread, *qkv)
        q, k, v = saved[1:4]
        last = layer == layers - 1
        attended, middle, before, result = mix_forward(
            own, hidden, q, k, v, seg[:, None], code[None, :], gains,
            (*proj, *up, *down), BF if last else F32,
        )
        stored.append((hidden, saved, attended, middle, before))
        hidden = result
    output = hidden.reshape(tokens.shape)

    made, shared = None, None
    totals = []
    d_hidden = cotangent[0]
    small = [None] * layers
    leaves = [None] * (2 * layers)
    for order, (layer, kind) in enumerate(
        (layer, kind) for layer in reversed(range(layers)) for kind in ("ffn", "attn")
    ):
        qkv, proj, up, down = gathered[layer]
        gains = gains_all[layer]
        h, saved, attended, middle, before = stored[layer]
        sums, sum_ins = [], []
        if paired and shared is not None:
            sums.append(Sum("gather", shared[1]))
            sum_ins.append(shared[0])
        if paired and made is not None:
            sums.append(Sum("scatter", made[1]))
            sum_ins += made[0]
        plan = PLANS[order - 1] if sums else {}
        if kind == "ffn":
            results = ffn_backward(
                d_hidden, before, middle, gains, (*up, *down), paired, sums, plan, sum_ins, order
            )
            d_middle, gain_two = results[:2]
        else:
            results = attn_backward(
                d_middle, h, saved, attended, (seg[None, :], code[:, None]), gains, heads, spread,
                (*qkv, *proj), paired, sums, plan, sum_ins, order,
            )
            d_hidden, gain_rest = results[:2]
            gain_rest = gain_rest.reshape(3, 8, D).sum(1)
            small[layer] = jnp.stack([gain_rest[0], gain_two.sum(0), gain_rest[1], gain_rest[2]])
        results = results[2:]
        leaves[order] = results[0]
        if paired:
            made, results = (results[:2], ORDERS[order]), results[2:]
            if shared is not None:
                totals.append(results[0])
                results = results[1:]
            shared = (results[0], sums[-1].orders) if results else None
    small = jnp.concatenate(small)
    input_grad = d_hidden.reshape(tokens.shape)

    updated = []
    wide = masters[2].shape[2] // D
    if paired:
        sums = [Sum("gather", shared[1]), Sum("both", made[1])]
        small, *rest = last_sums(sums, LAST_STEPS, small, [shared[0], *made[0]], 2 * layers)
        totals += rest
        totals = list(reversed(totals))
        for kind, (which, base) in enumerate(((0, 0), (0, 3), (1, 0), (1, wide))):
            updated.append(
                adam_step(masters[kind], firsts[kind], seconds[kind], totals[which::2], base)
            )
    else:
        small = lax.psum(small, ("dp", "fsdp"))
        leaves = list(reversed(leaves))
        attn, ffn = jnp.stack(leaves[0::2]), jnp.stack(leaves[1::2])
        across = lambda x: x.transpose(0, 2, 1, 3).reshape(layers, D, -1)
        full = (
            across(attn[:, :3]),
            attn[:, 3],
            across(ffn[:, :wide]),
            ffn[:, wide:].reshape(layers, wide, 2, D // 2, D).transpose(0, 2, 1, 3, 4)
            .reshape(layers, wide * D, D),
        )
        for kind in range(4):
            grad = lax.psum_scatter(full[kind], "fsdp", scatter_dimension=1, tiled=True)
            grad = lax.psum(grad, "dp").astype(F32)
            updated.append(adam(masters[kind], firsts[kind], seconds[kind], grad, D ** (-0.5), 0.1))
    small = small.reshape(layers, 4, D).transpose(0, 2, 1)
    share = masters[4].shape[1]
    small = lax.dynamic_slice_in_dim(small, me * share, share, 1)
    updated.append(adam(masters[4], firsts[4], seconds[4], small, 0.5, 0.0))
    return (output, input_grad, *[x for group in updated for x in group])


ORDERS = (
    (ZXY, XYZ, ZXY, XYZ, YZX, YXZ),
    (XYZ, ZYX, YXZ),
    (ZXY, ZYX, XYZ, YZX, ZYX, YXZ),
    (YXZ, XZY, ZXY),
)
PLANS = (
    {
        2: ((0, 0), (1, 0), (2, 0), (3, 0), (4, 0),),
        3: ((5, 0),),
        4: ((4, 1), (1, 1), (0, 1), (3, 1),),
        5: ((2, 1), (0, 2), (1, 2), (4, 2), (5, 1), (3, 2),),
        6: ((2, 2),),
        7: ((0, 3), (1, 3),),
        8: ((4, 3), (3, 3), (5, 2), (2, 3),),
        9: ((5, 3),),
    },
    {
        2: ((0, 0),),
        3: ((6, 0), (1, 0), (2, 0), (3, 0), (4, 0), (5, 0), (8, 0), (0, 1),),
        5: ((2, 1), (4, 1), (6, 1), (1, 1),),
        6: ((3, 1), (5, 1), (7, 0),),
        7: ((8, 1), (6, 2), (0, 2), (1, 2), (4, 2),),
        9: ((2, 2), (6, 3),),
        10: ((8, 2), (5, 2),),
        11: ((3, 2), (7, 1),),
        13: ((8, 3),),
        14: ((1, 3),),
        15: ((7, 2), (0, 3), (4, 3), (7, 3), (2, 3), (5, 3), (3, 3),),
    },
    {
        0: ((0, 0), (1, 0), (2, 0), (5, 0),),
        1: ((1, 1),),
        3: ((6, 0), (0, 1), (2, 1),),
        4: ((8, 0), (5, 1), (1, 2),),
        5: ((2, 2), (0, 2), (3, 0), (4, 0), (8, 1),),
        6: ((7, 0),),
        7: ((5, 2), (6, 1), (8, 2),),
        8: ((3, 1), (4, 1), (5, 3), (8, 3), (6, 2), (0, 3), (1, 3), (7, 1), (2, 3),),
        9: ((3, 2), (4, 2), (6, 3), (7, 2),),
        12: ((3, 3), (4, 3), (7, 3),),
    },
)
LAST_STEPS = ((0, 0), (1, 0), (6, 0), (2, 0), (7, 0), (3, 0), (4, 0), (5, 0), (0, 1), (1, 1), (2, 1), (5, 1), (3, 1), (4, 1), (7, 1), (6, 1), (1, 2), (0, 2), (8, 0), (5, 2), (2, 2), (7, 2), (8, 1), (6, 2), (4, 2), (3, 2), (7, 3), (8, 2), (6, 3), (2, 3), (7, 4), (8, 3), (6, 4), (5, 3), (7, 5), (3, 3), (8, 4), (8, 5), (6, 5), (1, 3), (0, 3), (8, 6), (7, 6), (6, 6), (4, 3), (8, 7), (7, 7), (6, 7))


def solution(mesh):
    rows = P(("dp", "fsdp"), None, None)
    weight = P(None, "fsdp", None)
    flat = P(("dp", "fsdp"), None)
    return jax.shard_map(
        functools.partial(per_device, mesh.shape["dp"], mesh.shape["fsdp"]),
        mesh=mesh,
        in_specs=(rows, rows, flat, flat) + (weight,) * 15,
        out_specs=(rows, rows) + (weight,) * 15,
        check_vma=False,
    )
```

```python
import functools
import math

import jax
import jax.numpy as jnp
import numpy as np
from jax import lax
from jax.experimental import pallas as pl
from jax.experimental.pallas import tpu as pltpu
from jax.sharding import PartitionSpec as P

D = 768
HEADS = 12
HEAD_DIM = 64
STEP = 5
BF = jnp.bfloat16
F32 = jnp.float32
norm_eps = 1e-06
adam_eps = 1e-08
VMEM_LIMIT = 62 * 1024 * 1024
LOG2E = 1.4426950408889634
MASKED = -1e30


def dot(a, b):
    return lax.dot_general(a, b, (((1,), (0,)), ((), ())), preferred_element_type=F32)


def dot_nt(a, b):
    return lax.dot_general(a, b, (((1,), (1,)), ((), ())), preferred_element_type=F32)


def dot_tn(a, b):
    return lax.dot_general(a, b, (((0,), (0,)), ((), ())), preferred_element_type=F32)


def head_mean(x, mean_mat, exact=False):
    width = mean_mat.shape[0]
    found = []
    for at in range(0, x.shape[1], width):
        part = x[:, at : at + width]
        high = part.astype(BF)
        mean = dot(high, mean_mat)
        if exact:
            mean = mean + dot((part - high.astype(F32)).astype(BF), mean_mat)
        found.append(mean)
    return jnp.concatenate(found, axis=1)


def normalise(values):
    average = jnp.mean(values, axis=-1, keepdims=True)
    centred = values - average
    spread = jnp.mean(centred * centred, axis=-1, keepdims=True)
    scale = lax.rsqrt(spread + norm_eps)
    return centred * scale, scale


def norm_back(grad, gain, unit, scale):
    scaled = grad * gain
    first = jnp.mean(scaled, axis=-1, keepdims=True)
    second = jnp.mean(scaled * unit, axis=-1, keepdims=True)
    return scale * (scaled - first - unit * second)


def column_sum(x):
    return jnp.sum(x.reshape(x.shape[0] // 8, 8, x.shape[1]), axis=0)


def start_all(copies):
    for copy in copies:
        copy.start()


def wait_all(copies):
    for copy in copies:
        copy.wait()


def whole(shape):
    zeros = (0,) * len(shape)
    return pl.BlockSpec(shape, lambda *_: zeros, pipeline_mode=pl.Buffered(1))


ANY = pl.BlockSpec(memory_space=pl.ANY)
SMEM = pl.BlockSpec(memory_space=pltpu.SMEM)


def params(steps=1):
    return pltpu.CompilerParams(
        dimension_semantics=("arbitrary",) * steps, vmem_limit_bytes=VMEM_LIMIT
    )


MESH = pl.DeviceIdType.MESH

BITS = 4
XYZ, YXZ, ZXY, YZX, XZY, ZYX = (
    (0, 1, 2, 3), (1, 0, 2, 3), (2, 0, 1, 3), (1, 2, 0, 3), (0, 2, 1, 3), (2, 1, 0, 3),
)
GROUP, SPLIT = 4, 3
UNIT = GROUP * D // 2
WIDTH = D // SPLIT
FINAL = UNIT >> BITS


def flip(index, bit):
    size = 1 << bit
    return index + size * (1 - 2 * ((index // size) % 2))


def meet(partners):
    me, core = lax.axis_index("dp"), lax.axis_index("fsdp")
    barrier = pltpu.get_barrier_semaphore()
    pl.semaphore_signal(barrier, inc=1, device_id=(me, 1 - core), device_id_type=MESH)
    for bit in range(partners):
        pl.semaphore_signal(barrier, inc=1, device_id=(flip(me, bit), core), device_id_type=MESH)
    pl.semaphore_wait(barrier, 1 + partners)


def add_rows(target, source, at, other, other_at, rows):
    chunk = FINAL

    def body(i, carry):
        here = pl.ds(pl.multiple_of(at + i * chunk, chunk), chunk)
        there = pl.ds(pl.multiple_of(other_at + i * chunk, chunk), chunk)
        target[here, :] = (source[here, :].astype(F32) + other[there, :].astype(F32)).astype(BF)
        return carry

    lax.fori_loop(0, rows // chunk, body, 0)


class Sum:
    def __init__(self, kind, orders):
        self.kind, self.orders, self.count = kind, orders, len(orders)
        self.scatters = kind != "gather"
        self.gathers = kind != "scatter"

    def blocks(self):
        return GROUP * self.count // SPLIT

    def out_shapes(self):
        if self.gathers:
            return [jax.ShapeDtypeStruct((self.blocks(), D // 2, D), BF)]
        return [jax.ShapeDtypeStruct((self.count, FINAL, WIDTH), BF)]

    def inputs(self):
        return 2 if self.scatters else 1

    def scratch(self):
        n = self.count
        found = []
        if self.scatters:
            found += [
                pltpu.VMEM((n, UNIT, WIDTH), BF),
                pltpu.VMEM((n, UNIT - FINAL, WIDTH), BF),
                pltpu.VMEM((2, UNIT, WIDTH), BF),
                pltpu.SemaphoreType.DMA((n, 2 * GROUP)),
                pltpu.SemaphoreType.DMA((n, BITS)),
                pltpu.SemaphoreType.DMA((n, BITS)),
            ]
        if self.gathers:
            found += [
                pltpu.VMEM((n, UNIT, WIDTH), BF),
                pltpu.SemaphoreType.DMA((n, GROUP)),
                pltpu.SemaphoreType.DMA((n, BITS)),
                pltpu.SemaphoreType.DMA((n, BITS)),
            ]
        else:
            found += [pltpu.SemaphoreType.DMA((n,))]
        return found

    def bind(self, ins, outs, scratch):
        self.me, self.core = lax.axis_index("dp"), lax.axis_index("fsdp")
        self.ins, self.out = ins, outs[0]
        scratch = list(scratch)
        if self.scatters:
            self.held, self.arrived, self.stage, self.load, self.send, self.recv = scratch[:6]
            scratch = scratch[6:]
        if self.gathers:
            self.final, self.local, self.gsend, self.grecv = scratch
        else:
            self.local = scratch[0]

    def spans(self, unit):
        found, base, size = [], 0, UNIT
        for bit in self.orders[unit]:
            size = size // 2
            side = (self.me // (1 << bit)) % 2
            found.append((base + side * size, base + (1 - side) * size, size))
            base = base + side * size
        return found

    def window(self, ref, unit, side):
        block = GROUP * (unit // SPLIT) + side
        return ref.at[block, :, pl.ds((unit % SPLIT) * WIDTH, WIDTH)]

    def loads(self, unit):
        return [
            pltpu.make_async_copy(
                self.window(source, unit, side),
                target.at[pl.ds(side * (D // 2), D // 2)],
                self.load.at[unit, GROUP * which + side],
            )
            for which, (source, target) in enumerate(
                ((self.ins[0], self.held.at[unit]), (self.ins[1], self.stage.at[unit % 2]))
            )
            for side in range(GROUP)
        ]

    def scatter_copy(self, unit, step):
        _, give, size = self.spans(unit)[step]
        return pltpu.make_async_remote_copy(
            src_ref=self.held.at[unit, pl.ds(pl.multiple_of(give, size), size)],
            dst_ref=self.arrived.at[unit, pl.ds(UNIT - 2 * size, size)],
            send_sem=self.send.at[unit, step], recv_sem=self.recv.at[unit, step],
            device_id=(flip(self.me, self.orders[unit][step]), self.core), device_id_type=MESH,
        )

    def gather_copy(self, unit, step):
        keep, _, size = self.spans(unit)[step]
        place = pl.ds(pl.multiple_of(keep, size), size)
        return pltpu.make_async_remote_copy(
            src_ref=self.final.at[unit, place], dst_ref=self.final.at[unit, place],
            send_sem=self.gsend.at[unit, step], recv_sem=self.grecv.at[unit, step],
            device_id=(flip(self.me, self.orders[unit][step]), self.core), device_id_type=MESH,
        )

    def share_copy(self, unit):
        keep, _, size = self.spans(unit)[BITS - 1]
        place = pl.ds(pl.multiple_of(keep, size), size)
        if self.scatters:
            return pltpu.make_async_copy(self.held.at[unit, place], self.out.at[unit], self.local.at[unit])
        return pltpu.make_async_copy(self.ins[0].at[unit], self.final.at[unit, place], self.local.at[unit, 0])

    def outs(self, unit):
        return [
            pltpu.make_async_copy(
                self.final.at[unit, pl.ds(side * (D // 2), D // 2)],
                self.window(self.out, unit, side),
                self.local.at[unit, side],
            )
            for side in range(GROUP)
        ]

    def begin(self):
        if not self.scatters:
            for unit in range(self.count):
                self.share_copy(unit).start()
            for unit in range(self.count):
                self.share_copy(unit).wait()
                self.gather_copy(unit, BITS - 1).start()
            return
        for unit in range(min(2, self.count)):
            start_all(self.loads(unit))
        for unit in range(self.count):
            wait_all(self.loads(unit))
            add_rows(self.held.at[unit], self.held.at[unit], 0, self.stage.at[unit % 2], 0, UNIT)
            self.scatter_copy(unit, 0).start()
            if unit + 2 < self.count:
                start_all(self.loads(unit + 2))

    def stages(self):
        return BITS * (self.scatters + self.gathers)

    def advance(self, unit, stage):
        if self.scatters and stage < BITS:
            self.scatter_copy(unit, stage).wait()
            keep, _, size = self.spans(unit)[stage]
            landing = UNIT - 2 * size
            target = self.final if self.gathers and stage == BITS - 1 else self.held
            add_rows(target.at[unit], self.held.at[unit], keep, self.arrived.at[unit], landing, size)
            if stage < BITS - 1:
                self.scatter_copy(unit, stage + 1).start()
            elif self.gathers:
                self.gather_copy(unit, BITS - 1).start()
            else:
                self.share_copy(unit).start()
            return
        step = BITS - 1 - (stage - BITS * self.scatters)
        self.gather_copy(unit, step).wait()
        if step:
            self.gather_copy(unit, step - 1).start()
        else:
            start_all(self.outs(unit))

    def finish(self):
        for unit in range(self.count):
            if self.gathers:
                wait_all(self.outs(unit))
            else:
                self.share_copy(unit).wait()


def bind_sums(sums, ins, outs, scratch):
    ins, outs, scratch = list(ins), list(outs), list(scratch)
    for one in sums:
        a, b, c = one.inputs(), 1, len(one.scratch())
        one.bind(ins[:a], outs[:b], scratch[:c])
        ins, outs, scratch = ins[a:], outs[b:], scratch[c:]


def run_steps(sums, steps):
    owners = [(one, unit) for one in sums for unit in range(one.count)]
    for unit, stage in steps:
        one, own = owners[unit]
        one.advance(own, stage)


class Pull:
    def __init__(self, shapes):
        self.chunks = [
            (which, down, across)
            for which, (downs, acrosses) in enumerate(shapes)
            for down in range(downs)
            for across in range(acrosses)
        ]
        self.shapes = shapes

    def scratch(self):
        n = len(self.chunks)
        return [
            pltpu.VMEM((3, D // 2, D), F32),
            pltpu.SemaphoreType.DMA((n,)),
            pltpu.SemaphoreType.DMA((n,)),
            pltpu.SemaphoreType.DMA((n,)),
        ]

    def bind(self, layer, sources, targets, scratch):
        self.layer, self.sources, self.targets = layer, sources, targets
        self.stage, self.loads, self.sends, self.recvs = scratch
        self.me, self.core = lax.axis_index("dp"), lax.axis_index("fsdp")

    def load(self, i):
        which, down, across = self.chunks[i]
        layer = self.layer[which]
        return pltpu.make_async_copy(
            self.sources[which].at[layer, pl.ds(down * (D // 2), D // 2), pl.ds(across * D, D)],
            self.stage.at[i % 3],
            self.loads.at[i],
        )

    def place(self, i):
        which, down, across = self.chunks[i]
        half = D // 2
        first = pl.multiple_of(self.core * (self.shapes[which][0] * half) + down * half, half)
        return pl.ds(first, half), pl.ds(across * D, D)

    def push(self, i):
        place = self.targets[self.chunks[i][0]].at[self.place(i)]
        return pltpu.make_async_remote_copy(
            src_ref=place, dst_ref=place, send_sem=self.sends.at[i], recv_sem=self.recvs.at[i],
            device_id=(self.me, 1 - self.core), device_id_type=MESH,
        )

    def begin(self):
        for i in range(min(3, len(self.chunks))):
            self.load(i).start()

    def turn(self, i):
        self.load(i).wait()
        self.targets[self.chunks[i][0]][self.place(i)] = self.stage[i % 3].astype(BF)
        self.push(i).start()
        if i + 3 < len(self.chunks):
            self.load(i + 3).start()

    def of(self, which):
        return [i for i, chunk in enumerate(self.chunks) if chunk[0] == which]

    def arrive(self, which):
        for i in self.of(which):
            self.push(i).wait()


def qkv_kernel(pull, h_ref, gain_ref, mean_ref, source, *refs):
    normed_ref, q_ref, k_ref, v_ref, scale_q_ref, scale_k_ref, full_ref = refs[:7]
    weight, sem = refs[7:9]
    step = pl.program_id(0)
    keep = pltpu.make_async_copy(weight, full_ref, sem)
    load = pltpu.make_async_copy(source, weight, sem)
    if pull:
        pull.bind([0], [source], [weight], refs[9:])

    @pl.when(step == 0)
    def _():
        if pull:
            pull.begin()
            meet(0)
            for i in range(len(pull.chunks)):
                pull.turn(i)
        else:
            load.start()

    unit, _ = normalise(h_ref[...].astype(F32))
    normed = (unit * gain_ref[0:1, :]).astype(BF)
    normed_ref[...] = normed

    @pl.when(step == 0)
    def _():
        if pull:
            pull.arrive(0)
            keep.start()
        else:
            load.wait()

    v_ref[...] = dot(normed, weight[:, 2 * D :]).astype(BF)
    for part, out_ref, scale_ref in ((0, q_ref, scale_q_ref), (1, k_ref, scale_k_ref)):
        raw = dot(normed, weight[:, part * D : (part + 1) * D])
        centred = raw - head_mean(raw, mean_ref[...], exact=True)
        scale = lax.rsqrt(head_mean(centred * centred, mean_ref[...]) + norm_eps)
        out_ref[...] = (centred * scale * gain_ref[2 + part : 3 + part, :]).astype(BF)
        scale_ref[...] = scale.astype(BF)

    if pull:

        @pl.when(step == pl.num_programs(0) - 1)
        def _():
            keep.wait()


def qkv_forward(h, gains, mean_mat, source, fresh, collective_id):
    rows = h.shape[0]
    block = min(512, rows)
    row = lambda width: pl.BlockSpec((block, width), lambda i: (i, 0))
    pull = Pull([(1, 3)]) if fresh else None
    full = [jax.ShapeDtypeStruct((D, 3 * D), BF)]
    results = pl.pallas_call(
        functools.partial(qkv_kernel, pull) if fresh else functools.partial(qkv_plain_kernel),
        name="qkv_forward",
        grid=(rows // block,),
        in_specs=[row(D), whole(gains.shape), whole(mean_mat.shape), ANY],
        out_specs=[row(D)] * 6 + [ANY] * fresh,
        out_shape=[jax.ShapeDtypeStruct((rows, D), BF)] * 6 + full * fresh,
        scratch_shapes=[pltpu.VMEM((D, 3 * D), BF), pltpu.SemaphoreType.DMA]
        + (pull.scratch() if fresh else []),
        compiler_params=remote_params(fresh, collective_id),
    )(h, gains, mean_mat, source)
    return results if fresh else [*results, source]


def qkv_plain_kernel(h_ref, gain_ref, mean_ref, source, *refs):
    qkv_kernel(None, h_ref, gain_ref, mean_ref, source, *refs[:6], source, *refs[6:])


def window_at(block, count):
    return block - 1 + (count - 1 - block) // (count - 1) - block // (count - 1)


def pair_stack(x, low_lanes):
    zero = jnp.zeros_like(x)
    return jnp.concatenate([jnp.where(low_lanes, x, zero), jnp.where(low_lanes, zero, x)], axis=0)


def mix_kernel(
    tile, reach, pull, layer, follow, n_source,
    h_ref, q_ref, k_ref, v_ref, seg_ref, code_ref, gain_ref, *refs,
):
    sources, outs, follows, scratch, pull_scratch = carve(
        refs, n_source, 4 + (3 if pull else 0), int(follow), 4 + int(follow), len(refs)
    )
    attended_ref, middle_ref, before_ref, out_ref = outs[:4]
    proj, up, down, sems = scratch[:4]
    weights = (proj, up, down)
    if pull:
        targets = list(weights) + ([scratch[4]] if follow else [])
        pull.bind([layer] * 3 + [layer + 1] * follow, sources, targets, pull_scratch)
        keeps = [
            pltpu.make_async_copy(weight, full, sems.at[i])
            for i, (weight, full) in enumerate(zip(targets, outs[4:] + follows))
        ]
    else:
        loads = [
            pltpu.make_async_copy(source, weight, sems.at[i])
            for i, (source, weight) in enumerate(zip(sources, weights))
        ]
    step = pl.program_id(0)
    count = k_ref.shape[0] // tile
    keys = reach * tile
    factor = LOG2E * HEAD_DIM ** (-0.5)
    low_lanes = lax.broadcasted_iota(jnp.int32, (tile, 128), 1) < HEAD_DIM

    @pl.when(step == 0)
    def _():
        if pull:
            pull.begin()
            meet(0)
        else:
            start_all(loads)

    @pl.when(step < count)
    def _():
        first = pl.multiple_of(window_at(step, count) * tile if count > reach else 0, tile)
        window = pl.ds(first, keys)
        here = pl.ds(pl.multiple_of(step * tile, tile), tile)
        seg = seg_ref[here, :]
        code = code_ref[:, window]
        query_at = step * tile + lax.broadcasted_iota(jnp.int32, (tile, keys), 0)
        key_at = first + lax.broadcasted_iota(jnp.int32, (tile, keys), 1)
        bias = jnp.where((seg == code) | (query_at == key_at), 0.0, MASKED)
        bias = jnp.concatenate([bias, bias], axis=0)
        for pair in range(HEADS // 2):
            lanes = slice(pair * 128, (pair + 1) * 128)
            queries = pair_stack(q_ref[here, lanes], low_lanes)
            scores = dot_nt(queries, k_ref[window, lanes])
            expo = jnp.exp2(scores * factor + bias)
            total = jnp.sum(expo, axis=-1, keepdims=True)
            mixed = dot(expo.astype(BF), v_ref[window, lanes]) * (1.0 / total)
            attended_ref[here, lanes] = jnp.where(low_lanes, mixed[:tile], mixed[tile:]).astype(BF)

    if pull:
        per_step = -(-len(pull.chunks) // count)
        for turn in range(count):
            mine = range(turn * per_step, min((turn + 1) * per_step, len(pull.chunks)))
            if mine:

                @pl.when(step == turn)
                def _():
                    for i in mine:
                        pull.turn(i)

    @pl.when(step == count)
    def _():
        if pull:
            for which in range(3):
                pull.arrive(which)
                keeps[which].start()
        else:
            wait_all(loads)

    @pl.when(step >= count)
    def _():
        rows = h_ref.shape[0]
        here = pl.ds(pl.multiple_of((step - count) * rows, rows), rows)
        middle = h_ref[...].astype(F32) + dot(attended_ref[here, :], proj[...])
        middle_ref[...] = middle
        unit, _ = normalise(middle)
        normed = (unit * gain_ref[1:2, :]).astype(BF)
        result = middle
        for part in range(up.shape[1] // D):
            lanes = slice(part * D, (part + 1) * D)
            before = dot(normed, up[:, lanes])
            before_ref[:, lanes] = before.astype(BF)
            active = jax.nn.gelu(before, approximate=True).astype(BF)
            result = result + dot(active, down[lanes, :])
        out_ref[...] = result.astype(out_ref.dtype)

    if pull:

        @pl.when(step == pl.num_programs(0) - 1)
        def _():
            if follow:
                pull.arrive(3)
                keeps[3].start()
            wait_all(keeps)


def mix_forward(h, q, k, v, seg, code, gains, sources, out_type, layer, paired, collective_id):
    rows = h.shape[0]
    block = min(512, rows)
    tile = min(128, rows)
    reach = min(3, rows // tile)
    count = rows // tile
    width = sources[1].shape[-1]
    follow = len(sources) > 3
    shapes = [(1, 1), (1, width // D), (width // D, 1)] + [(1, 3)] * follow
    pull = Pull(shapes) if paired else None
    row = lambda w: pl.BlockSpec((block, w), lambda i: (jnp.maximum(i - count, 0), 0))
    outs = [(D, F32), (width, BF), (D, out_type)]
    fulls = [(D, D), (D, width), (width, D)]
    follows = [(D, 3 * D)] * follow
    results = pl.pallas_call(
        functools.partial(mix_kernel, tile, reach, pull, layer, follow, len(sources)),
        name="mix_forward",
        grid=(count + rows // block,),
        in_specs=[row(D)] + [whole(x.shape) for x in (q, k, v, seg, code, gains)] + [ANY] * len(sources),
        out_specs=[pl.BlockSpec((rows, D), lambda i: (0, 0), pipeline_mode=pl.Buffered(1))]
        + [row(w) for w, _ in outs]
        + [ANY] * (len(fulls + follows) if paired else 0),
        out_shape=[jax.ShapeDtypeStruct((rows, D), BF)]
        + [jax.ShapeDtypeStruct((rows, w), t) for w, t in outs]
        + [jax.ShapeDtypeStruct(x, BF) for x in (fulls + follows if paired else [])],
        scratch_shapes=[pltpu.VMEM(x, BF) for x in fulls]
        + [pltpu.SemaphoreType.DMA((4,))]
        + [pltpu.VMEM(x, BF) for x in follows]
        + (pull.scratch() if paired else []),
        compiler_params=remote_params(paired, collective_id),
    )(h, q, k, v, seg, code, gains, *sources)
    return results if paired else [*results, *sources]


class Blocks:
    def __init__(self, count, paired):
        self.count, self.paired = count, paired

    def out_shapes(self):
        rows = D // 2 if self.paired else D
        return [jax.ShapeDtypeStruct((self.count, rows, D), BF)] * (1 + self.paired)

    def scratch(self):
        return [pltpu.SemaphoreType.DMA((self.count,))] * (1 + 2 * self.paired)

    def bind(self, outs, sems):
        self.outs, self.sems = outs, sems

    def copies(self, block, lanes, ref, first_row):
        if not self.paired:
            return [
                pltpu.make_async_copy(
                    ref.at[pl.ds(first_row, D), lanes], self.outs[0].at[block], self.sems[0].at[block]
                )
            ]
        core = lax.axis_index("fsdp")
        half = D // 2
        mine = pl.multiple_of(first_row + core * half, half)
        theirs = pl.multiple_of(first_row + (1 - core) * half, half)
        return [
            pltpu.make_async_copy(
                ref.at[pl.ds(mine, half), lanes], self.outs[0].at[block], self.sems[0].at[block]
            ),
            pltpu.make_async_remote_copy(
                src_ref=ref.at[pl.ds(theirs, half), lanes], dst_ref=self.outs[1].at[block],
                send_sem=self.sems[1].at[block], recv_sem=self.sems[2].at[block],
                device_id=(lax.axis_index("dp"), 1 - core), device_id_type=MESH,
            ),
        ]


def carve(refs, *sizes):
    found, at = [], 0
    for size in sizes:
        found.append(refs[at : at + size])
        at += size
    return found


def sums_in(sums):
    return sum(one.inputs() for one in sums)


def sums_scratch(sums):
    return [shape for one in sums for shape in one.scratch()]


def sums_outs(sums):
    return [shape for one in sums for shape in one.out_shapes()]


def remote_params(paired, collective_id):
    if not paired:
        return params()
    return pltpu.CompilerParams(
        dimension_semantics=("arbitrary",), vmem_limit_bytes=VMEM_LIMIT,
        collective_id=collective_id, has_side_effects=True,
    )


def ffn_back_kernel(blocks, store, sums, plan, dh_ref, before_ref, middle_ref, gain_ref, *refs):
    weights, ins, outs, store_outs, sum_outs, own_scratch, store_sems, sum_scratch = carve(
        refs, 2, sums_in(sums), 2, 1 + store.paired, len(sums), 7, 1 + 2 * store.paired,
        len(sums_scratch(sums)),
    )
    dmid_ref, dgain_ref = outs
    up, down, active, dbefore, dbranch, normed, sems = own_scratch
    store.bind(store_outs, store_sems)
    bind_sums(sums, ins, sum_outs, sum_scratch)
    step = pl.program_id(0)
    copies = [
        pltpu.make_async_copy(source, target, sems.at[i])
        for i, (source, target) in enumerate(zip(weights, (up, down)))
    ]
    parts = up.shape[1] // D
    rows = dh_ref.shape[0]

    @pl.when(step == 0)
    def _():
        start_all(copies)
        dgain_ref[...] = jnp.zeros_like(dgain_ref)
        if store.paired:
            meet(BITS if sums else 0)
        for one in sums:
            one.begin()

    @pl.when(step < blocks)
    def _():
        here = pl.ds(pl.multiple_of(step * rows, rows), rows)
        dh = dh_ref[...].astype(F32)
        branch = dh.astype(BF)
        dbranch[here, :] = branch
        gain = gain_ref[1:2, :]
        unit, scale = normalise(middle_ref[...])
        normed[here, :] = (unit * gain).astype(BF)

        @pl.when(step == 0)
        def _():
            wait_all(copies)

        dnormed = jnp.zeros((rows, D), F32)
        for part in range(parts):
            lanes = slice(part * D, (part + 1) * D)
            dactive = dot_nt(branch, down[lanes, :])
            value = before_ref[:, lanes].astype(F32)
            root = math.sqrt(2.0 / math.pi)
            square = value * value
            curve = jnp.tanh(value * (root + (root * 0.044715) * square))
            half = 0.5 * (1.0 + curve)
            active[here, lanes] = (value * half).astype(BF)
            slope = half + (0.5 * value) * (1.0 - curve * curve) * (
                root + (3.0 * 0.044715 * root) * square
            )
            dpart = (dactive * slope).astype(BF)
            dbefore[here, lanes] = dpart
            dnormed = dnormed + dot_nt(dpart, up[:, lanes])
            for block in range(blocks):
                if block * parts + part in plan:

                    @pl.when(step == block)
                    def _():
                        run_steps(sums, plan[block * parts + part])

        dmid_ref[...] = dh + norm_back(dnormed, gain, unit, scale)
        dgain_ref[...] += column_sum(dnormed * unit)

    late = blocks * parts - blocks
    for tick in sorted(plan):
        if tick >= blocks * parts:

            @pl.when(step == tick - late)
            def _():
                run_steps(sums, plan[tick])

    every = slice(0, D)

    @pl.when((step >= blocks) & (step < blocks + parts))
    def _():
        part = step - blocks
        lanes = pl.ds(pl.multiple_of(part * D, D), D)
        up[:, lanes] = dot_tn(normed[...], dbefore[:, lanes]).astype(BF)
        start_all(store.copies(part, lanes, up, 0))

    @pl.when(step >= blocks + parts)
    def _():
        part = step - blocks - parts
        half = D // 2
        base = down.shape[0] // 2
        first_row = pl.multiple_of(part * D, D)
        for side in range(2):
            lanes = pl.ds(pl.multiple_of(side * base + part * half, half), half)
            here = pl.ds(pl.multiple_of(first_row + side * half, half), half)
            down[here, :] = dot_tn(active[:, lanes], dbranch[...]).astype(BF)
        start_all(store.copies(parts + part, every, down, first_row))

    @pl.when(step == blocks + 2 * parts - 1)
    def _():
        for part in range(parts):
            wait_all(store.copies(part, slice(part * D, (part + 1) * D), up, 0))
        for part in range(parts):
            wait_all(store.copies(parts + part, every, down, part * D))
        for one in sums:
            one.finish()


def ffn_backward(dh, before, middle, gains, shards, paired, sums, plan, sum_ins, collective_id):
    rows, width = before.shape
    block = min(512, rows)
    blocks = rows // block
    parts = width // D
    store = Blocks(2 * parts, paired)
    row = lambda w, **mode: pl.BlockSpec((block, w), lambda i: (jnp.minimum(i, blocks - 1), 0), **mode)
    once = {"pipeline_mode": pl.Buffered(1)}
    outs = store.out_shapes() + sums_outs(sums)
    return pl.pallas_call(
        functools.partial(ffn_back_kernel, blocks, store, sums, plan),
        name="ffn_backward",
        grid=(blocks + 2 * parts,),
        in_specs=[row(D, **once), row(width), row(D, **once), whole(gains.shape)] + [ANY] * (2 + len(sum_ins)),
        out_specs=[row(D), pl.BlockSpec((8, D), lambda i: (0, 0))] + [ANY] * len(outs),
        out_shape=[jax.ShapeDtypeStruct((rows, D), F32), jax.ShapeDtypeStruct((8, D), F32)] + outs,
        scratch_shapes=[
            pltpu.VMEM((D, width), BF),
            pltpu.VMEM((width, D), BF),
            pltpu.VMEM((rows, width), BF),
            pltpu.VMEM((rows, width), BF),
            pltpu.VMEM((rows, D), BF),
            pltpu.VMEM((rows, D), BF),
            pltpu.SemaphoreType.DMA((2,)),
        ]
        + store.scratch()
        + sums_scratch(sums),
        compiler_params=remote_params(paired, collective_id),
    )(dh, before, middle, gains, *shards, *sum_ins)


def attn_back_kernel(
    tile, reach, rows, store, sums, plan,
    dmid_ref, h_ref, q_ref, k_ref, v_ref, scale_q_ref, scale_k_ref,
    attended_ref, seg_ref, code_ref, gain_ref, heads_ref, mean_ref, *refs,
):
    weights, ins, outs, store_outs, sum_outs, own_scratch, store_sems, sum_scratch = carve(
        refs, 3, sums_in(sums), 2, 1 + store.paired, len(sums), 9, 1 + 2 * store.paired,
        len(sums_scratch(sums)),
    )
    normed_ref, qkv_ref, proj_ref = weights
    dh_ref, dgain_ref = outs
    qkv, proj, dattended, inner, dk, dv, dmixed, sems, normed_sem = own_scratch
    store.bind(store_outs, store_sems)
    bind_sums(sums, ins, sum_outs, sum_scratch)
    step = pl.program_id(0)
    total_rows = k_ref.shape[0]
    count = total_rows // tile
    keys = reach * tile
    blocks = total_rows // rows
    proj_copy = pltpu.make_async_copy(proj_ref, proj, sems.at[0])
    qkv_copy = pltpu.make_async_copy(qkv_ref, qkv, sems.at[1])
    normed_copy = pltpu.make_async_copy(normed_ref, dattended, normed_sem)
    root = HEAD_DIM ** (-0.5)

    def head_norm_back(grad, gain, unit, scale):
        scaled = grad * gain
        first = head_mean(scaled, mean_ref[...])
        second = head_mean(scaled * unit, mean_ref[...])
        return scale.astype(F32) * (scaled - first - unit * second)

    @pl.when(step == 0)
    def _():
        proj_copy.start()
        qkv_copy.start()
        dgain_ref[...] = jnp.zeros_like(dgain_ref)
        dk[...] = jnp.zeros_like(dk)
        dv[...] = jnp.zeros_like(dv)
        if store.paired:
            meet(BITS if sums else 0)
        for one in sums:
            one.begin()
        proj_copy.wait()
        for block in range(blocks):
            here = slice(block * rows, (block + 1) * rows)
            back = dot_nt(dmid_ref[here, :].astype(BF), proj[...]).astype(BF)
            dattended[here, :] = back
            product = back.astype(F32) * attended_ref[here, :].astype(F32)
            high = product.astype(BF)
            low = (product - high.astype(F32)).astype(BF)
            turn = (((0,), (1,)), ((), ()))
            inner[:, here] = lax.dot_general(
                heads_ref[...], high, turn, preferred_element_type=F32
            ) + lax.dot_general(heads_ref[...], low, turn, preferred_element_type=F32)

    for tick in sorted(plan):

        @pl.when(step == tick)
        def _():
            run_steps(sums, plan[tick])

    @pl.when(step < count)
    def _():
        first = pl.multiple_of(window_at(step, count) * tile if count > reach else 0, tile)
        window = pl.ds(first, keys)
        here = pl.ds(pl.multiple_of(step * tile, tile), tile)
        low_lanes = lax.broadcasted_iota(jnp.int32, (tile, 128), 1) < HEAD_DIM
        seg = seg_ref[:, here]
        code = code_ref[window, :]
        key_at = first + lax.broadcasted_iota(jnp.int32, (keys, tile), 0)
        query_at = step * tile + lax.broadcasted_iota(jnp.int32, (keys, tile), 1)
        bias = jnp.where((seg == code) | (query_at == key_at), 0.0, MASKED)
        bias = jnp.concatenate([bias, bias], axis=1)
        dq_parts = []
        for pair in range(HEADS // 2):
            lanes = slice(pair * 128, (pair + 1) * 128)
            queries = pair_stack(q_ref[here, lanes], low_lanes)
            grads = pair_stack(dattended[here, lanes], low_lanes)
            keys_part = k_ref[window, lanes]
            scores = dot_nt(keys_part, queries)
            expo = jnp.exp2(scores * (LOG2E * root) + bias)
            probs = expo * (1.0 / jnp.sum(expo, axis=0, keepdims=True))
            dprobs = dot_nt(v_ref[window, lanes], grads)
            less = jnp.concatenate(
                [inner[2 * pair : 2 * pair + 1, here], inner[2 * pair + 1 : 2 * pair + 2, here]],
                axis=1,
            )
            dscores = (probs * (dprobs - less)).astype(BF)
            dv[window, lanes] += dot(probs.astype(BF), grads)
            dk[window, lanes] += dot(dscores, queries)
            dq = dot_tn(dscores, keys_part)
            dq_parts.append(jnp.where(low_lanes, dq[:tile], dq[tile:]))
        dq = jnp.concatenate(dq_parts, axis=1) * root
        gain = gain_ref[2:3, :]
        unit = q_ref[here, :].astype(F32) * (1.0 / gain)
        dmixed[here, 0:D] = head_norm_back(dq, gain, unit, scale_q_ref[here, :]).astype(BF)
        dgain_ref[8:16, :] += column_sum(dq * unit)

    @pl.when(step == count)
    def _():
        normed_copy.start()
        qkv_copy.wait()

    @pl.when((step >= count) & (step < count + blocks))
    def _():
        here = pl.ds(pl.multiple_of((step - count) * rows, rows), rows)
        grad = dk[here, :] * root
        gain = gain_ref[3:4, :]
        unit = k_ref[here, :].astype(F32) * (1.0 / gain)
        dmixed[here, D : 2 * D] = head_norm_back(grad, gain, unit, scale_k_ref[here, :]).astype(BF)
        dgain_ref[16:24, :] += column_sum(grad * unit)
        dmixed[here, 2 * D :] = dv[here, :].astype(BF)
        dnormed = dot_nt(dmixed[here, :], qkv[...])
        unit, scale = normalise(h_ref[here, :].astype(F32))
        dh_ref[...] = dmid_ref[here, :] + norm_back(dnormed, gain_ref[0:1, :], unit, scale)
        dgain_ref[0:8, :] += column_sum(dnormed * unit)

    @pl.when(step == count + blocks)
    def _():
        normed_copy.wait()

    @pl.when((step >= count + blocks) & (step < count + blocks + 3))
    def _():
        part = step - count - blocks
        lanes = pl.ds(pl.multiple_of(part * D, D), D)
        qkv[:, lanes] = dot_tn(dattended[...], dmixed[:, lanes]).astype(BF)
        start_all(store.copies(part, lanes, qkv, 0))

    every = slice(0, D)

    @pl.when(step == count + blocks + 3)
    def _():
        proj[...] = dot_tn(attended_ref[...], dmid_ref[...].astype(BF)).astype(BF)
        start_all(store.copies(3, every, proj, 0))
        for part in range(3):
            wait_all(store.copies(part, slice(part * D, (part + 1) * D), qkv, 0))
        wait_all(store.copies(3, every, proj, 0))
        for one in sums:
            one.finish()


def attn_backward(
    dmid, h, saved, attended, segs, gains, heads, mean_mat, shards, paired, sums, plan, sum_ins, collective_id
):
    total = h.shape[0]
    rows = min(512, total)
    tile = min(128, total)
    reach = min(3, total // tile)
    count, blocks = total // tile, total // rows
    normed, q, k, v, scale_q, scale_k = saved
    ins = [dmid, h, q, k, v, scale_q, scale_k, attended, *segs, gains, heads, mean_mat]
    store = Blocks(4, paired)
    outs = store.out_shapes() + sums_outs(sums)
    return pl.pallas_call(
        functools.partial(attn_back_kernel, tile, reach, rows, store, sums, plan),
        name="attn_backward",
        grid=(count + blocks + 4,),
        in_specs=[whole(x.shape) for x in ins] + [ANY] * (3 + len(sum_ins)),
        out_specs=[
            pl.BlockSpec((rows, D), lambda i: (jnp.clip(i - count, 0, blocks - 1), 0)),
            pl.BlockSpec((24, D), lambda i: (0, 0)),
        ]
        + [ANY] * len(outs),
        out_shape=[jax.ShapeDtypeStruct((total, D), F32), jax.ShapeDtypeStruct((24, D), F32)] + outs,
        scratch_shapes=[
            pltpu.VMEM((D, 3 * D), BF),
            pltpu.VMEM((D, D), BF),
            pltpu.VMEM((total, D), BF),
            pltpu.VMEM((128, total), F32),
            pltpu.VMEM((total, D), F32),
            pltpu.VMEM((total, D), F32),
            pltpu.VMEM((total, 3 * D), BF),
            pltpu.SemaphoreType.DMA((2,)),
            pltpu.SemaphoreType.DMA,
        ]
        + store.scratch()
        + sums_scratch(sums),
        compiler_params=remote_params(paired, collective_id),
    )(*ins, normed, *shards, *sum_ins)


def last_sums_kernel(sums, steps, counts, *refs):
    n_in, n_out = counts
    small, ins = refs[0], refs[1 : 1 + n_in]
    small_total, outs = refs[1 + n_in], refs[2 + n_in : 2 + n_in + n_out]
    small_held, small_arrived, small_send, small_recv = refs[2 + n_in + n_out : 6 + n_in + n_out]
    bind_sums(sums, ins, outs, refs[6 + n_in + n_out :])
    me, core = lax.axis_index("dp"), lax.axis_index("fsdp")
    meet(BITS)

    def small_copy(step):
        to = (me, 1 - core) if step == 0 else (flip(me, step - 1), core)
        return pltpu.make_async_remote_copy(
            src_ref=small_held.at[step], dst_ref=small_arrived.at[step],
            send_sem=small_send.at[step], recv_sem=small_recv.at[step],
            device_id=to, device_id_type=MESH,
        )

    small_held[0] = small[...]
    small_copy(0).start()
    for one in sums:
        one.begin()
    each = -(-len(steps) // (BITS + 1))
    for stage in range(BITS + 1):
        run_steps(sums, steps[stage * each : (stage + 1) * each])
        small_copy(stage).wait()
        value = small_held[stage] + small_arrived[stage]
        if stage < BITS:
            small_held[stage + 1] = value
            small_copy(stage + 1).start()
        else:
            small_total[...] = value
    for one in sums:
        one.finish()


def last_sums(sums, steps, small, ins, collective_id):
    vmem = pl.BlockSpec(memory_space=pltpu.VMEM)
    outs = [shape for one in sums for shape in one.out_shapes()]
    return pl.pallas_call(
        functools.partial(last_sums_kernel, sums, steps, (len(ins), len(outs))),
        name="last_sums",
        in_specs=[vmem] + [ANY] * len(ins),
        out_specs=[vmem] + [ANY] * len(outs),
        out_shape=[jax.ShapeDtypeStruct(small.shape, F32)] + outs,
        scratch_shapes=[
            pltpu.VMEM((BITS + 1, *small.shape), F32),
            pltpu.VMEM((BITS + 1, *small.shape), F32),
            pltpu.SemaphoreType.DMA((BITS + 1,)),
            pltpu.SemaphoreType.DMA((BITS + 1,)),
        ]
        + [shape for one in sums for shape in one.scratch()],
        compiler_params=pltpu.CompilerParams(
            collective_id=collective_id, has_side_effects=True, vmem_limit_bytes=VMEM_LIMIT
        ),
    )(small, *ins)


CORRECTION = 1.0 - 0.5**STEP


def adam(weight, first, second, grad, rate, decay):
    first = 0.5 * first + 0.5 * grad
    second = 0.5 * second + 0.5 * grad * grad
    step = first / CORRECTION / (jnp.sqrt(second / CORRECTION) + adam_eps)
    return weight - rate * (step + decay * weight), first, second


def adam_kernel(weight_ref, first_ref, second_ref, *refs):
    grad_refs, outs = refs[:-3], refs[-3:]
    for layer, grad_ref in enumerate(grad_refs):

        @pl.when(pl.program_id(0) == layer)
        def _():
            results = adam(
                weight_ref[0], first_ref[0], second_ref[0], grad_ref[0].astype(F32), D ** (-0.5), 0.1
            )
            for out, result in zip(outs, results):
                out[0] = result


def adam_step(weight, first, second, totals, base):
    layers, rows, width = weight.shape
    half = D // 2
    down, across = rows // half, width // D
    last = down * across - 1
    part = pl.BlockSpec((1, half, D), lambda l, i, j: (l, i, j))

    def grad_spec(layer):
        def at(l, i, j):
            inside = jnp.where(l < layer, 0, last)
            return (base + jnp.where(l == layer, i * across + j, inside), 0, 0)

        return pl.BlockSpec((1, half, D), at)

    return pl.pallas_call(
        adam_kernel,
        name="adam_step",
        grid=(layers, down, across),
        in_specs=[part] * 3 + [grad_spec(layer) for layer in range(layers)],
        out_specs=[part] * 3,
        out_shape=[jax.ShapeDtypeStruct(weight.shape, F32)] * 3,
        compiler_params=params(3),
    )(weight, first, second, *totals)


def per_device(dp, fsdp, *args):
    tokens, cotangent, segments, keep_mask = args[:4]
    masters, firsts, seconds = args[4::3], args[5::3], args[6::3]
    packs, length, width = tokens.shape
    layers = masters[0].shape[0]
    paired = (dp, fsdp) == (1 << BITS, 2)
    me = lax.axis_index("fsdp")

    def gather(shard):
        return lax.all_gather(shard.astype(BF), "fsdp", axis=0, tiled=True)

    gains_all = lax.all_gather(masters[4].astype(BF), "fsdp", axis=1, tiled=True).astype(F32)
    gains_all = jnp.pad(gains_all.transpose(0, 2, 1), ((0, 0), (0, 4), (0, 0)))
    channel = np.arange(D) // HEAD_DIM
    heads = (channel[:, None] == np.arange(128)[None, :]).astype(BF)
    mean_mat = ((channel[:256, None] == channel[None, :256]) / HEAD_DIM).astype(BF)
    seg = segments[0]
    code = jnp.where(keep_mask[0] == 1, seg, -1)

    hidden = tokens[0]
    stored, held = [], []
    qkv = masters[0] if paired else gather(masters[0][0])
    for layer in range(layers):
        gains = gains_all[layer]
        last = layer == layers - 1
        fresh = paired and layer == 0
        *saved, qkv = qkv_forward(hidden, gains, mean_mat, qkv, fresh, 2 * layers + 1)
        q, k, v = saved[1:4]
        if paired:
            sources = [masters[kind] for kind in (1, 2, 3)] + ([] if last else [masters[0]])
        else:
            sources = [gather(masters[kind][layer]) for kind in (1, 2, 3)]
        attended, middle, before, result, proj, up, down, *following = mix_forward(
            hidden, q, k, v, seg[:, None], code[None, :], gains, sources, BF if last else F32,
            layer, paired, 2 * layers + 2 + layer,
        )
        stored.append((hidden, saved, attended, middle, before))
        held.append((qkv, proj, up, down))
        hidden = result
        if not last:
            qkv = following[0] if paired else gather(masters[0][layer + 1])
    output = hidden.reshape(tokens.shape)

    made, shared = None, None
    totals = []
    d_hidden = cotangent[0]
    small = [None] * layers
    leaves = [None] * (2 * layers)
    for order, (layer, kind) in enumerate(
        (layer, kind) for layer in reversed(range(layers)) for kind in ("ffn", "attn")
    ):
        qkv, proj, up, down = held[layer]
        gains = gains_all[layer]
        h, saved, attended, middle, before = stored[layer]
        sums, sum_ins = [], []
        if paired and shared is not None:
            sums.append(Sum("gather", shared[1]))
            sum_ins.append(shared[0])
        if paired and made is not None:
            sums.append(Sum("scatter", made[1]))
            sum_ins += made[0]
        plan = PLANS[order - 1] if sums else {}
        if kind == "ffn":
            results = ffn_backward(
                d_hidden, before, middle, gains, (up, down), paired, sums, plan, sum_ins, order
            )
            d_middle, gain_two = results[:2]
        else:
            results = attn_backward(
                d_middle, h, saved, attended, (seg[None, :], code[:, None]), gains, heads, mean_mat,
                (qkv, proj), paired, sums, plan, sum_ins, order,
            )
            d_hidden, gain_rest = results[:2]
            gain_rest = gain_rest.reshape(3, 8, D).sum(1)
            small[layer] = jnp.stack([gain_rest[0], gain_two.sum(0), gain_rest[1], gain_rest[2]])
        results = results[2:]
        leaves[order] = results[0]
        if paired:
            made, results = (results[:2], ORDERS[order]), results[2:]
            if shared is not None:
                totals.append(results[0])
                results = results[1:]
            shared = (results[0], sums[-1].orders) if results else None
    small = jnp.concatenate(small)
    input_grad = d_hidden.reshape(tokens.shape)

    updated = []
    wide = masters[2].shape[2] // D
    if paired:
        sums = [Sum("gather", shared[1]), Sum("both", made[1])]
        small, *rest = last_sums(sums, LAST_STEPS, small, [shared[0], *made[0]], 2 * layers)
        totals += rest
        totals = list(reversed(totals))
        for kind, (which, base) in enumerate(((0, 0), (0, 3), (1, 0), (1, wide))):
            updated.append(
                adam_step(masters[kind], firsts[kind], seconds[kind], totals[which::2], base)
            )
    else:
        small = lax.psum(small, ("dp", "fsdp"))
        leaves = list(reversed(leaves))
        attn, ffn = jnp.stack(leaves[0::2]), jnp.stack(leaves[1::2])
        across = lambda x: x.transpose(0, 2, 1, 3).reshape(layers, D, -1)
        full = (
            across(attn[:, :3]),
            attn[:, 3],
            across(ffn[:, :wide]),
            ffn[:, wide:].reshape(layers, wide, 2, D // 2, D).transpose(0, 2, 1, 3, 4)
            .reshape(layers, wide * D, D),
        )
        for kind in range(4):
            grad = lax.psum_scatter(full[kind], "fsdp", scatter_dimension=1, tiled=True)
            grad = lax.psum(grad, "dp").astype(F32)
            updated.append(adam(masters[kind], firsts[kind], seconds[kind], grad, D ** (-0.5), 0.1))
    small = small.reshape(layers, 4, D).transpose(0, 2, 1)
    share = masters[4].shape[1]
    small = lax.dynamic_slice_in_dim(small, me * share, share, 1)
    updated.append(adam(masters[4], firsts[4], seconds[4], small, 0.5, 0.0))
    return (output, input_grad, *[x for group in updated for x in group])


ORDERS = (
    (ZXY, XYZ, ZXY, XYZ, YZX, YXZ),
    (XYZ, ZYX, YXZ),
    (ZXY, ZYX, XYZ, YZX, ZYX, YXZ),
    (YXZ, XZY, ZXY),
)
PLANS = (
    {
        2: ((0, 0), (1, 0), (2, 0), (3, 0), (4, 0),),
        3: ((5, 0),),
        4: ((4, 1), (1, 1), (0, 1), (3, 1),),
        5: ((2, 1), (0, 2), (1, 2), (4, 2), (5, 1), (3, 2),),
        6: ((2, 2),),
        7: ((0, 3), (1, 3),),
        8: ((4, 3), (3, 3), (5, 2), (2, 3),),
        9: ((5, 3),),
    },
    {
        2: ((0, 0),),
        3: ((6, 0), (1, 0), (2, 0), (3, 0), (4, 0), (5, 0), (8, 0), (0, 1),),
        5: ((2, 1), (4, 1), (6, 1), (1, 1),),
        6: ((3, 1), (5, 1), (7, 0),),
        7: ((8, 1), (6, 2), (0, 2), (1, 2), (4, 2),),
        9: ((2, 2), (6, 3),),
        10: ((8, 2), (5, 2),),
        11: ((3, 2), (7, 1),),
        13: ((8, 3),),
        14: ((1, 3),),
        15: ((7, 2), (0, 3), (4, 3), (7, 3), (2, 3), (5, 3), (3, 3),),
    },
    {
        0: ((0, 0), (1, 0), (2, 0), (5, 0),),
        1: ((1, 1),),
        3: ((6, 0), (0, 1), (2, 1),),
        4: ((8, 0), (5, 1), (1, 2),),
        5: ((2, 2), (0, 2), (3, 0), (4, 0), (8, 1),),
        6: ((7, 0),),
        7: ((5, 2), (6, 1), (8, 2),),
        8: ((3, 1), (4, 1), (5, 3), (8, 3), (6, 2), (0, 3), (1, 3), (7, 1), (2, 3),),
        9: ((3, 2), (4, 2), (6, 3), (7, 2),),
        12: ((3, 3), (4, 3), (7, 3),),
    },
)
LAST_STEPS = ((0, 0), (1, 0), (6, 0), (2, 0), (7, 0), (3, 0), (4, 0), (5, 0), (0, 1), (1, 1), (2, 1), (5, 1), (3, 1), (4, 1), (7, 1), (6, 1), (1, 2), (0, 2), (8, 0), (5, 2), (2, 2), (7, 2), (8, 1), (6, 2), (4, 2), (3, 2), (7, 3), (8, 2), (6, 3), (2, 3), (7, 4), (8, 3), (6, 4), (5, 3), (7, 5), (3, 3), (8, 4), (8, 5), (6, 5), (1, 3), (0, 3), (8, 6), (7, 6), (6, 6), (4, 3), (8, 7), (7, 7), (6, 7))


def solution(mesh):
    rows = P(("dp", "fsdp"), None, None)
    weight = P(None, "fsdp", None)
    flat = P(("dp", "fsdp"), None)
    return jax.shard_map(
        functools.partial(per_device, mesh.shape["dp"], mesh.shape["fsdp"]),
        mesh=mesh,
        in_specs=(rows, rows, flat, flat) + (weight,) * 15,
        out_specs=(rows, rows) + (weight,) * 15,
        check_vma=False,
    )
```

```python
import functools
import math

import jax
import jax.numpy as jnp
import numpy as np
from jax import lax
from jax.experimental import pallas as pl
from jax.experimental.pallas import tpu as pltpu
from jax.sharding import PartitionSpec as P

D = 768
HEADS = 12
HEAD_DIM = 64
STEP = 5
BF = jnp.bfloat16
F32 = jnp.float32
norm_eps = 1e-06
adam_eps = 1e-08
VMEM_LIMIT = 62 * 1024 * 1024
LOG2E = 1.4426950408889634
MASKED = -1e30


def dot(a, b):
    return lax.dot_general(a, b, (((1,), (0,)), ((), ())), preferred_element_type=F32)


def dot_nt(a, b):
    return lax.dot_general(a, b, (((1,), (1,)), ((), ())), preferred_element_type=F32)


def dot_tn(a, b):
    return lax.dot_general(a, b, (((0,), (0,)), ((), ())), preferred_element_type=F32)


def head_mean(x, mean_mat, exact=False):
    width = mean_mat.shape[0]
    found = []
    for at in range(0, x.shape[1], width):
        part = x[:, at : at + width]
        high = part.astype(BF)
        mean = dot(high, mean_mat)
        if exact:
            mean = mean + dot((part - high.astype(F32)).astype(BF), mean_mat)
        found.append(mean)
    return jnp.concatenate(found, axis=1)


def normalise(values):
    average = jnp.mean(values, axis=-1, keepdims=True)
    centred = values - average
    spread = jnp.mean(centred * centred, axis=-1, keepdims=True)
    scale = lax.rsqrt(spread + norm_eps)
    return centred * scale, scale


def norm_back(grad, gain, unit, scale):
    scaled = grad * gain
    first = jnp.mean(scaled, axis=-1, keepdims=True)
    second = jnp.mean(scaled * unit, axis=-1, keepdims=True)
    return scale * (scaled - first - unit * second)


def column_sum(x):
    return jnp.sum(x.reshape(x.shape[0] // 8, 8, x.shape[1]), axis=0)


def start_all(copies):
    for copy in copies:
        copy.start()


def wait_all(copies):
    for copy in copies:
        copy.wait()


def whole(shape):
    zeros = (0,) * len(shape)
    return pl.BlockSpec(shape, lambda *_: zeros, pipeline_mode=pl.Buffered(1))


ANY = pl.BlockSpec(memory_space=pl.ANY)
SMEM = pl.BlockSpec(memory_space=pltpu.SMEM)


def params(steps=1):
    return pltpu.CompilerParams(
        dimension_semantics=("arbitrary",) * steps, vmem_limit_bytes=VMEM_LIMIT
    )


MESH = pl.DeviceIdType.MESH

BITS = 4
XYZ, YXZ, ZXY, YZX, XZY, ZYX = (
    (0, 1, 2, 3), (1, 0, 2, 3), (2, 0, 1, 3), (1, 2, 0, 3), (0, 2, 1, 3), (2, 1, 0, 3),
)
GROUP, SPLIT = 4, 3
UNIT = GROUP * D // 2
WIDTH = D // SPLIT
FINAL = UNIT >> BITS


def flip(index, bit):
    size = 1 << bit
    return index + size * (1 - 2 * ((index // size) % 2))


def meet(partners):
    me, core = lax.axis_index("dp"), lax.axis_index("fsdp")
    barrier = pltpu.get_barrier_semaphore()
    pl.semaphore_signal(barrier, inc=1, device_id=(me, 1 - core), device_id_type=MESH)
    for bit in range(partners):
        pl.semaphore_signal(barrier, inc=1, device_id=(flip(me, bit), core), device_id_type=MESH)
    pl.semaphore_wait(barrier, 1 + partners)


def add_rows(target, source, at, other, other_at, rows):
    chunk = FINAL

    def body(i, carry):
        here = pl.ds(pl.multiple_of(at + i * chunk, chunk), chunk)
        there = pl.ds(pl.multiple_of(other_at + i * chunk, chunk), chunk)
        target[here, :] = (source[here, :].astype(F32) + other[there, :].astype(F32)).astype(BF)
        return carry

    lax.fori_loop(0, rows // chunk, body, 0)


class Sum:
    def __init__(self, kind, orders):
        self.kind, self.orders, self.count = kind, orders, len(orders)
        self.scatters = kind != "gather"
        self.gathers = kind != "scatter"

    def blocks(self):
        return GROUP * self.count // SPLIT

    def out_shapes(self):
        if self.gathers:
            return [jax.ShapeDtypeStruct((self.blocks(), D // 2, D), BF)]
        return [jax.ShapeDtypeStruct((self.count, FINAL, WIDTH), BF)]

    def inputs(self):
        return 2 if self.scatters else 1

    def scratch(self):
        n = self.count
        found = []
        if self.scatters:
            found += [
                pltpu.VMEM((n, UNIT, WIDTH), BF),
                pltpu.VMEM((n, UNIT - FINAL, WIDTH), BF),
                pltpu.VMEM((2, UNIT, WIDTH), BF),
                pltpu.SemaphoreType.DMA((n, 2 * GROUP)),
                pltpu.SemaphoreType.DMA((n, BITS)),
                pltpu.SemaphoreType.DMA((n, BITS)),
            ]
        if self.gathers:
            found += [
                pltpu.VMEM((n, UNIT, WIDTH), BF),
                pltpu.SemaphoreType.DMA((n, GROUP)),
                pltpu.SemaphoreType.DMA((n, BITS)),
                pltpu.SemaphoreType.DMA((n, BITS)),
            ]
        else:
            found += [pltpu.SemaphoreType.DMA((n,))]
        return found

    def bind(self, ins, outs, scratch):
        self.me, self.core = lax.axis_index("dp"), lax.axis_index("fsdp")
        self.ins, self.out = ins, outs[0]
        scratch = list(scratch)
        if self.scatters:
            self.held, self.arrived, self.stage, self.load, self.send, self.recv = scratch[:6]
            scratch = scratch[6:]
        if self.gathers:
            self.final, self.local, self.gsend, self.grecv = scratch
        else:
            self.local = scratch[0]

    def spans(self, unit):
        found, base, size = [], 0, UNIT
        for bit in self.orders[unit]:
            size = size // 2
            side = (self.me // (1 << bit)) % 2
            found.append((base + side * size, base + (1 - side) * size, size))
            base = base + side * size
        return found

    def window(self, ref, unit, side):
        block = GROUP * (unit // SPLIT) + side
        return ref.at[block, :, pl.ds((unit % SPLIT) * WIDTH, WIDTH)]

    def loads(self, unit):
        return [
            pltpu.make_async_copy(
                self.window(source, unit, side),
                target.at[pl.ds(side * (D // 2), D // 2)],
                self.load.at[unit, GROUP * which + side],
            )
            for which, (source, target) in enumerate(
                ((self.ins[0], self.held.at[unit]), (self.ins[1], self.stage.at[unit % 2]))
            )
            for side in range(GROUP)
        ]

    def scatter_copy(self, unit, step):
        _, give, size = self.spans(unit)[step]
        return pltpu.make_async_remote_copy(
            src_ref=self.held.at[unit, pl.ds(pl.multiple_of(give, size), size)],
            dst_ref=self.arrived.at[unit, pl.ds(UNIT - 2 * size, size)],
            send_sem=self.send.at[unit, step], recv_sem=self.recv.at[unit, step],
            device_id=(flip(self.me, self.orders[unit][step]), self.core), device_id_type=MESH,
        )

    def gather_copy(self, unit, step):
        keep, _, size = self.spans(unit)[step]
        place = pl.ds(pl.multiple_of(keep, size), size)
        return pltpu.make_async_remote_copy(
            src_ref=self.final.at[unit, place], dst_ref=self.final.at[unit, place],
            send_sem=self.gsend.at[unit, step], recv_sem=self.grecv.at[unit, step],
            device_id=(flip(self.me, self.orders[unit][step]), self.core), device_id_type=MESH,
        )

    def share_copy(self, unit):
        keep, _, size = self.spans(unit)[BITS - 1]
        place = pl.ds(pl.multiple_of(keep, size), size)
        if self.scatters:
            return pltpu.make_async_copy(self.held.at[unit, place], self.out.at[unit], self.local.at[unit])
        return pltpu.make_async_copy(self.ins[0].at[unit], self.final.at[unit, place], self.local.at[unit, 0])

    def outs(self, unit):
        return [
            pltpu.make_async_copy(
                self.final.at[unit, pl.ds(side * (D // 2), D // 2)],
                self.window(self.out, unit, side),
                self.local.at[unit, side],
            )
            for side in range(GROUP)
        ]

    def prefetch(self):
        if self.scatters:
            for unit in range(min(2, self.count)):
                start_all(self.loads(unit))
        else:
            for unit in range(self.count):
                self.share_copy(unit).start()

    def begin(self):
        if not self.scatters:
            for unit in range(self.count):
                self.share_copy(unit).wait()
                self.gather_copy(unit, BITS - 1).start()
            return
        for unit in range(self.count):
            wait_all(self.loads(unit))
            add_rows(self.held.at[unit], self.held.at[unit], 0, self.stage.at[unit % 2], 0, UNIT)
            self.scatter_copy(unit, 0).start()
            if unit + 2 < self.count:
                start_all(self.loads(unit + 2))

    def stages(self):
        return BITS * (self.scatters + self.gathers)

    def advance(self, unit, stage):
        if self.scatters and stage < BITS:
            self.scatter_copy(unit, stage).wait()
            keep, _, size = self.spans(unit)[stage]
            landing = UNIT - 2 * size
            target = self.final if self.gathers and stage == BITS - 1 else self.held
            add_rows(target.at[unit], self.held.at[unit], keep, self.arrived.at[unit], landing, size)
            if stage < BITS - 1:
                self.scatter_copy(unit, stage + 1).start()
            elif self.gathers:
                self.gather_copy(unit, BITS - 1).start()
            else:
                self.share_copy(unit).start()
            return
        step = BITS - 1 - (stage - BITS * self.scatters)
        self.gather_copy(unit, step).wait()
        if step:
            self.gather_copy(unit, step - 1).start()
        else:
            start_all(self.outs(unit))

    def finish(self):
        for unit in range(self.count):
            if self.gathers:
                wait_all(self.outs(unit))
            else:
                self.share_copy(unit).wait()


def bind_sums(sums, ins, outs, scratch):
    ins, outs, scratch = list(ins), list(outs), list(scratch)
    for one in sums:
        a, b, c = one.inputs(), 1, len(one.scratch())
        one.bind(ins[:a], outs[:b], scratch[:c])
        ins, outs, scratch = ins[a:], outs[b:], scratch[c:]


def run_steps(sums, steps):
    owners = [(one, unit) for one in sums for unit in range(one.count)]
    for unit, stage in steps:
        one, own = owners[unit]
        one.advance(own, stage)


class Pull:
    def __init__(self, shapes):
        self.chunks = [
            (which, down, across)
            for which, (downs, acrosses) in enumerate(shapes)
            for down in range(downs)
            for across in range(acrosses)
        ]
        self.shapes = shapes

    def scratch(self):
        n = len(self.chunks)
        return [
            pltpu.VMEM((3, D // 2, D), F32),
            pltpu.SemaphoreType.DMA((n,)),
            pltpu.SemaphoreType.DMA((n,)),
            pltpu.SemaphoreType.DMA((n,)),
        ]

    def bind(self, layer, sources, targets, scratch):
        self.layer, self.sources, self.targets = layer, sources, targets
        self.stage, self.loads, self.sends, self.recvs = scratch
        self.me, self.core = lax.axis_index("dp"), lax.axis_index("fsdp")

    def load(self, i):
        which, down, across = self.chunks[i]
        layer = self.layer[which]
        return pltpu.make_async_copy(
            self.sources[which].at[layer, pl.ds(down * (D // 2), D // 2), pl.ds(across * D, D)],
            self.stage.at[i % 3],
            self.loads.at[i],
        )

    def place(self, i):
        which, down, across = self.chunks[i]
        half = D // 2
        first = pl.multiple_of(self.core * (self.shapes[which][0] * half) + down * half, half)
        return pl.ds(first, half), pl.ds(across * D, D)

    def push(self, i):
        place = self.targets[self.chunks[i][0]].at[self.place(i)]
        return pltpu.make_async_remote_copy(
            src_ref=place, dst_ref=place, send_sem=self.sends.at[i], recv_sem=self.recvs.at[i],
            device_id=(self.me, 1 - self.core), device_id_type=MESH,
        )

    def begin(self):
        for i in range(min(3, len(self.chunks))):
            self.load(i).start()

    def turn(self, i):
        self.load(i).wait()
        self.targets[self.chunks[i][0]][self.place(i)] = self.stage[i % 3].astype(BF)
        self.push(i).start()
        if i + 3 < len(self.chunks):
            self.load(i + 3).start()

    def of(self, which):
        return [i for i, chunk in enumerate(self.chunks) if chunk[0] == which]

    def arrive(self, which):
        for i in self.of(which):
            self.push(i).wait()


def qkv_kernel(pull, h_ref, gain_ref, mean_ref, source, *refs):
    normed_ref, q_ref, k_ref, v_ref, scale_q_ref, scale_k_ref, full_ref = refs[:7]
    weight, sem = refs[7:9]
    step = pl.program_id(0)
    keep = pltpu.make_async_copy(weight, full_ref, sem)
    load = pltpu.make_async_copy(source, weight, sem)
    if pull:
        pull.bind([0], [source], [weight], refs[9:])

    @pl.when(step == 0)
    def _():
        if pull:
            pull.begin()
            meet(0)
            for i in range(len(pull.chunks)):
                pull.turn(i)
        else:
            load.start()

    unit, _ = normalise(h_ref[...].astype(F32))
    normed = (unit * gain_ref[0:1, :]).astype(BF)
    normed_ref[...] = normed

    @pl.when(step == 0)
    def _():
        if pull:
            pull.arrive(0)
            keep.start()
        else:
            load.wait()

    v_ref[...] = dot(normed, weight[:, 2 * D :]).astype(BF)
    for part, out_ref, scale_ref in ((0, q_ref, scale_q_ref), (1, k_ref, scale_k_ref)):
        raw = dot(normed, weight[:, part * D : (part + 1) * D])
        centred = raw - head_mean(raw, mean_ref[...], exact=True)
        scale = lax.rsqrt(head_mean(centred * centred, mean_ref[...]) + norm_eps)
        out_ref[...] = (centred * scale * gain_ref[2 + part : 3 + part, :]).astype(BF)
        scale_ref[...] = scale.astype(BF)

    if pull:

        @pl.when(step == pl.num_programs(0) - 1)
        def _():
            keep.wait()


def qkv_forward(h, gains, mean_mat, source, fresh, collective_id):
    rows = h.shape[0]
    block = min(512, rows)
    row = lambda width: pl.BlockSpec((block, width), lambda i: (i, 0))
    pull = Pull([(1, 3)]) if fresh else None
    full = [jax.ShapeDtypeStruct((D, 3 * D), BF)]
    results = pl.pallas_call(
        functools.partial(qkv_kernel, pull) if fresh else functools.partial(qkv_plain_kernel),
        name="qkv_forward",
        grid=(rows // block,),
        in_specs=[row(D), whole(gains.shape), whole(mean_mat.shape), ANY],
        out_specs=[row(D)] * 6 + [ANY] * fresh,
        out_shape=[jax.ShapeDtypeStruct((rows, D), BF)] * 6 + full * fresh,
        scratch_shapes=[pltpu.VMEM((D, 3 * D), BF), pltpu.SemaphoreType.DMA]
        + (pull.scratch() if fresh else []),
        compiler_params=remote_params(fresh, collective_id),
    )(h, gains, mean_mat, source)
    return results if fresh else [*results, source]


def qkv_plain_kernel(h_ref, gain_ref, mean_ref, source, *refs):
    qkv_kernel(None, h_ref, gain_ref, mean_ref, source, *refs[:6], source, *refs[6:])


def window_at(block, count):
    return block - 1 + (count - 1 - block) // (count - 1) - block // (count - 1)


def pair_stack(x, low_lanes):
    zero = jnp.zeros_like(x)
    return jnp.concatenate([jnp.where(low_lanes, x, zero), jnp.where(low_lanes, zero, x)], axis=0)


def mix_kernel(
    tile, reach, pull, layer, follow, n_source,
    h_ref, q_ref, k_ref, v_ref, seg_ref, code_ref, gain_ref, *refs,
):
    sources, outs, follows, scratch, pull_scratch = carve(
        refs, n_source, 4 + (3 if pull else 0), int(follow), 4 + int(follow), len(refs)
    )
    attended_ref, middle_ref, before_ref, out_ref = outs[:4]
    proj, up, down, sems = scratch[:4]
    weights = (proj, up, down)
    if pull:
        targets = list(weights) + ([scratch[4]] if follow else [])
        pull.bind([layer] * 3 + [layer + 1] * follow, sources, targets, pull_scratch)
        keeps = [
            pltpu.make_async_copy(weight, full, sems.at[i])
            for i, (weight, full) in enumerate(zip(targets, outs[4:] + follows))
        ]
    else:
        loads = [
            pltpu.make_async_copy(source, weight, sems.at[i])
            for i, (source, weight) in enumerate(zip(sources, weights))
        ]
    step = pl.program_id(0)
    count = k_ref.shape[0] // tile
    keys = reach * tile
    factor = LOG2E * HEAD_DIM ** (-0.5)
    low_lanes = lax.broadcasted_iota(jnp.int32, (tile, 128), 1) < HEAD_DIM

    @pl.when(step == 0)
    def _():
        if pull:
            pull.begin()
            meet(0)
        else:
            start_all(loads)

    @pl.when(step < count)
    def _():
        first = pl.multiple_of(window_at(step, count) * tile if count > reach else 0, tile)
        window = pl.ds(first, keys)
        here = pl.ds(pl.multiple_of(step * tile, tile), tile)
        seg = seg_ref[here, :]
        code = code_ref[:, window]
        query_at = step * tile + lax.broadcasted_iota(jnp.int32, (tile, keys), 0)
        key_at = first + lax.broadcasted_iota(jnp.int32, (tile, keys), 1)
        bias = jnp.where((seg == code) | (query_at == key_at), 0.0, MASKED)
        bias = jnp.concatenate([bias, bias], axis=0)

        def front(pair):
            lanes = slice(pair * 128, (pair + 1) * 128)
            return dot_nt(pair_stack(q_ref[here, lanes], low_lanes), k_ref[window, lanes])

        following = front(0)
        for pair in range(HEADS // 2):
            lanes = slice(pair * 128, (pair + 1) * 128)
            scores = following
            if pair + 1 < HEADS // 2:
                following = front(pair + 1)
            expo = jnp.exp2(scores * factor + bias)
            total = jnp.sum(expo, axis=-1, keepdims=True)
            mixed = dot(expo.astype(BF), v_ref[window, lanes]) * (1.0 / total)
            attended_ref[here, lanes] = jnp.where(low_lanes, mixed[:tile], mixed[tile:]).astype(BF)

    if pull:
        per_step = -(-len(pull.chunks) // count)
        for turn in range(count):
            mine = range(turn * per_step, min((turn + 1) * per_step, len(pull.chunks)))
            if mine:

                @pl.when(step == turn)
                def _():
                    for i in mine:
                        pull.turn(i)

    @pl.when(step == count)
    def _():
        if pull:
            for which in range(3):
                pull.arrive(which)
                keeps[which].start()
        else:
            wait_all(loads)

    @pl.when(step >= count)
    def _():
        rows = h_ref.shape[0]
        here = pl.ds(pl.multiple_of((step - count) * rows, rows), rows)
        middle = h_ref[...].astype(F32) + dot(attended_ref[here, :], proj[...])
        middle_ref[...] = middle
        unit, _ = normalise(middle)
        normed = (unit * gain_ref[1:2, :]).astype(BF)
        result = middle
        for part in range(up.shape[1] // D):
            lanes = slice(part * D, (part + 1) * D)
            before = dot(normed, up[:, lanes])
            before_ref[:, lanes] = before.astype(BF)
            active = jax.nn.gelu(before, approximate=True).astype(BF)
            result = result + dot(active, down[lanes, :])
        out_ref[...] = result.astype(out_ref.dtype)

    if pull:

        @pl.when(step == pl.num_programs(0) - 1)
        def _():
            if follow:
                pull.arrive(3)
                keeps[3].start()
            wait_all(keeps)


def mix_forward(h, q, k, v, seg, code, gains, sources, out_type, layer, paired, collective_id):
    rows = h.shape[0]
    block = min(512, rows)
    tile = min(128, rows)
    reach = min(3, rows // tile)
    count = rows // tile
    width = sources[1].shape[-1]
    follow = len(sources) > 3
    shapes = [(1, 1), (1, width // D), (width // D, 1)] + [(1, 3)] * follow
    pull = Pull(shapes) if paired else None
    row = lambda w: pl.BlockSpec((block, w), lambda i: (jnp.maximum(i - count, 0), 0))
    outs = [(D, F32), (width, BF), (D, out_type)]
    fulls = [(D, D), (D, width), (width, D)]
    follows = [(D, 3 * D)] * follow
    results = pl.pallas_call(
        functools.partial(mix_kernel, tile, reach, pull, layer, follow, len(sources)),
        name="mix_forward",
        grid=(count + rows // block,),
        in_specs=[row(D)] + [whole(x.shape) for x in (q, k, v, seg, code, gains)] + [ANY] * len(sources),
        out_specs=[pl.BlockSpec((rows, D), lambda i: (0, 0), pipeline_mode=pl.Buffered(1))]
        + [row(w) for w, _ in outs]
        + [ANY] * (len(fulls + follows) if paired else 0),
        out_shape=[jax.ShapeDtypeStruct((rows, D), BF)]
        + [jax.ShapeDtypeStruct((rows, w), t) for w, t in outs]
        + [jax.ShapeDtypeStruct(x, BF) for x in (fulls + follows if paired else [])],
        scratch_shapes=[pltpu.VMEM(x, BF) for x in fulls]
        + [pltpu.SemaphoreType.DMA((4,))]
        + [pltpu.VMEM(x, BF) for x in follows]
        + (pull.scratch() if paired else []),
        compiler_params=remote_params(paired, collective_id),
    )(h, q, k, v, seg, code, gains, *sources)
    return results if paired else [*results, *sources]


class Blocks:
    def __init__(self, count, paired):
        self.count, self.paired = count, paired

    def out_shapes(self):
        rows = D // 2 if self.paired else D
        return [jax.ShapeDtypeStruct((self.count, rows, D), BF)] * (1 + self.paired)

    def scratch(self):
        return [pltpu.SemaphoreType.DMA((self.count,))] * (1 + 2 * self.paired)

    def bind(self, outs, sems):
        self.outs, self.sems = outs, sems

    def copies(self, block, lanes, ref, first_row):
        if not self.paired:
            return [
                pltpu.make_async_copy(
                    ref.at[pl.ds(first_row, D), lanes], self.outs[0].at[block], self.sems[0].at[block]
                )
            ]
        core = lax.axis_index("fsdp")
        half = D // 2
        mine = pl.multiple_of(first_row + core * half, half)
        theirs = pl.multiple_of(first_row + (1 - core) * half, half)
        return [
            pltpu.make_async_copy(
                ref.at[pl.ds(mine, half), lanes], self.outs[0].at[block], self.sems[0].at[block]
            ),
            pltpu.make_async_remote_copy(
                src_ref=ref.at[pl.ds(theirs, half), lanes], dst_ref=self.outs[1].at[block],
                send_sem=self.sems[1].at[block], recv_sem=self.sems[2].at[block],
                device_id=(lax.axis_index("dp"), 1 - core), device_id_type=MESH,
            ),
        ]


def carve(refs, *sizes):
    found, at = [], 0
    for size in sizes:
        found.append(refs[at : at + size])
        at += size
    return found


def sums_in(sums):
    return sum(one.inputs() for one in sums)


def sums_scratch(sums):
    return [shape for one in sums for shape in one.scratch()]


def sums_outs(sums):
    return [shape for one in sums for shape in one.out_shapes()]


def remote_params(paired, collective_id):
    if not paired:
        return params()
    return pltpu.CompilerParams(
        dimension_semantics=("arbitrary",), vmem_limit_bytes=VMEM_LIMIT,
        collective_id=collective_id, has_side_effects=True,
    )


def ffn_back_kernel(blocks, store, sums, plan, dh_ref, before_ref, middle_ref, gain_ref, *refs):
    weights, ins, outs, store_outs, sum_outs, own_scratch, store_sems, sum_scratch = carve(
        refs, 2, sums_in(sums), 2, 1 + store.paired, len(sums), 7, 1 + 2 * store.paired,
        len(sums_scratch(sums)),
    )
    dmid_ref, dgain_ref = outs
    up, down, active, dbefore, dbranch, normed, sems = own_scratch
    store.bind(store_outs, store_sems)
    bind_sums(sums, ins, sum_outs, sum_scratch)
    step = pl.program_id(0)
    copies = [
        pltpu.make_async_copy(source, target, sems.at[i])
        for i, (source, target) in enumerate(zip(weights, (up, down)))
    ]
    parts = up.shape[1] // D
    rows = dh_ref.shape[0]

    @pl.when(step == 0)
    def _():
        start_all(copies)
        dgain_ref[...] = jnp.zeros_like(dgain_ref)
        for one in sums:
            one.prefetch()
        if store.paired:
            meet(BITS if sums else 0)
        for one in sums:
            one.begin()

    @pl.when(step < blocks)
    def _():
        here = pl.ds(pl.multiple_of(step * rows, rows), rows)
        dh = dh_ref[...].astype(F32)
        branch = dh.astype(BF)
        dbranch[here, :] = branch
        gain = gain_ref[1:2, :]
        unit, scale = normalise(middle_ref[...])
        normed[here, :] = (unit * gain).astype(BF)

        @pl.when(step == 0)
        def _():
            wait_all(copies)

        dnormed = jnp.zeros((rows, D), F32)
        for part in range(parts):
            lanes = slice(part * D, (part + 1) * D)
            dactive = dot_nt(branch, down[lanes, :])
            value = before_ref[:, lanes].astype(F32)
            root = math.sqrt(2.0 / math.pi)
            square = value * value
            curve = jnp.tanh(value * (root + (root * 0.044715) * square))
            half = 0.5 * (1.0 + curve)
            active[here, lanes] = (value * half).astype(BF)
            slope = half + (0.5 * value) * (1.0 - curve * curve) * (
                root + (3.0 * 0.044715 * root) * square
            )
            dpart = (dactive * slope).astype(BF)
            dbefore[here, lanes] = dpart
            dnormed = dnormed + dot_nt(dpart, up[:, lanes])
            for block in range(blocks):
                if block * parts + part in plan:

                    @pl.when(step == block)
                    def _():
                        run_steps(sums, plan[block * parts + part])

        dmid_ref[...] = dh + norm_back(dnormed, gain, unit, scale)
        dgain_ref[...] += column_sum(dnormed * unit)

    late = blocks * parts - blocks
    for tick in sorted(plan):
        if tick >= blocks * parts:

            @pl.when(step == tick - late)
            def _():
                run_steps(sums, plan[tick])

    every = slice(0, D)

    @pl.when((step >= blocks) & (step < blocks + parts))
    def _():
        part = step - blocks
        lanes = pl.ds(pl.multiple_of(part * D, D), D)
        up[:, lanes] = dot_tn(normed[...], dbefore[:, lanes]).astype(BF)
        start_all(store.copies(part, lanes, up, 0))

    @pl.when(step >= blocks + parts)
    def _():
        part = step - blocks - parts
        half = D // 2
        base = down.shape[0] // 2
        first_row = pl.multiple_of(part * D, D)
        for side in range(2):
            lanes = pl.ds(pl.multiple_of(side * base + part * half, half), half)
            here = pl.ds(pl.multiple_of(first_row + side * half, half), half)
            down[here, :] = dot_tn(active[:, lanes], dbranch[...]).astype(BF)
        start_all(store.copies(parts + part, every, down, first_row))

    @pl.when(step == blocks + 2 * parts - 1)
    def _():
        for part in range(parts):
            wait_all(store.copies(part, slice(part * D, (part + 1) * D), up, 0))
        for part in range(parts):
            wait_all(store.copies(parts + part, every, down, part * D))
        for one in sums:
            one.finish()


def ffn_backward(dh, before, middle, gains, shards, paired, sums, plan, sum_ins, collective_id):
    rows, width = before.shape
    block = min(512, rows)
    blocks = rows // block
    parts = width // D
    store = Blocks(2 * parts, paired)
    row = lambda w, **mode: pl.BlockSpec((block, w), lambda i: (jnp.minimum(i, blocks - 1), 0), **mode)
    once = {"pipeline_mode": pl.Buffered(1)}
    outs = store.out_shapes() + sums_outs(sums)
    return pl.pallas_call(
        functools.partial(ffn_back_kernel, blocks, store, sums, plan),
        name="ffn_backward",
        grid=(blocks + 2 * parts,),
        in_specs=[row(D, **once), row(width), row(D, **once), whole(gains.shape)] + [ANY] * (2 + len(sum_ins)),
        out_specs=[row(D), pl.BlockSpec((8, D), lambda i: (0, 0))] + [ANY] * len(outs),
        out_shape=[jax.ShapeDtypeStruct((rows, D), F32), jax.ShapeDtypeStruct((8, D), F32)] + outs,
        scratch_shapes=[
            pltpu.VMEM((D, width), BF),
            pltpu.VMEM((width, D), BF),
            pltpu.VMEM((rows, width), BF),
            pltpu.VMEM((rows, width), BF),
            pltpu.VMEM((rows, D), BF),
            pltpu.VMEM((rows, D), BF),
            pltpu.SemaphoreType.DMA((2,)),
        ]
        + store.scratch()
        + sums_scratch(sums),
        compiler_params=remote_params(paired, collective_id),
    )(dh, before, middle, gains, *shards, *sum_ins)


def attn_back_kernel(
    tile, reach, rows, store, sums, plan,
    seg_ref, code_ref, gain_ref, heads_ref, mean_ref, *refs,
):
    sources, refs = refs[:8], refs[8:]
    weights, ins, outs, store_outs, sum_outs, own_scratch, store_sems, sum_scratch = carve(
        refs, 3, sums_in(sums), 2, 1 + store.paired, len(sums), 18, 1 + 2 * store.paired,
        len(sums_scratch(sums)),
    )
    normed_ref, qkv_ref, proj_ref = weights
    dh_ref, dgain_ref = outs
    qkv, proj, dattended, inner, dk, dv, dmixed, sems, normed_sem = own_scratch[:9]
    held = own_scratch[9:17]
    dmid_ref, attended_ref, q_ref, k_ref, v_ref, scale_q_ref, scale_k_ref, h_ref = held
    loads = [
        pltpu.make_async_copy(source, target, own_scratch[17].at[i])
        for i, (source, target) in enumerate(zip(sources, held))
    ]
    store.bind(store_outs, store_sems)
    bind_sums(sums, ins, sum_outs, sum_scratch)
    step = pl.program_id(0)
    total_rows = k_ref.shape[0]
    count = total_rows // tile
    keys = reach * tile
    blocks = total_rows // rows
    proj_copy = pltpu.make_async_copy(proj_ref, proj, sems.at[0])
    qkv_copy = pltpu.make_async_copy(qkv_ref, qkv, sems.at[1])
    normed_copy = pltpu.make_async_copy(normed_ref, dattended, normed_sem)
    root = HEAD_DIM ** (-0.5)

    def head_norm_back(grad, gain, unit, scale):
        scaled = grad * gain
        first = head_mean(scaled, mean_ref[...])
        second = head_mean(scaled * unit, mean_ref[...])
        return scale.astype(F32) * (scaled - first - unit * second)

    @pl.when(step == 0)
    def _():
        proj_copy.start()
        start_all(loads)
        qkv_copy.start()
        dgain_ref[...] = jnp.zeros_like(dgain_ref)
        dk[...] = jnp.zeros_like(dk)
        dv[...] = jnp.zeros_like(dv)
        for one in sums:
            one.prefetch()
        if store.paired:
            meet(BITS if sums else 0)
        for one in sums:
            one.begin()
        proj_copy.wait()
        wait_all(loads[:2])
        for block in range(blocks):
            here = slice(block * rows, (block + 1) * rows)
            back = dot_nt(dmid_ref[here, :].astype(BF), proj[...]).astype(BF)
            dattended[here, :] = back
            product = back.astype(F32) * attended_ref[here, :].astype(F32)
            high = product.astype(BF)
            low = (product - high.astype(F32)).astype(BF)
            turn = (((0,), (1,)), ((), ()))
            inner[:, here] = lax.dot_general(
                heads_ref[...], high, turn, preferred_element_type=F32
            ) + lax.dot_general(heads_ref[...], low, turn, preferred_element_type=F32)

        wait_all(loads[2:6])

    for tick in sorted(plan):

        @pl.when(step == tick)
        def _():
            run_steps(sums, plan[tick])

    @pl.when(step < count)
    def _():
        first = pl.multiple_of(window_at(step, count) * tile if count > reach else 0, tile)
        window = pl.ds(first, keys)
        here = pl.ds(pl.multiple_of(step * tile, tile), tile)
        low_lanes = lax.broadcasted_iota(jnp.int32, (tile, 128), 1) < HEAD_DIM
        seg = seg_ref[:, here]
        code = code_ref[window, :]
        key_at = first + lax.broadcasted_iota(jnp.int32, (keys, tile), 0)
        query_at = step * tile + lax.broadcasted_iota(jnp.int32, (keys, tile), 1)
        bias = jnp.where((seg == code) | (query_at == key_at), 0.0, MASKED)
        bias = jnp.concatenate([bias, bias], axis=1)
        dq_parts = []

        def front(pair):
            lanes = slice(pair * 128, (pair + 1) * 128)
            queries = pair_stack(q_ref[here, lanes], low_lanes)
            grads = pair_stack(dattended[here, lanes], low_lanes)
            keys_part = k_ref[window, lanes]
            scores = dot_nt(keys_part, queries)
            return queries, grads, keys_part, scores, dot_nt(v_ref[window, lanes], grads)

        following = front(0)
        for pair in range(HEADS // 2):
            lanes = slice(pair * 128, (pair + 1) * 128)
            queries, grads, keys_part, scores, dprobs = following
            if pair + 1 < HEADS // 2:
                following = front(pair + 1)
            expo = jnp.exp2(scores * (LOG2E * root) + bias)
            probs = expo * (1.0 / jnp.sum(expo, axis=0, keepdims=True))
            less = jnp.concatenate(
                [inner[2 * pair : 2 * pair + 1, here], inner[2 * pair + 1 : 2 * pair + 2, here]],
                axis=1,
            )
            dscores = (probs * (dprobs - less)).astype(BF)
            dv[window, lanes] += dot(probs.astype(BF), grads)
            dk[window, lanes] += dot(dscores, queries)
            dq = dot_tn(dscores, keys_part)
            dq_parts.append(jnp.where(low_lanes, dq[:tile], dq[tile:]))
        dq = jnp.concatenate(dq_parts, axis=1) * root
        gain = gain_ref[2:3, :]
        unit = q_ref[here, :].astype(F32) * (1.0 / gain)
        dmixed[here, 0:D] = head_norm_back(dq, gain, unit, scale_q_ref[here, :]).astype(BF)
        dgain_ref[8:16, :] += column_sum(dq * unit)

    @pl.when(step == count)
    def _():
        normed_copy.start()
        qkv_copy.wait()
        wait_all(loads[6:])

    @pl.when((step >= count) & (step < count + blocks))
    def _():
        here = pl.ds(pl.multiple_of((step - count) * rows, rows), rows)
        grad = dk[here, :] * root
        gain = gain_ref[3:4, :]
        unit = k_ref[here, :].astype(F32) * (1.0 / gain)
        dmixed[here, D : 2 * D] = head_norm_back(grad, gain, unit, scale_k_ref[here, :]).astype(BF)
        dgain_ref[16:24, :] += column_sum(grad * unit)
        dmixed[here, 2 * D :] = dv[here, :].astype(BF)
        dnormed = dot_nt(dmixed[here, :], qkv[...])
        unit, scale = normalise(h_ref[here, :].astype(F32))
        dh_ref[...] = dmid_ref[here, :] + norm_back(dnormed, gain_ref[0:1, :], unit, scale)
        dgain_ref[0:8, :] += column_sum(dnormed * unit)

    @pl.when(step == count + blocks)
    def _():
        normed_copy.wait()

    @pl.when((step >= count + blocks) & (step < count + blocks + 3))
    def _():
        part = step - count - blocks
        lanes = pl.ds(pl.multiple_of(part * D, D), D)
        qkv[:, lanes] = dot_tn(dattended[...], dmixed[:, lanes]).astype(BF)
        start_all(store.copies(part, lanes, qkv, 0))

    every = slice(0, D)

    @pl.when(step == count + blocks + 3)
    def _():
        proj[...] = dot_tn(attended_ref[...], dmid_ref[...].astype(BF)).astype(BF)
        start_all(store.copies(3, every, proj, 0))
        for part in range(3):
            wait_all(store.copies(part, slice(part * D, (part + 1) * D), qkv, 0))
        wait_all(store.copies(3, every, proj, 0))
        for one in sums:
            one.finish()


def attn_backward(
    dmid, h, saved, attended, segs, gains, heads, mean_mat, shards, paired, sums, plan, sum_ins, collective_id
):
    total = h.shape[0]
    rows = min(512, total)
    tile = min(128, total)
    reach = min(3, total // tile)
    count, blocks = total // tile, total // rows
    normed, q, k, v, scale_q, scale_k = saved
    ins = [*segs, gains, heads, mean_mat]
    large = [dmid, attended, q, k, v, scale_q, scale_k, h]
    store = Blocks(4, paired)
    outs = store.out_shapes() + sums_outs(sums)
    return pl.pallas_call(
        functools.partial(attn_back_kernel, tile, reach, rows, store, sums, plan),
        name="attn_backward",
        grid=(count + blocks + 4,),
        in_specs=[whole(x.shape) for x in ins] + [ANY] * (len(large) + 3 + len(sum_ins)),
        out_specs=[
            pl.BlockSpec((rows, D), lambda i: (jnp.clip(i - count, 0, blocks - 1), 0)),
            pl.BlockSpec((24, D), lambda i: (0, 0)),
        ]
        + [ANY] * len(outs),
        out_shape=[jax.ShapeDtypeStruct((total, D), F32), jax.ShapeDtypeStruct((24, D), F32)] + outs,
        scratch_shapes=[
            pltpu.VMEM((D, 3 * D), BF),
            pltpu.VMEM((D, D), BF),
            pltpu.VMEM((total, D), BF),
            pltpu.VMEM((128, total), F32),
            pltpu.VMEM((total, D), F32),
            pltpu.VMEM((total, D), F32),
            pltpu.VMEM((total, 3 * D), BF),
            pltpu.SemaphoreType.DMA((2,)),
            pltpu.SemaphoreType.DMA,
        ]
        + [pltpu.VMEM(x.shape, x.dtype) for x in large]
        + [pltpu.SemaphoreType.DMA((len(large),))]
        + store.scratch()
        + sums_scratch(sums),
        compiler_params=remote_params(paired, collective_id),
    )(*ins, *large, normed, *shards, *sum_ins)


def last_sums_kernel(sums, steps, counts, *refs):
    n_in, n_out = counts
    small, ins = refs[0], refs[1 : 1 + n_in]
    small_total, outs = refs[1 + n_in], refs[2 + n_in : 2 + n_in + n_out]
    small_held, small_arrived, small_send, small_recv = refs[2 + n_in + n_out : 6 + n_in + n_out]
    bind_sums(sums, ins, outs, refs[6 + n_in + n_out :])
    me, core = lax.axis_index("dp"), lax.axis_index("fsdp")
    for one in sums:
        one.prefetch()
    meet(BITS)

    def small_copy(step):
        to = (me, 1 - core) if step == 0 else (flip(me, step - 1), core)
        return pltpu.make_async_remote_copy(
            src_ref=small_held.at[step], dst_ref=small_arrived.at[step],
            send_sem=small_send.at[step], recv_sem=small_recv.at[step],
            device_id=to, device_id_type=MESH,
        )

    small_held[0] = small[...]
    small_copy(0).start()
    for one in sums:
        one.begin()
    each = -(-len(steps) // (BITS + 1))
    for stage in range(BITS + 1):
        run_steps(sums, steps[stage * each : (stage + 1) * each])
        small_copy(stage).wait()
        value = small_held[stage] + small_arrived[stage]
        if stage < BITS:
            small_held[stage + 1] = value
            small_copy(stage + 1).start()
        else:
            small_total[...] = value
    for one in sums:
        one.finish()


def last_sums(sums, steps, small, ins, collective_id):
    vmem = pl.BlockSpec(memory_space=pltpu.VMEM)
    outs = [shape for one in sums for shape in one.out_shapes()]
    return pl.pallas_call(
        functools.partial(last_sums_kernel, sums, steps, (len(ins), len(outs))),
        name="last_sums",
        in_specs=[vmem] + [ANY] * len(ins),
        out_specs=[vmem] + [ANY] * len(outs),
        out_shape=[jax.ShapeDtypeStruct(small.shape, F32)] + outs,
        scratch_shapes=[
            pltpu.VMEM((BITS + 1, *small.shape), F32),
            pltpu.VMEM((BITS + 1, *small.shape), F32),
            pltpu.SemaphoreType.DMA((BITS + 1,)),
            pltpu.SemaphoreType.DMA((BITS + 1,)),
        ]
        + [shape for one in sums for shape in one.scratch()],
        compiler_params=pltpu.CompilerParams(
            collective_id=collective_id, has_side_effects=True, vmem_limit_bytes=VMEM_LIMIT
        ),
    )(small, *ins)


CORRECTION = 1.0 - 0.5**STEP


def adam(weight, first, second, grad, rate, decay):
    first = 0.5 * first + 0.5 * grad
    second = 0.5 * second + 0.5 * grad * grad
    step = first / CORRECTION / (jnp.sqrt(second / CORRECTION) + adam_eps)
    return weight - rate * (step + decay * weight), first, second


def adam_kernel(weight_ref, first_ref, second_ref, *refs):
    grad_refs, outs = refs[:-3], refs[-3:]
    for layer, grad_ref in enumerate(grad_refs):

        @pl.when(pl.program_id(0) == layer)
        def _():
            results = adam(
                weight_ref[0], first_ref[0], second_ref[0], grad_ref[0].astype(F32), D ** (-0.5), 0.1
            )
            for out, result in zip(outs, results):
                out[0] = result


def adam_step(weight, first, second, totals, base):
    layers, rows, width = weight.shape
    half = D // 2
    down, across = rows // half, width // D
    last = down * across - 1
    part = pl.BlockSpec((1, half, D), lambda l, i, j: (l, i, j))

    def grad_spec(layer):
        def at(l, i, j):
            inside = jnp.where(l < layer, 0, last)
            return (base + jnp.where(l == layer, i * across + j, inside), 0, 0)

        return pl.BlockSpec((1, half, D), at)

    return pl.pallas_call(
        adam_kernel,
        name="adam_step",
        grid=(layers, down, across),
        in_specs=[part] * 3 + [grad_spec(layer) for layer in range(layers)],
        out_specs=[part] * 3,
        out_shape=[jax.ShapeDtypeStruct(weight.shape, F32)] * 3,
        compiler_params=params(3),
    )(weight, first, second, *totals)


def per_device(dp, fsdp, *args):
    tokens, cotangent, segments, keep_mask = args[:4]
    masters, firsts, seconds = args[4::3], args[5::3], args[6::3]
    packs, length, width = tokens.shape
    layers = masters[0].shape[0]
    paired = (dp, fsdp) == (1 << BITS, 2)
    me = lax.axis_index("fsdp")

    def gather(shard):
        return lax.all_gather(shard.astype(BF), "fsdp", axis=0, tiled=True)

    gains_all = lax.all_gather(masters[4].astype(BF), "fsdp", axis=1, tiled=True).astype(F32)
    gains_all = jnp.pad(gains_all.transpose(0, 2, 1), ((0, 0), (0, 4), (0, 0)))
    channel = np.arange(D) // HEAD_DIM
    heads = (channel[:, None] == np.arange(128)[None, :]).astype(BF)
    mean_mat = ((channel[:256, None] == channel[None, :256]) / HEAD_DIM).astype(BF)
    seg = segments[0]
    code = jnp.where(keep_mask[0] == 1, seg, -1)

    hidden = tokens[0]
    stored, held = [], []
    qkv = masters[0] if paired else gather(masters[0][0])
    for layer in range(layers):
        gains = gains_all[layer]
        last = layer == layers - 1
        fresh = paired and layer == 0
        *saved, qkv = qkv_forward(hidden, gains, mean_mat, qkv, fresh, 2 * layers + 1)
        q, k, v = saved[1:4]
        if paired:
            sources = [masters[kind] for kind in (1, 2, 3)] + ([] if last else [masters[0]])
        else:
            sources = [gather(masters[kind][layer]) for kind in (1, 2, 3)]
        attended, middle, before, result, proj, up, down, *following = mix_forward(
            hidden, q, k, v, seg[:, None], code[None, :], gains, sources, BF if last else F32,
            layer, paired, 2 * layers + 2 + layer,
        )
        stored.append((hidden, saved, attended, middle, before))
        held.append((qkv, proj, up, down))
        hidden = result
        if not last:
            qkv = following[0] if paired else gather(masters[0][layer + 1])
    output = hidden.reshape(tokens.shape)

    made, shared = None, None
    totals = []
    d_hidden = cotangent[0]
    small = [None] * layers
    leaves = [None] * (2 * layers)
    for order, (layer, kind) in enumerate(
        (layer, kind) for layer in reversed(range(layers)) for kind in ("ffn", "attn")
    ):
        qkv, proj, up, down = held[layer]
        gains = gains_all[layer]
        h, saved, attended, middle, before = stored[layer]
        sums, sum_ins = [], []
        if paired and shared is not None:
            sums.append(Sum("gather", shared[1]))
            sum_ins.append(shared[0])
        if paired and made is not None:
            sums.append(Sum("scatter", made[1]))
            sum_ins += made[0]
        plan = PLANS[order - 1] if sums else {}
        if kind == "ffn":
            results = ffn_backward(
                d_hidden, before, middle, gains, (up, down), paired, sums, plan, sum_ins, order
            )
            d_middle, gain_two = results[:2]
        else:
            results = attn_backward(
                d_middle, h, saved, attended, (seg[None, :], code[:, None]), gains, heads, mean_mat,
                (qkv, proj), paired, sums, plan, sum_ins, order,
            )
            d_hidden, gain_rest = results[:2]
            gain_rest = gain_rest.reshape(3, 8, D).sum(1)
            small[layer] = jnp.stack([gain_rest[0], gain_two.sum(0), gain_rest[1], gain_rest[2]])
        results = results[2:]
        leaves[order] = results[0]
        if paired:
            made, results = (results[:2], ORDERS[order]), results[2:]
            if shared is not None:
                totals.append(results[0])
                results = results[1:]
            shared = (results[0], sums[-1].orders) if results else None
    small = jnp.concatenate(small)
    input_grad = d_hidden.reshape(tokens.shape)

    updated = []
    wide = masters[2].shape[2] // D
    if paired:
        sums = [Sum("gather", shared[1]), Sum("both", made[1])]
        small, *rest = last_sums(sums, LAST_STEPS, small, [shared[0], *made[0]], 2 * layers)
        totals += rest
        totals = list(reversed(totals))
        for kind, (which, base) in enumerate(((0, 0), (0, 3), (1, 0), (1, wide))):
            updated.append(
                adam_step(masters[kind], firsts[kind], seconds[kind], totals[which::2], base)
            )
    else:
        small = lax.psum(small, ("dp", "fsdp"))
        leaves = list(reversed(leaves))
        attn, ffn = jnp.stack(leaves[0::2]), jnp.stack(leaves[1::2])
        across = lambda x: x.transpose(0, 2, 1, 3).reshape(layers, D, -1)
        full = (
            across(attn[:, :3]),
            attn[:, 3],
            across(ffn[:, :wide]),
            ffn[:, wide:].reshape(layers, wide, 2, D // 2, D).transpose(0, 2, 1, 3, 4)
            .reshape(layers, wide * D, D),
        )
        for kind in range(4):
            grad = lax.psum_scatter(full[kind], "fsdp", scatter_dimension=1, tiled=True)
            grad = lax.psum(grad, "dp").astype(F32)
            updated.append(adam(masters[kind], firsts[kind], seconds[kind], grad, D ** (-0.5), 0.1))
    small = small.reshape(layers, 4, D).transpose(0, 2, 1)
    share = masters[4].shape[1]
    small = lax.dynamic_slice_in_dim(small, me * share, share, 1)
    updated.append(adam(masters[4], firsts[4], seconds[4], small, 0.5, 0.0))
    return (output, input_grad, *[x for group in updated for x in group])


ORDERS = (
    (XYZ, XZY, YXZ, YXZ, ZXY, ZYX),
    (XZY, YZX, XYZ),
    (XYZ, ZYX, YXZ, YZX, XZY, ZXY),
    (YXZ, XYZ, ZXY),
)
PLANS = (
    {
        4: ((0, 0), (1, 0), (2, 0), (3, 0),),
        5: ((4, 0), (5, 0),),
        6: ((0, 1), (1, 1),),
        8: ((5, 1), (0, 2), (1, 2), (2, 1), (3, 1), (4, 1),),
        9: ((5, 2), (0, 3), (4, 2), (1, 3),),
        10: ((2, 2), (3, 2),),
        11: ((5, 3),),
        12: ((4, 3),),
        13: ((2, 3), (3, 3),),
    },
    {
        2: ((0, 0), (1, 0), (2, 0), (7, 0), (3, 0), (4, 0), (5, 0),),
        3: ((1, 1),),
        4: ((4, 1), (6, 0), (0, 1), (5, 1), (8, 0), (2, 1),),
        5: ((3, 1),),
        6: ((7, 1), (4, 2),),
        7: ((1, 2), (6, 1),),
        8: ((2, 2), (0, 2), (5, 2), (8, 1),),
        9: ((7, 2), (6, 2), (3, 2),),
        13: ((7, 3), (6, 3), (4, 3), (8, 2),),
        15: ((2, 3), (8, 3), (1, 3), (0, 3), (5, 3), (3, 3),),
    },
    {
        0: ((0, 0), (1, 0), (2, 0),),
        3: ((3, 0), (1, 1), (0, 1), (2, 1),),
        4: ((7, 0), (5, 0),),
        5: ((4, 0), (6, 0),),
        6: ((8, 0), (5, 1),),
        7: ((3, 1), (2, 2),),
        8: ((4, 1), (8, 1),),
        9: ((1, 2), (0, 2), (5, 2), (8, 2), (7, 1), (3, 2), (4, 2), (6, 1),),
        10: ((2, 3),),
        12: ((7, 2), (5, 3), (6, 2), (8, 3),),
        13: ((3, 3), (4, 3), (1, 3), (0, 3), (7, 3), (6, 3),),
    },
)
LAST_STEPS = ((0, 0), (1, 0), (6, 0), (2, 0), (7, 0), (3, 0), (4, 0), (5, 0), (0, 1), (1, 1), (2, 1), (3, 1), (6, 1), (4, 1), (5, 1), (2, 2), (7, 1), (8, 0), (5, 2), (6, 2), (0, 2), (1, 2), (8, 1), (3, 2), (7, 2), (6, 3), (8, 2), (4, 2), (0, 3), (2, 3), (7, 3), (6, 4), (8, 3), (3, 3), (7, 4), (4, 3), (8, 4), (6, 5), (8, 5), (7, 5), (5, 3), (1, 3), (6, 6), (7, 6), (8, 6), (6, 7), (7, 7), (8, 7))


def solution(mesh):
    rows = P(("dp", "fsdp"), None, None)
    weight = P(None, "fsdp", None)
    flat = P(("dp", "fsdp"), None)
    return jax.shard_map(
        functools.partial(per_device, mesh.shape["dp"], mesh.shape["fsdp"]),
        mesh=mesh,
        in_specs=(rows, rows, flat, flat) + (weight,) * 15,
        out_specs=(rows, rows) + (weight,) * 15,
        check_vma=False,
    )
```

```python
import functools
import math

import jax
import jax.numpy as jnp
import numpy as np
from jax import lax
from jax.experimental import pallas as pl
from jax.experimental.pallas import tpu as pltpu
from jax.sharding import PartitionSpec as P

D = 768
HEADS = 12
HEAD_DIM = 64
STEP = 5
BF = jnp.bfloat16
F32 = jnp.float32
norm_eps = 1e-06
adam_eps = 1e-08
VMEM_LIMIT = 62 * 1024 * 1024
LOG2E = 1.4426950408889634
MASKED = -1e30


def dot(a, b):
    return lax.dot_general(a, b, (((1,), (0,)), ((), ())), preferred_element_type=F32)


def dot_nt(a, b):
    return lax.dot_general(a, b, (((1,), (1,)), ((), ())), preferred_element_type=F32)


def dot_tn(a, b):
    return lax.dot_general(a, b, (((0,), (0,)), ((), ())), preferred_element_type=F32)


def head_mean(x, mean_mat, exact=False):
    width = mean_mat.shape[0]
    found = []
    for at in range(0, x.shape[1], width):
        part = x[:, at : at + width]
        high = part.astype(BF)
        mean = dot(high, mean_mat)
        if exact:
            mean = mean + dot((part - high.astype(F32)).astype(BF), mean_mat)
        found.append(mean)
    return jnp.concatenate(found, axis=1)


def normalise(values):
    average = jnp.mean(values, axis=-1, keepdims=True)
    centred = values - average
    spread = jnp.mean(centred * centred, axis=-1, keepdims=True)
    scale = lax.rsqrt(spread + norm_eps)
    return centred * scale, scale


def norm_back(grad, gain, unit, scale):
    scaled = grad * gain
    first = jnp.mean(scaled, axis=-1, keepdims=True)
    second = jnp.mean(scaled * unit, axis=-1, keepdims=True)
    return scale * (scaled - first - unit * second)


def column_sum(x):
    return jnp.sum(x.reshape(x.shape[0] // 8, 8, x.shape[1]), axis=0)


def start_all(copies):
    for copy in copies:
        copy.start()


def wait_all(copies):
    for copy in copies:
        copy.wait()


def whole(shape):
    zeros = (0,) * len(shape)
    return pl.BlockSpec(shape, lambda *_: zeros, pipeline_mode=pl.Buffered(1))


ANY = pl.BlockSpec(memory_space=pl.ANY)
SMEM = pl.BlockSpec(memory_space=pltpu.SMEM)


def params(steps=1):
    return pltpu.CompilerParams(
        dimension_semantics=("arbitrary",) * steps, vmem_limit_bytes=VMEM_LIMIT
    )


MESH = pl.DeviceIdType.MESH

BITS = 4
XYZ, YXZ, ZXY, YZX, XZY, ZYX = (
    (0, 1, 2, 3), (1, 0, 2, 3), (2, 0, 1, 3), (1, 2, 0, 3), (0, 2, 1, 3), (2, 1, 0, 3),
)
GROUP, SPLIT = 4, 3
UNIT = GROUP * D // 2
WIDTH = D // SPLIT
FINAL = UNIT >> BITS


def flip(index, bit):
    size = 1 << bit
    return index + size * (1 - 2 * ((index // size) % 2))


def meet(partners):
    me, core = lax.axis_index("dp"), lax.axis_index("fsdp")
    barrier = pltpu.get_barrier_semaphore()
    pl.semaphore_signal(barrier, inc=1, device_id=(me, 1 - core), device_id_type=MESH)
    for bit in range(partners):
        pl.semaphore_signal(barrier, inc=1, device_id=(flip(me, bit), core), device_id_type=MESH)
    pl.semaphore_wait(barrier, 1 + partners)


def add_rows(target, source, at, other, other_at, rows):
    chunk = FINAL

    def body(i, carry):
        here = pl.ds(pl.multiple_of(at + i * chunk, chunk), chunk)
        there = pl.ds(pl.multiple_of(other_at + i * chunk, chunk), chunk)
        target[here, :] = source[here, :] + other[there, :]
        return carry

    lax.fori_loop(0, rows // chunk, body, 0)


class Sum:
    def __init__(self, kind, orders):
        self.kind, self.orders, self.count = kind, orders, len(orders)
        self.scatters = kind != "gather"
        self.gathers = kind != "scatter"

    def blocks(self):
        return GROUP * self.count // SPLIT

    def out_shapes(self):
        if self.gathers:
            return [jax.ShapeDtypeStruct((self.blocks(), D // 2, D), BF)]
        return [jax.ShapeDtypeStruct((self.count, FINAL, WIDTH), BF)]

    def inputs(self):
        return 2 if self.scatters else 1

    def scratch(self):
        n = self.count
        found = []
        if self.scatters:
            found += [
                pltpu.VMEM((n, UNIT, WIDTH), BF),
                pltpu.VMEM((n, UNIT - FINAL, WIDTH), BF),
                pltpu.VMEM((2, UNIT, WIDTH), BF),
                pltpu.SemaphoreType.DMA((n, 2 * GROUP)),
                pltpu.SemaphoreType.DMA((n, BITS)),
                pltpu.SemaphoreType.DMA((n, BITS)),
            ]
        if self.gathers:
            found += [
                pltpu.VMEM((n, UNIT, WIDTH), BF),
                pltpu.SemaphoreType.DMA((n, GROUP)),
                pltpu.SemaphoreType.DMA((n, BITS)),
                pltpu.SemaphoreType.DMA((n, BITS)),
            ]
        else:
            found += [pltpu.SemaphoreType.DMA((n,))]
        return found

    def bind(self, ins, outs, scratch):
        self.me, self.core = lax.axis_index("dp"), lax.axis_index("fsdp")
        self.ins, self.out = ins, outs[0]
        scratch = list(scratch)
        if self.scatters:
            self.held, self.arrived, self.stage, self.load, self.send, self.recv = scratch[:6]
            scratch = scratch[6:]
        if self.gathers:
            self.final, self.local, self.gsend, self.grecv = scratch
        else:
            self.local = scratch[0]

    def spans(self, unit):
        found, base, size = [], 0, UNIT
        for bit in self.orders[unit]:
            size = size // 2
            side = (self.me // (1 << bit)) % 2
            found.append((base + side * size, base + (1 - side) * size, size))
            base = base + side * size
        return found

    def window(self, ref, unit, side):
        block = GROUP * (unit // SPLIT) + side
        return ref.at[block, :, pl.ds((unit % SPLIT) * WIDTH, WIDTH)]

    def loads(self, unit):
        return [
            pltpu.make_async_copy(
                self.window(source, unit, side),
                target.at[pl.ds(side * (D // 2), D // 2)],
                self.load.at[unit, GROUP * which + side],
            )
            for which, (source, target) in enumerate(
                ((self.ins[0], self.held.at[unit]), (self.ins[1], self.stage.at[unit % 2]))
            )
            for side in range(GROUP)
        ]

    def scatter_copy(self, unit, step):
        _, give, size = self.spans(unit)[step]
        return pltpu.make_async_remote_copy(
            src_ref=self.held.at[unit, pl.ds(pl.multiple_of(give, size), size)],
            dst_ref=self.arrived.at[unit, pl.ds(UNIT - 2 * size, size)],
            send_sem=self.send.at[unit, step], recv_sem=self.recv.at[unit, step],
            device_id=(flip(self.me, self.orders[unit][step]), self.core), device_id_type=MESH,
        )

    def gather_copy(self, unit, step):
        keep, _, size = self.spans(unit)[step]
        place = pl.ds(pl.multiple_of(keep, size), size)
        return pltpu.make_async_remote_copy(
            src_ref=self.final.at[unit, place], dst_ref=self.final.at[unit, place],
            send_sem=self.gsend.at[unit, step], recv_sem=self.grecv.at[unit, step],
            device_id=(flip(self.me, self.orders[unit][step]), self.core), device_id_type=MESH,
        )

    def share_copy(self, unit):
        keep, _, size = self.spans(unit)[BITS - 1]
        place = pl.ds(pl.multiple_of(keep, size), size)
        if self.scatters:
            return pltpu.make_async_copy(self.held.at[unit, place], self.out.at[unit], self.local.at[unit])
        return pltpu.make_async_copy(self.ins[0].at[unit], self.final.at[unit, place], self.local.at[unit, 0])

    def outs(self, unit):
        return [
            pltpu.make_async_copy(
                self.final.at[unit, pl.ds(side * (D // 2), D // 2)],
                self.window(self.out, unit, side),
                self.local.at[unit, side],
            )
            for side in range(GROUP)
        ]

    def prefetch(self):
        if self.scatters:
            for unit in range(min(2, self.count)):
                start_all(self.loads(unit))
        else:
            for unit in range(self.count):
                self.share_copy(unit).start()

    def begin(self):
        if not self.scatters:
            for unit in range(self.count):
                self.share_copy(unit).wait()
                self.gather_copy(unit, BITS - 1).start()
            return
        for unit in range(self.count):
            wait_all(self.loads(unit))
            add_rows(self.held.at[unit], self.held.at[unit], 0, self.stage.at[unit % 2], 0, UNIT)
            self.scatter_copy(unit, 0).start()
            if unit + 2 < self.count:
                start_all(self.loads(unit + 2))

    def stages(self):
        return BITS * (self.scatters + self.gathers)

    def advance(self, unit, stage):
        if self.scatters and stage < BITS:
            self.scatter_copy(unit, stage).wait()
            keep, _, size = self.spans(unit)[stage]
            landing = UNIT - 2 * size
            target = self.final if self.gathers and stage == BITS - 1 else self.held
            add_rows(target.at[unit], self.held.at[unit], keep, self.arrived.at[unit], landing, size)
            if stage < BITS - 1:
                self.scatter_copy(unit, stage + 1).start()
            elif self.gathers:
                self.gather_copy(unit, BITS - 1).start()
            else:
                self.share_copy(unit).start()
            return
        step = BITS - 1 - (stage - BITS * self.scatters)
        self.gather_copy(unit, step).wait()
        if step:
            self.gather_copy(unit, step - 1).start()
        else:
            start_all(self.outs(unit))

    def finish(self):
        for unit in range(self.count):
            if self.gathers:
                wait_all(self.outs(unit))
            else:
                self.share_copy(unit).wait()


def bind_sums(sums, ins, outs, scratch):
    ins, outs, scratch = list(ins), list(outs), list(scratch)
    for one in sums:
        a, b, c = one.inputs(), 1, len(one.scratch())
        one.bind(ins[:a], outs[:b], scratch[:c])
        ins, outs, scratch = ins[a:], outs[b:], scratch[c:]


def run_steps(sums, steps):
    owners = [(one, unit) for one in sums for unit in range(one.count)]
    for unit, stage in steps:
        one, own = owners[unit]
        one.advance(own, stage)


class Pull:
    def __init__(self, shapes):
        self.chunks = [
            (which, down, across)
            for which, (downs, acrosses) in enumerate(shapes)
            for down in range(downs)
            for across in range(acrosses)
        ]
        self.shapes = shapes

    def scratch(self):
        n = len(self.chunks)
        return [
            pltpu.VMEM((3, D // 2, D), F32),
            pltpu.SemaphoreType.DMA((n,)),
            pltpu.SemaphoreType.DMA((n,)),
            pltpu.SemaphoreType.DMA((n,)),
        ]

    def bind(self, layer, sources, targets, scratch):
        self.layer, self.sources, self.targets = layer, sources, targets
        self.stage, self.loads, self.sends, self.recvs = scratch
        self.me, self.core = lax.axis_index("dp"), lax.axis_index("fsdp")

    def load(self, i):
        which, down, across = self.chunks[i]
        layer = self.layer[which]
        return pltpu.make_async_copy(
            self.sources[which].at[layer, pl.ds(down * (D // 2), D // 2), pl.ds(across * D, D)],
            self.stage.at[i % 3],
            self.loads.at[i],
        )

    def place(self, i):
        which, down, across = self.chunks[i]
        half = D // 2
        first = pl.multiple_of(self.core * (self.shapes[which][0] * half) + down * half, half)
        return pl.ds(first, half), pl.ds(across * D, D)

    def push(self, i):
        place = self.targets[self.chunks[i][0]].at[self.place(i)]
        return pltpu.make_async_remote_copy(
            src_ref=place, dst_ref=place, send_sem=self.sends.at[i], recv_sem=self.recvs.at[i],
            device_id=(self.me, 1 - self.core), device_id_type=MESH,
        )

    def begin(self):
        for i in range(min(3, len(self.chunks))):
            self.load(i).start()

    def turn(self, i):
        self.load(i).wait()
        self.targets[self.chunks[i][0]][self.place(i)] = self.stage[i % 3].astype(BF)
        self.push(i).start()
        if i + 3 < len(self.chunks):
            self.load(i + 3).start()

    def of(self, which):
        return [i for i, chunk in enumerate(self.chunks) if chunk[0] == which]

    def arrive(self, which):
        for i in self.of(which):
            self.push(i).wait()


def qkv_kernel(pull, h_ref, gain_ref, mean_ref, source, *refs):
    normed_ref, q_ref, k_ref, v_ref, scale_q_ref, scale_k_ref, full_ref = refs[:7]
    weight, sem = refs[7:9]
    step = pl.program_id(0)
    keep = pltpu.make_async_copy(weight, full_ref, sem)
    load = pltpu.make_async_copy(source, weight, sem)
    if pull:
        pull.bind([0], [source], [weight], refs[9:])

    @pl.when(step == 0)
    def _():
        if pull:
            pull.begin()
            meet(0)
            for i in range(len(pull.chunks)):
                pull.turn(i)
        else:
            load.start()

    unit, _ = normalise(h_ref[...].astype(F32))
    normed = (unit * gain_ref[0:1, :]).astype(BF)
    normed_ref[...] = normed

    @pl.when(step == 0)
    def _():
        if pull:
            pull.arrive(0)
            keep.start()
        else:
            load.wait()

    v_ref[...] = dot(normed, weight[:, 2 * D :]).astype(BF)
    for part, out_ref, scale_ref in ((0, q_ref, scale_q_ref), (1, k_ref, scale_k_ref)):
        raw = dot(normed, weight[:, part * D : (part + 1) * D])
        centred = raw - head_mean(raw, mean_ref[...], exact=True)
        scale = lax.rsqrt(head_mean(centred * centred, mean_ref[...]) + norm_eps)
        out_ref[...] = (centred * scale * gain_ref[2 + part : 3 + part, :]).astype(BF)
        scale_ref[...] = scale.astype(BF)

    if pull:

        @pl.when(step == pl.num_programs(0) - 1)
        def _():
            keep.wait()


def qkv_forward(h, gains, mean_mat, source, fresh, collective_id):
    rows = h.shape[0]
    block = min(512, rows)
    row = lambda width: pl.BlockSpec((block, width), lambda i: (i, 0))
    pull = Pull([(1, 3)]) if fresh else None
    full = [jax.ShapeDtypeStruct((D, 3 * D), BF)]
    results = pl.pallas_call(
        functools.partial(qkv_kernel, pull) if fresh else functools.partial(qkv_plain_kernel),
        name="qkv_forward",
        grid=(rows // block,),
        in_specs=[row(D), whole(gains.shape), whole(mean_mat.shape), ANY],
        out_specs=[row(D)] * 6 + [ANY] * fresh,
        out_shape=[jax.ShapeDtypeStruct((rows, D), BF)] * 6 + full * fresh,
        scratch_shapes=[pltpu.VMEM((D, 3 * D), BF), pltpu.SemaphoreType.DMA]
        + (pull.scratch() if fresh else []),
        compiler_params=remote_params(fresh, collective_id),
    )(h, gains, mean_mat, source)
    return results if fresh else [*results, source]


def qkv_plain_kernel(h_ref, gain_ref, mean_ref, source, *refs):
    qkv_kernel(None, h_ref, gain_ref, mean_ref, source, *refs[:6], source, *refs[6:])


def window_at(block, count):
    return block - 1 + (count - 1 - block) // (count - 1) - block // (count - 1)


def pair_stack(x, low_lanes):
    zero = jnp.zeros_like(x)
    return jnp.concatenate([jnp.where(low_lanes, x, zero), jnp.where(low_lanes, zero, x)], axis=0)


def mix_kernel(
    tile, reach, pull, layer, follow, n_source,
    h_ref, q_ref, k_ref, v_ref, seg_ref, code_ref, gain_ref, *refs,
):
    sources, outs, follows, scratch, pull_scratch = carve(
        refs, n_source, 4 + (3 if pull else 0), int(follow), 4 + int(follow), len(refs)
    )
    attended_ref, middle_ref, before_ref, out_ref = outs[:4]
    proj, up, down, sems = scratch[:4]
    weights = (proj, up, down)
    if pull:
        targets = list(weights) + ([scratch[4]] if follow else [])
        pull.bind([layer] * 3 + [layer + 1] * follow, sources, targets, pull_scratch)
        keeps = [
            pltpu.make_async_copy(weight, full, sems.at[i])
            for i, (weight, full) in enumerate(zip(targets, outs[4:] + follows))
        ]
    else:
        loads = [
            pltpu.make_async_copy(source, weight, sems.at[i])
            for i, (source, weight) in enumerate(zip(sources, weights))
        ]
    step = pl.program_id(0)
    count = k_ref.shape[0] // tile
    keys = reach * tile
    factor = LOG2E * HEAD_DIM ** (-0.5)
    low_lanes = lax.broadcasted_iota(jnp.int32, (tile, 128), 1) < HEAD_DIM

    @pl.when(step == 0)
    def _():
        if pull:
            pull.begin()
            meet(0)
        else:
            start_all(loads)

    @pl.when(step < count)
    def _():
        first = pl.multiple_of(window_at(step, count) * tile if count > reach else 0, tile)
        window = pl.ds(first, keys)
        here = pl.ds(pl.multiple_of(step * tile, tile), tile)
        seg = seg_ref[here, :]
        code = code_ref[:, window]
        query_at = step * tile + lax.broadcasted_iota(jnp.int32, (tile, keys), 0)
        key_at = first + lax.broadcasted_iota(jnp.int32, (tile, keys), 1)
        bias = jnp.where((seg == code) | (query_at == key_at), 0.0, MASKED)
        bias = jnp.concatenate([bias, bias], axis=0)

        def front(pair):
            lanes = slice(pair * 128, (pair + 1) * 128)
            return dot_nt(pair_stack(q_ref[here, lanes], low_lanes), k_ref[window, lanes])

        following = front(0)
        for pair in range(HEADS // 2):
            lanes = slice(pair * 128, (pair + 1) * 128)
            scores = following
            if pair + 1 < HEADS // 2:
                following = front(pair + 1)
            expo = jnp.exp2(scores * factor + bias)
            total = jnp.sum(expo, axis=-1, keepdims=True)
            mixed = dot(expo.astype(BF), v_ref[window, lanes]) * (1.0 / total)
            attended_ref[here, lanes] = jnp.where(low_lanes, mixed[:tile], mixed[tile:]).astype(BF)

    if pull:
        per_step = -(-len(pull.chunks) // count)
        for turn in range(count):
            mine = range(turn * per_step, min((turn + 1) * per_step, len(pull.chunks)))
            if mine:

                @pl.when(step == turn)
                def _():
                    for i in mine:
                        pull.turn(i)

    @pl.when(step == count)
    def _():
        if pull:
            for which in range(3):
                pull.arrive(which)
                keeps[which].start()
        else:
            wait_all(loads)

    @pl.when(step >= count)
    def _():
        rows = h_ref.shape[0]
        here = pl.ds(pl.multiple_of((step - count) * rows, rows), rows)
        middle = h_ref[...].astype(F32) + dot(attended_ref[here, :], proj[...])
        middle_ref[...] = middle
        unit, _ = normalise(middle)
        normed = (unit * gain_ref[1:2, :]).astype(BF)
        result = middle
        for part in range(up.shape[1] // D):
            lanes = slice(part * D, (part + 1) * D)
            before = dot(normed, up[:, lanes])
            before_ref[:, lanes] = before.astype(BF)
            active = jax.nn.gelu(before, approximate=True).astype(BF)
            result = result + dot(active, down[lanes, :])
        out_ref[...] = result.astype(out_ref.dtype)

    if pull:

        @pl.when(step == pl.num_programs(0) - 1)
        def _():
            if follow:
                pull.arrive(3)
                keeps[3].start()
            wait_all(keeps)


def mix_forward(h, q, k, v, seg, code, gains, sources, out_type, layer, paired, collective_id):
    rows = h.shape[0]
    block = min(512, rows)
    tile = min(128, rows)
    reach = min(3, rows // tile)
    count = rows // tile
    width = sources[1].shape[-1]
    follow = len(sources) > 3
    shapes = [(1, 1), (1, width // D), (width // D, 1)] + [(1, 3)] * follow
    pull = Pull(shapes) if paired else None
    row = lambda w: pl.BlockSpec((block, w), lambda i: (jnp.maximum(i - count, 0), 0))
    outs = [(D, F32), (width, BF), (D, out_type)]
    fulls = [(D, D), (D, width), (width, D)]
    follows = [(D, 3 * D)] * follow
    results = pl.pallas_call(
        functools.partial(mix_kernel, tile, reach, pull, layer, follow, len(sources)),
        name="mix_forward",
        grid=(count + rows // block,),
        in_specs=[row(D)] + [whole(x.shape) for x in (q, k, v, seg, code, gains)] + [ANY] * len(sources),
        out_specs=[pl.BlockSpec((rows, D), lambda i: (0, 0), pipeline_mode=pl.Buffered(1))]
        + [row(w) for w, _ in outs]
        + [ANY] * (len(fulls + follows) if paired else 0),
        out_shape=[jax.ShapeDtypeStruct((rows, D), BF)]
        + [jax.ShapeDtypeStruct((rows, w), t) for w, t in outs]
        + [jax.ShapeDtypeStruct(x, BF) for x in (fulls + follows if paired else [])],
        scratch_shapes=[pltpu.VMEM(x, BF) for x in fulls]
        + [pltpu.SemaphoreType.DMA((4,))]
        + [pltpu.VMEM(x, BF) for x in follows]
        + (pull.scratch() if paired else []),
        compiler_params=remote_params(paired, collective_id),
    )(h, q, k, v, seg, code, gains, *sources)
    return results if paired else [*results, *sources]


class Blocks:
    def __init__(self, count, paired):
        self.count, self.paired = count, paired

    def out_shapes(self):
        rows = D // 2 if self.paired else D
        return [jax.ShapeDtypeStruct((self.count, rows, D), BF)] * (1 + self.paired)

    def scratch(self):
        return [pltpu.SemaphoreType.DMA((self.count,))] * (1 + 2 * self.paired)

    def bind(self, outs, sems):
        self.outs, self.sems = outs, sems

    def copies(self, block, lanes, ref, first_row):
        if not self.paired:
            return [
                pltpu.make_async_copy(
                    ref.at[pl.ds(first_row, D), lanes], self.outs[0].at[block], self.sems[0].at[block]
                )
            ]
        core = lax.axis_index("fsdp")
        half = D // 2
        mine = pl.multiple_of(first_row + core * half, half)
        theirs = pl.multiple_of(first_row + (1 - core) * half, half)
        return [
            pltpu.make_async_copy(
                ref.at[pl.ds(mine, half), lanes], self.outs[0].at[block], self.sems[0].at[block]
            ),
            pltpu.make_async_remote_copy(
                src_ref=ref.at[pl.ds(theirs, half), lanes], dst_ref=self.outs[1].at[block],
                send_sem=self.sems[1].at[block], recv_sem=self.sems[2].at[block],
                device_id=(lax.axis_index("dp"), 1 - core), device_id_type=MESH,
            ),
        ]


def carve(refs, *sizes):
    found, at = [], 0
    for size in sizes:
        found.append(refs[at : at + size])
        at += size
    return found


def sums_in(sums):
    return sum(one.inputs() for one in sums)


def sums_scratch(sums):
    return [shape for one in sums for shape in one.scratch()]


def sums_outs(sums):
    return [shape for one in sums for shape in one.out_shapes()]


def remote_params(paired, collective_id):
    if not paired:
        return params()
    return pltpu.CompilerParams(
        dimension_semantics=("arbitrary",), vmem_limit_bytes=VMEM_LIMIT,
        collective_id=collective_id, has_side_effects=True,
    )


def ffn_back_kernel(blocks, store, sums, plan, dh_ref, before_ref, middle_ref, gain_ref, *refs):
    weights, ins, outs, store_outs, sum_outs, own_scratch, store_sems, sum_scratch = carve(
        refs, 2, sums_in(sums), 2, 1 + store.paired, len(sums), 7, 1 + 2 * store.paired,
        len(sums_scratch(sums)),
    )
    dmid_ref, dgain_ref = outs
    up, down, active, dbefore, dbranch, normed, sems = own_scratch
    store.bind(store_outs, store_sems)
    bind_sums(sums, ins, sum_outs, sum_scratch)
    step = pl.program_id(0)
    copies = [
        pltpu.make_async_copy(source, target, sems.at[i])
        for i, (source, target) in enumerate(zip(weights, (up, down)))
    ]
    parts = up.shape[1] // D
    rows = dh_ref.shape[0]

    @pl.when(step == 0)
    def _():
        start_all(copies)
        dgain_ref[...] = jnp.zeros_like(dgain_ref)
        for one in sums:
            one.prefetch()
        if store.paired:
            meet(BITS if sums else 0)
        for one in sums:
            one.begin()

    @pl.when(step < blocks)
    def _():
        here = pl.ds(pl.multiple_of(step * rows, rows), rows)
        dh = dh_ref[...].astype(F32)
        branch = dh.astype(BF)
        dbranch[here, :] = branch
        gain = gain_ref[1:2, :]
        unit, scale = normalise(middle_ref[...])
        normed[here, :] = (unit * gain).astype(BF)

        @pl.when(step == 0)
        def _():
            wait_all(copies)

        def front(part):
            return dot_nt(branch, down[part * D : (part + 1) * D, :])

        dnormed = jnp.zeros((rows, D), F32)
        early = not sums
        following = front(0) if early else None
        for part in range(parts):
            lanes = slice(part * D, (part + 1) * D)
            dactive = following if early else front(part)
            if early and part + 1 < parts:
                following = front(part + 1)
            value = before_ref[:, lanes].astype(F32)
            root = math.sqrt(2.0 / math.pi)
            square = value * value
            curve = jnp.tanh(value * (root + (root * 0.044715) * square))
            half = 0.5 * (1.0 + curve)
            active[here, lanes] = (value * half).astype(BF)
            slope = half + (0.5 * value) * (1.0 - curve * curve) * (
                root + (3.0 * 0.044715 * root) * square
            )
            dpart = (dactive * slope).astype(BF)
            dbefore[here, lanes] = dpart
            dnormed = dnormed + dot_nt(dpart, up[:, lanes])
            for block in range(blocks):
                if block * parts + part in plan:

                    @pl.when(step == block)
                    def _():
                        run_steps(sums, plan[block * parts + part])

        dmid_ref[...] = dh + norm_back(dnormed, gain, unit, scale)
        dgain_ref[...] += column_sum(dnormed * unit)

    late = blocks * parts - blocks
    for tick in sorted(plan):
        if tick >= blocks * parts:

            @pl.when(step == tick - late)
            def _():
                run_steps(sums, plan[tick])

    every = slice(0, D)

    @pl.when((step >= blocks) & (step < blocks + parts))
    def _():
        part = step - blocks
        lanes = pl.ds(pl.multiple_of(part * D, D), D)
        up[:, lanes] = dot_tn(normed[...], dbefore[:, lanes]).astype(BF)
        start_all(store.copies(part, lanes, up, 0))

    @pl.when(step >= blocks + parts)
    def _():
        part = step - blocks - parts
        half = D // 2
        base = down.shape[0] // 2
        first_row = pl.multiple_of(part * D, D)
        for side in range(2):
            lanes = pl.ds(pl.multiple_of(side * base + part * half, half), half)
            here = pl.ds(pl.multiple_of(first_row + side * half, half), half)
            down[here, :] = dot_tn(active[:, lanes], dbranch[...]).astype(BF)
        start_all(store.copies(parts + part, every, down, first_row))

    @pl.when(step == blocks + 2 * parts - 1)
    def _():
        for part in range(parts):
            wait_all(store.copies(part, slice(part * D, (part + 1) * D), up, 0))
        for part in range(parts):
            wait_all(store.copies(parts + part, every, down, part * D))
        for one in sums:
            one.finish()


def ffn_backward(dh, before, middle, gains, shards, paired, sums, plan, sum_ins, collective_id):
    rows, width = before.shape
    block = min(512, rows)
    blocks = rows // block
    parts = width // D
    store = Blocks(2 * parts, paired)
    row = lambda w, **mode: pl.BlockSpec((block, w), lambda i: (jnp.minimum(i, blocks - 1), 0), **mode)
    once = {"pipeline_mode": pl.Buffered(1)} if sums else {}
    outs = store.out_shapes() + sums_outs(sums)
    return pl.pallas_call(
        functools.partial(ffn_back_kernel, blocks, store, sums, plan),
        name="ffn_backward",
        grid=(blocks + 2 * parts,),
        in_specs=[row(D, **once), row(width), row(D, **once), whole(gains.shape)] + [ANY] * (2 + len(sum_ins)),
        out_specs=[row(D), pl.BlockSpec((8, D), lambda i: (0, 0))] + [ANY] * len(outs),
        out_shape=[jax.ShapeDtypeStruct((rows, D), F32), jax.ShapeDtypeStruct((8, D), F32)] + outs,
        scratch_shapes=[
            pltpu.VMEM((D, width), BF),
            pltpu.VMEM((width, D), BF),
            pltpu.VMEM((rows, width), BF),
            pltpu.VMEM((rows, width), BF),
            pltpu.VMEM((rows, D), BF),
            pltpu.VMEM((rows, D), BF),
            pltpu.SemaphoreType.DMA((2,)),
        ]
        + store.scratch()
        + sums_scratch(sums),
        compiler_params=remote_params(paired, collective_id),
    )(dh, before, middle, gains, *shards, *sum_ins)


def attn_back_kernel(
    tile, reach, rows, store, sums, plan,
    seg_ref, code_ref, gain_ref, heads_ref, mean_ref, *refs,
):
    sources, refs = refs[:8], refs[8:]
    weights, ins, outs, store_outs, sum_outs, own_scratch, store_sems, sum_scratch = carve(
        refs, 3, sums_in(sums), 2, 1 + store.paired, len(sums), 18, 1 + 2 * store.paired,
        len(sums_scratch(sums)),
    )
    normed_ref, qkv_ref, proj_ref = weights
    dh_ref, dgain_ref = outs
    qkv, proj, dattended, inner, dk, dv, dmixed, sems, normed_sem = own_scratch[:9]
    held = own_scratch[9:17]
    dmid_ref, attended_ref, q_ref, k_ref, v_ref, scale_q_ref, scale_k_ref, h_ref = held
    loads = [
        pltpu.make_async_copy(source, target, own_scratch[17].at[i])
        for i, (source, target) in enumerate(zip(sources, held))
    ]
    store.bind(store_outs, store_sems)
    bind_sums(sums, ins, sum_outs, sum_scratch)
    step = pl.program_id(0)
    total_rows = k_ref.shape[0]
    count = total_rows // tile
    keys = reach * tile
    blocks = total_rows // rows
    proj_copy = pltpu.make_async_copy(proj_ref, proj, sems.at[0])
    qkv_copy = pltpu.make_async_copy(qkv_ref, qkv, sems.at[1])
    normed_copy = pltpu.make_async_copy(normed_ref, dattended, normed_sem)
    root = HEAD_DIM ** (-0.5)

    def head_norm_back(grad, gain, unit, scale):
        scaled = grad * gain
        first = head_mean(scaled, mean_ref[...])
        second = head_mean(scaled * unit, mean_ref[...])
        return scale.astype(F32) * (scaled - first - unit * second)

    @pl.when(step == 0)
    def _():
        proj_copy.start()
        start_all(loads)
        qkv_copy.start()
        dgain_ref[...] = jnp.zeros_like(dgain_ref)
        dk[...] = jnp.zeros_like(dk)
        dv[...] = jnp.zeros_like(dv)
        for one in sums:
            one.prefetch()
        if store.paired:
            meet(BITS if sums else 0)
        for one in sums:
            one.begin()
        proj_copy.wait()
        wait_all(loads[:2])
        for block in range(blocks):
            here = slice(block * rows, (block + 1) * rows)
            back = dot_nt(dmid_ref[here, :].astype(BF), proj[...]).astype(BF)
            dattended[here, :] = back
            product = back.astype(F32) * attended_ref[here, :].astype(F32)
            high = product.astype(BF)
            low = (product - high.astype(F32)).astype(BF)
            turn = (((0,), (1,)), ((), ()))
            inner[:, here] = lax.dot_general(
                heads_ref[...], high, turn, preferred_element_type=F32
            ) + lax.dot_general(heads_ref[...], low, turn, preferred_element_type=F32)

        wait_all(loads[2:6])

    for tick in sorted(plan):

        @pl.when(step == tick)
        def _():
            run_steps(sums, plan[tick])

    @pl.when(step < count)
    def _():
        first = pl.multiple_of(window_at(step, count) * tile if count > reach else 0, tile)
        window = pl.ds(first, keys)
        here = pl.ds(pl.multiple_of(step * tile, tile), tile)
        low_lanes = lax.broadcasted_iota(jnp.int32, (tile, 128), 1) < HEAD_DIM
        seg = seg_ref[:, here]
        code = code_ref[window, :]
        key_at = first + lax.broadcasted_iota(jnp.int32, (keys, tile), 0)
        query_at = step * tile + lax.broadcasted_iota(jnp.int32, (keys, tile), 1)
        bias = jnp.where((seg == code) | (query_at == key_at), 0.0, MASKED)
        bias = jnp.concatenate([bias, bias], axis=1)
        dq_parts = []

        def front(pair):
            lanes = slice(pair * 128, (pair + 1) * 128)
            queries = pair_stack(q_ref[here, lanes], low_lanes)
            grads = pair_stack(dattended[here, lanes], low_lanes)
            keys_part = k_ref[window, lanes]
            scores = dot_nt(keys_part, queries)
            return queries, grads, keys_part, scores, dot_nt(v_ref[window, lanes], grads)

        following = front(0)
        for pair in range(HEADS // 2):
            lanes = slice(pair * 128, (pair + 1) * 128)
            queries, grads, keys_part, scores, dprobs = following
            if pair + 1 < HEADS // 2:
                following = front(pair + 1)
            expo = jnp.exp2(scores * (LOG2E * root) + bias)
            probs = expo * (1.0 / jnp.sum(expo, axis=0, keepdims=True))
            less = jnp.concatenate(
                [inner[2 * pair : 2 * pair + 1, here], inner[2 * pair + 1 : 2 * pair + 2, here]],
                axis=1,
            )
            dscores = (probs * (dprobs - less)).astype(BF)
            dv[window, lanes] += dot(probs.astype(BF), grads)
            dk[window, lanes] += dot(dscores, queries)
            dq = dot_tn(dscores, keys_part)
            dq_parts.append(jnp.where(low_lanes, dq[:tile], dq[tile:]))
        dq = jnp.concatenate(dq_parts, axis=1) * root
        gain = gain_ref[2:3, :]
        unit = q_ref[here, :].astype(F32) * (1.0 / gain)
        dmixed[here, 0:D] = head_norm_back(dq, gain, unit, scale_q_ref[here, :]).astype(BF)
        dgain_ref[8:16, :] += column_sum(dq * unit)

    @pl.when(step == count)
    def _():
        normed_copy.start()
        qkv_copy.wait()
        wait_all(loads[6:])

    @pl.when((step >= count) & (step < count + blocks))
    def _():
        here = pl.ds(pl.multiple_of((step - count) * rows, rows), rows)
        grad = dk[here, :] * root
        gain = gain_ref[3:4, :]
        unit = k_ref[here, :].astype(F32) * (1.0 / gain)
        dmixed[here, D : 2 * D] = head_norm_back(grad, gain, unit, scale_k_ref[here, :]).astype(BF)
        dgain_ref[16:24, :] += column_sum(grad * unit)
        dmixed[here, 2 * D :] = dv[here, :].astype(BF)
        dnormed = dot_nt(dmixed[here, :], qkv[...])
        unit, scale = normalise(h_ref[here, :].astype(F32))
        dh_ref[...] = dmid_ref[here, :] + norm_back(dnormed, gain_ref[0:1, :], unit, scale)
        dgain_ref[0:8, :] += column_sum(dnormed * unit)

    @pl.when(step == count + blocks)
    def _():
        normed_copy.wait()

    @pl.when((step >= count + blocks) & (step < count + blocks + 3))
    def _():
        part = step - count - blocks
        lanes = pl.ds(pl.multiple_of(part * D, D), D)
        qkv[:, lanes] = dot_tn(dattended[...], dmixed[:, lanes]).astype(BF)
        start_all(store.copies(part, lanes, qkv, 0))

    every = slice(0, D)

    @pl.when(step == count + blocks + 3)
    def _():
        proj[...] = dot_tn(attended_ref[...], dmid_ref[...].astype(BF)).astype(BF)
        start_all(store.copies(3, every, proj, 0))
        for part in range(3):
            wait_all(store.copies(part, slice(part * D, (part + 1) * D), qkv, 0))
        wait_all(store.copies(3, every, proj, 0))
        for one in sums:
            one.finish()


def attn_backward(
    dmid, h, saved, attended, segs, gains, heads, mean_mat, shards, paired, sums, plan, sum_ins, collective_id
):
    total = h.shape[0]
    rows = min(512, total)
    tile = min(128, total)
    reach = min(3, total // tile)
    count, blocks = total // tile, total // rows
    normed, q, k, v, scale_q, scale_k = saved
    ins = [*segs, gains, heads, mean_mat]
    large = [dmid, attended, q, k, v, scale_q, scale_k, h]
    store = Blocks(4, paired)
    outs = store.out_shapes() + sums_outs(sums)
    return pl.pallas_call(
        functools.partial(attn_back_kernel, tile, reach, rows, store, sums, plan),
        name="attn_backward",
        grid=(count + blocks + 4,),
        in_specs=[whole(x.shape) for x in ins] + [ANY] * (len(large) + 3 + len(sum_ins)),
        out_specs=[
            pl.BlockSpec((rows, D), lambda i: (jnp.clip(i - count, 0, blocks - 1), 0)),
            pl.BlockSpec((24, D), lambda i: (0, 0)),
        ]
        + [ANY] * len(outs),
        out_shape=[jax.ShapeDtypeStruct((total, D), F32), jax.ShapeDtypeStruct((24, D), F32)] + outs,
        scratch_shapes=[
            pltpu.VMEM((D, 3 * D), BF),
            pltpu.VMEM((D, D), BF),
            pltpu.VMEM((total, D), BF),
            pltpu.VMEM((128, total), F32),
            pltpu.VMEM((total, D), F32),
            pltpu.VMEM((total, D), F32),
            pltpu.VMEM((total, 3 * D), BF),
            pltpu.SemaphoreType.DMA((2,)),
            pltpu.SemaphoreType.DMA,
        ]
        + [pltpu.VMEM(x.shape, x.dtype) for x in large]
        + [pltpu.SemaphoreType.DMA((len(large),))]
        + store.scratch()
        + sums_scratch(sums),
        compiler_params=remote_params(paired, collective_id),
    )(*ins, *large, normed, *shards, *sum_ins)


def last_sums_kernel(sums, steps, counts, *refs):
    n_in, n_out = counts
    small, ins = refs[0], refs[1 : 1 + n_in]
    small_total, outs = refs[1 + n_in], refs[2 + n_in : 2 + n_in + n_out]
    small_held, small_arrived, small_send, small_recv = refs[2 + n_in + n_out : 6 + n_in + n_out]
    bind_sums(sums, ins, outs, refs[6 + n_in + n_out :])
    me, core = lax.axis_index("dp"), lax.axis_index("fsdp")
    for one in sums:
        one.prefetch()
    meet(BITS)

    def small_copy(step):
        to = (me, 1 - core) if step == 0 else (flip(me, step - 1), core)
        return pltpu.make_async_remote_copy(
            src_ref=small_held.at[step], dst_ref=small_arrived.at[step],
            send_sem=small_send.at[step], recv_sem=small_recv.at[step],
            device_id=to, device_id_type=MESH,
        )

    small_held[0] = small[...]
    small_copy(0).start()
    for one in sums:
        one.begin()
    each = -(-len(steps) // (BITS + 1))
    for stage in range(BITS + 1):
        run_steps(sums, steps[stage * each : (stage + 1) * each])
        small_copy(stage).wait()
        value = small_held[stage] + small_arrived[stage]
        if stage < BITS:
            small_held[stage + 1] = value
            small_copy(stage + 1).start()
        else:
            small_total[...] = value
    for one in sums:
        one.finish()


def last_sums(sums, steps, small, ins, collective_id):
    vmem = pl.BlockSpec(memory_space=pltpu.VMEM)
    outs = [shape for one in sums for shape in one.out_shapes()]
    return pl.pallas_call(
        functools.partial(last_sums_kernel, sums, steps, (len(ins), len(outs))),
        name="last_sums",
        in_specs=[vmem] + [ANY] * len(ins),
        out_specs=[vmem] + [ANY] * len(outs),
        out_shape=[jax.ShapeDtypeStruct(small.shape, F32)] + outs,
        scratch_shapes=[
            pltpu.VMEM((BITS + 1, *small.shape), F32),
            pltpu.VMEM((BITS + 1, *small.shape), F32),
            pltpu.SemaphoreType.DMA((BITS + 1,)),
            pltpu.SemaphoreType.DMA((BITS + 1,)),
        ]
        + [shape for one in sums for shape in one.scratch()],
        compiler_params=pltpu.CompilerParams(
            collective_id=collective_id, has_side_effects=True, vmem_limit_bytes=VMEM_LIMIT
        ),
    )(small, *ins)


CORRECTION = 1.0 - 0.5**STEP


def adam(weight, first, second, grad, rate, decay):
    first = 0.5 * first + 0.5 * grad
    second = 0.5 * second + 0.5 * grad * grad
    step = first / CORRECTION / (jnp.sqrt(second / CORRECTION) + adam_eps)
    return weight - rate * (step + decay * weight), first, second


def adam_kernel(weight_ref, first_ref, second_ref, *refs):
    grad_refs, outs = refs[:-3], refs[-3:]
    for layer, grad_ref in enumerate(grad_refs):

        @pl.when(pl.program_id(0) == layer)
        def _():
            results = adam(
                weight_ref[0], first_ref[0], second_ref[0], grad_ref[0].astype(F32), D ** (-0.5), 0.1
            )
            for out, result in zip(outs, results):
                out[0] = result


def adam_step(weight, first, second, totals, base):
    layers, rows, width = weight.shape
    half = D // 2
    down, across = rows // half, width // D
    last = down * across - 1
    part = pl.BlockSpec((1, half, D), lambda l, i, j: (l, i, j))

    def grad_spec(layer):
        def at(l, i, j):
            inside = jnp.where(l < layer, 0, last)
            return (base + jnp.where(l == layer, i * across + j, inside), 0, 0)

        return pl.BlockSpec((1, half, D), at)

    return pl.pallas_call(
        adam_kernel,
        name="adam_step",
        grid=(layers, down, across),
        in_specs=[part] * 3 + [grad_spec(layer) for layer in range(layers)],
        out_specs=[part] * 3,
        out_shape=[jax.ShapeDtypeStruct(weight.shape, F32)] * 3,
        compiler_params=params(3),
    )(weight, first, second, *totals)


def per_device(dp, fsdp, *args):
    tokens, cotangent, segments, keep_mask = args[:4]
    masters, firsts, seconds = args[4::3], args[5::3], args[6::3]
    packs, length, width = tokens.shape
    layers = masters[0].shape[0]
    paired = (dp, fsdp) == (1 << BITS, 2)
    me = lax.axis_index("fsdp")

    def gather(shard):
        return lax.all_gather(shard.astype(BF), "fsdp", axis=0, tiled=True)

    gains_all = lax.all_gather(masters[4].astype(BF), "fsdp", axis=1, tiled=True).astype(F32)
    gains_all = jnp.pad(gains_all.transpose(0, 2, 1), ((0, 0), (0, 4), (0, 0)))
    channel = np.arange(D) // HEAD_DIM
    heads = (channel[:, None] == np.arange(128)[None, :]).astype(BF)
    mean_mat = ((channel[:256, None] == channel[None, :256]) / HEAD_DIM).astype(BF)
    seg = segments[0]
    code = jnp.where(keep_mask[0] == 1, seg, -1)

    hidden = tokens[0]
    stored, held = [], []
    qkv = masters[0] if paired else gather(masters[0][0])
    for layer in range(layers):
        gains = gains_all[layer]
        last = layer == layers - 1
        fresh = paired and layer == 0
        *saved, qkv = qkv_forward(hidden, gains, mean_mat, qkv, fresh, 2 * layers + 1)
        q, k, v = saved[1:4]
        if paired:
            sources = [masters[kind] for kind in (1, 2, 3)] + ([] if last else [masters[0]])
        else:
            sources = [gather(masters[kind][layer]) for kind in (1, 2, 3)]
        attended, middle, before, result, proj, up, down, *following = mix_forward(
            hidden, q, k, v, seg[:, None], code[None, :], gains, sources, BF if last else F32,
            layer, paired, 2 * layers + 2 + layer,
        )
        stored.append((hidden, saved, attended, middle, before))
        held.append((qkv, proj, up, down))
        hidden = result
        if not last:
            qkv = following[0] if paired else gather(masters[0][layer + 1])
    output = hidden.reshape(tokens.shape)

    made, shared = None, None
    totals = []
    d_hidden = cotangent[0]
    small = [None] * layers
    leaves = [None] * (2 * layers)
    for order, (layer, kind) in enumerate(
        (layer, kind) for layer in reversed(range(layers)) for kind in ("ffn", "attn")
    ):
        qkv, proj, up, down = held[layer]
        gains = gains_all[layer]
        h, saved, attended, middle, before = stored[layer]
        sums, sum_ins = [], []
        if paired and shared is not None:
            sums.append(Sum("gather", shared[1]))
            sum_ins.append(shared[0])
        if paired and made is not None:
            sums.append(Sum("scatter", made[1]))
            sum_ins += made[0]
        plan = PLANS[order - 1] if sums else {}
        if kind == "ffn":
            results = ffn_backward(
                d_hidden, before, middle, gains, (up, down), paired, sums, plan, sum_ins, order
            )
            d_middle, gain_two = results[:2]
        else:
            results = attn_backward(
                d_middle, h, saved, attended, (seg[None, :], code[:, None]), gains, heads, mean_mat,
                (qkv, proj), paired, sums, plan, sum_ins, order,
            )
            d_hidden, gain_rest = results[:2]
            gain_rest = gain_rest.reshape(3, 8, D).sum(1)
            small[layer] = jnp.stack([gain_rest[0], gain_two.sum(0), gain_rest[1], gain_rest[2]])
        results = results[2:]
        leaves[order] = results[0]
        if paired:
            made, results = (results[:2], ORDERS[order]), results[2:]
            if shared is not None:
                totals.append(results[0])
                results = results[1:]
            shared = (results[0], sums[-1].orders) if results else None
    small = jnp.concatenate(small)
    input_grad = d_hidden.reshape(tokens.shape)

    updated = []
    wide = masters[2].shape[2] // D
    if paired:
        sums = [Sum("gather", shared[1]), Sum("both", made[1])]
        small, *rest = last_sums(sums, LAST_STEPS, small, [shared[0], *made[0]], 2 * layers)
        totals += rest
        totals = list(reversed(totals))
        for kind, (which, base) in enumerate(((0, 0), (0, 3), (1, 0), (1, wide))):
            updated.append(
                adam_step(masters[kind], firsts[kind], seconds[kind], totals[which::2], base)
            )
    else:
        small = lax.psum(small, ("dp", "fsdp"))
        leaves = list(reversed(leaves))
        attn, ffn = jnp.stack(leaves[0::2]), jnp.stack(leaves[1::2])
        across = lambda x: x.transpose(0, 2, 1, 3).reshape(layers, D, -1)
        full = (
            across(attn[:, :3]),
            attn[:, 3],
            across(ffn[:, :wide]),
            ffn[:, wide:].reshape(layers, wide, 2, D // 2, D).transpose(0, 2, 1, 3, 4)
            .reshape(layers, wide * D, D),
        )
        for kind in range(4):
            grad = lax.psum_scatter(full[kind], "fsdp", scatter_dimension=1, tiled=True)
            grad = lax.psum(grad, "dp").astype(F32)
            updated.append(adam(masters[kind], firsts[kind], seconds[kind], grad, D ** (-0.5), 0.1))
    small = small.reshape(layers, 4, D).transpose(0, 2, 1)
    share = masters[4].shape[1]
    small = lax.dynamic_slice_in_dim(small, me * share, share, 1)
    updated.append(adam(masters[4], firsts[4], seconds[4], small, 0.5, 0.0))
    return (output, input_grad, *[x for group in updated for x in group])


ORDERS = (
    (XYZ, XZY, YXZ, YXZ, ZXY, ZYX),
    (XZY, YZX, XYZ),
    (XYZ, ZYX, YXZ, YZX, XZY, ZXY),
    (YXZ, XYZ, ZXY),
)
PLANS = (
    {
        4: ((0, 0), (1, 0), (2, 0), (3, 0),),
        5: ((4, 0), (5, 0),),
        6: ((0, 1), (1, 1),),
        8: ((5, 1), (0, 2), (1, 2), (2, 1), (3, 1), (4, 1),),
        9: ((5, 2), (0, 3), (4, 2), (1, 3),),
        10: ((2, 2), (3, 2),),
        11: ((5, 3),),
        12: ((4, 3),),
        13: ((2, 3), (3, 3),),
    },
    {
        2: ((0, 0), (1, 0), (2, 0), (7, 0), (3, 0), (4, 0), (5, 0),),
        3: ((1, 1),),
        4: ((4, 1), (6, 0), (0, 1), (5, 1), (8, 0), (2, 1),),
        5: ((3, 1),),
        6: ((7, 1), (4, 2),),
        7: ((1, 2), (6, 1),),
        8: ((2, 2), (0, 2), (5, 2), (8, 1),),
        9: ((7, 2), (6, 2), (3, 2),),
        13: ((7, 3), (6, 3), (4, 3), (8, 2),),
        15: ((2, 3), (8, 3), (1, 3), (0, 3), (5, 3), (3, 3),),
    },
    {
        0: ((0, 0), (1, 0), (2, 0),),
        3: ((3, 0), (1, 1), (0, 1), (2, 1),),
        4: ((7, 0), (5, 0),),
        5: ((4, 0), (6, 0),),
        6: ((8, 0), (5, 1),),
        7: ((3, 1), (2, 2),),
        8: ((4, 1), (8, 1),),
        9: ((1, 2), (0, 2), (5, 2), (8, 2), (7, 1), (3, 2), (4, 2), (6, 1),),
        10: ((2, 3),),
        12: ((7, 2), (5, 3), (6, 2), (8, 3),),
        13: ((3, 3), (4, 3), (1, 3), (0, 3), (7, 3), (6, 3),),
    },
)
LAST_STEPS = ((0, 0), (1, 0), (6, 0), (2, 0), (7, 0), (3, 0), (4, 0), (5, 0), (0, 1), (1, 1), (2, 1), (3, 1), (6, 1), (4, 1), (5, 1), (2, 2), (7, 1), (8, 0), (5, 2), (6, 2), (0, 2), (1, 2), (8, 1), (3, 2), (7, 2), (6, 3), (8, 2), (4, 2), (0, 3), (2, 3), (7, 3), (6, 4), (8, 3), (3, 3), (7, 4), (4, 3), (8, 4), (6, 5), (8, 5), (7, 5), (5, 3), (1, 3), (6, 6), (7, 6), (8, 6), (6, 7), (7, 7), (8, 7))


def solution(mesh):
    rows = P(("dp", "fsdp"), None, None)
    weight = P(None, "fsdp", None)
    flat = P(("dp", "fsdp"), None)
    return jax.shard_map(
        functools.partial(per_device, mesh.shape["dp"], mesh.shape["fsdp"]),
        mesh=mesh,
        in_specs=(rows, rows, flat, flat) + (weight,) * 15,
        out_specs=(rows, rows) + (weight,) * 15,
        check_vma=False,
    )
```

```python
import functools
import math

import jax
import jax.numpy as jnp
import numpy as np
from jax import lax
from jax.experimental import pallas as pl
from jax.experimental.pallas import tpu as pltpu
from jax.sharding import PartitionSpec as P

D = 768
HEADS = 12
HEAD_DIM = 64
STEP = 5
BF = jnp.bfloat16
F32 = jnp.float32
norm_eps = 1e-06
adam_eps = 1e-08
VMEM_LIMIT = 62 * 1024 * 1024
LOG2E = 1.4426950408889634
MASKED = -1e30


def dot(a, b):
    return lax.dot_general(a, b, (((1,), (0,)), ((), ())), preferred_element_type=F32)


def dot_nt(a, b):
    return lax.dot_general(a, b, (((1,), (1,)), ((), ())), preferred_element_type=F32)


def dot_tn(a, b):
    return lax.dot_general(a, b, (((0,), (0,)), ((), ())), preferred_element_type=F32)


def head_mean(x, mean_mat, exact=False):
    width = mean_mat.shape[0]
    found = []
    for at in range(0, x.shape[1], width):
        part = x[:, at : at + width]
        high = part.astype(BF)
        mean = dot(high, mean_mat)
        if exact:
            mean = mean + dot((part - high.astype(F32)).astype(BF), mean_mat)
        found.append(mean)
    return jnp.concatenate(found, axis=1)


def normalise(values):
    average = jnp.mean(values, axis=-1, keepdims=True)
    centred = values - average
    spread = jnp.mean(centred * centred, axis=-1, keepdims=True)
    scale = lax.rsqrt(spread + norm_eps)
    return centred * scale, scale


def norm_back(grad, gain, unit, scale):
    scaled = grad * gain
    first = jnp.mean(scaled, axis=-1, keepdims=True)
    second = jnp.mean(scaled * unit, axis=-1, keepdims=True)
    return scale * (scaled - first - unit * second)


def column_sum(x):
    return jnp.sum(x.reshape(x.shape[0] // 8, 8, x.shape[1]), axis=0)


def start_all(copies):
    for copy in copies:
        copy.start()


def wait_all(copies):
    for copy in copies:
        copy.wait()


def whole(shape):
    zeros = (0,) * len(shape)
    return pl.BlockSpec(shape, lambda *_: zeros, pipeline_mode=pl.Buffered(1))


ANY = pl.BlockSpec(memory_space=pl.ANY)
SMEM = pl.BlockSpec(memory_space=pltpu.SMEM)


def params(steps=1):
    return pltpu.CompilerParams(
        dimension_semantics=("arbitrary",) * steps, vmem_limit_bytes=VMEM_LIMIT
    )


MESH = pl.DeviceIdType.MESH

BITS = 4
XYZ, YXZ, ZXY, YZX, XZY, ZYX = (
    (0, 1, 2, 3), (1, 0, 2, 3), (2, 0, 1, 3), (1, 2, 0, 3), (0, 2, 1, 3), (2, 1, 0, 3),
)
GROUP, SPLIT = 4, 3
UNIT = GROUP * D // 2
WIDTH = D // SPLIT
FINAL = UNIT >> BITS


def flip(index, bit):
    size = 1 << bit
    return index + size * (1 - 2 * ((index // size) % 2))


def meet(partners):
    me, core = lax.axis_index("dp"), lax.axis_index("fsdp")
    barrier = pltpu.get_barrier_semaphore()
    pl.semaphore_signal(barrier, inc=1, device_id=(me, 1 - core), device_id_type=MESH)
    for bit in range(partners):
        pl.semaphore_signal(barrier, inc=1, device_id=(flip(me, bit), core), device_id_type=MESH)
    pl.semaphore_wait(barrier, 1 + partners)


def add_rows(target, source, at, other, other_at, rows):
    chunk = FINAL

    def body(i, carry):
        here = pl.ds(pl.multiple_of(at + i * chunk, chunk), chunk)
        there = pl.ds(pl.multiple_of(other_at + i * chunk, chunk), chunk)
        target[here, :] = source[here, :] + other[there, :]
        return carry

    lax.fori_loop(0, rows // chunk, body, 0)


class Sum:
    def __init__(self, kind, orders):
        self.kind, self.orders, self.count = kind, orders, len(orders)
        self.scatters = kind != "gather"
        self.gathers = kind != "scatter"

    def blocks(self):
        return GROUP * self.count // SPLIT

    def out_shapes(self):
        if self.gathers:
            return [jax.ShapeDtypeStruct((self.blocks(), D // 2, D), BF)]
        return [jax.ShapeDtypeStruct((self.count, FINAL, WIDTH), BF)]

    def inputs(self):
        return 2 if self.scatters else 1

    def scratch(self):
        n = self.count
        found = []
        if self.scatters:
            found += [
                pltpu.VMEM((n, UNIT, WIDTH), BF),
                pltpu.VMEM((n, UNIT - FINAL, WIDTH), BF),
                pltpu.VMEM((2, UNIT, WIDTH), BF),
                pltpu.SemaphoreType.DMA((n, 2 * GROUP)),
                pltpu.SemaphoreType.DMA((n, BITS)),
                pltpu.SemaphoreType.DMA((n, BITS)),
            ]
        if self.gathers:
            found += [
                pltpu.VMEM((n, UNIT, WIDTH), BF),
                pltpu.SemaphoreType.DMA((n, GROUP)),
                pltpu.SemaphoreType.DMA((n, BITS)),
                pltpu.SemaphoreType.DMA((n, BITS)),
            ]
        else:
            found += [pltpu.SemaphoreType.DMA((n,))]
        return found

    def bind(self, ins, outs, scratch):
        self.me, self.core = lax.axis_index("dp"), lax.axis_index("fsdp")
        self.ins, self.out = ins, outs[0]
        scratch = list(scratch)
        if self.scatters:
            self.held, self.arrived, self.stage, self.load, self.send, self.recv = scratch[:6]
            scratch = scratch[6:]
        if self.gathers:
            self.final, self.local, self.gsend, self.grecv = scratch
        else:
            self.local = scratch[0]

    def spans(self, unit):
        found, base, size = [], 0, UNIT
        for bit in self.orders[unit]:
            size = size // 2
            side = (self.me // (1 << bit)) % 2
            found.append((base + side * size, base + (1 - side) * size, size))
            base = base + side * size
        return found

    def window(self, ref, unit, side):
        block = GROUP * (unit // SPLIT) + side
        return ref.at[block, :, pl.ds((unit % SPLIT) * WIDTH, WIDTH)]

    def loads(self, unit):
        return [
            pltpu.make_async_copy(
                self.window(source, unit, side),
                target.at[pl.ds(side * (D // 2), D // 2)],
                self.load.at[unit, GROUP * which + side],
            )
            for which, (source, target) in enumerate(
                ((self.ins[0], self.held.at[unit]), (self.ins[1], self.stage.at[unit % 2]))
            )
            for side in range(GROUP)
        ]

    def scatter_copy(self, unit, step):
        _, give, size = self.spans(unit)[step]
        return pltpu.make_async_remote_copy(
            src_ref=self.held.at[unit, pl.ds(pl.multiple_of(give, size), size)],
            dst_ref=self.arrived.at[unit, pl.ds(UNIT - 2 * size, size)],
            send_sem=self.send.at[unit, step], recv_sem=self.recv.at[unit, step],
            device_id=(flip(self.me, self.orders[unit][step]), self.core), device_id_type=MESH,
        )

    def gather_copy(self, unit, step):
        keep, _, size = self.spans(unit)[step]
        place = pl.ds(pl.multiple_of(keep, size), size)
        return pltpu.make_async_remote_copy(
            src_ref=self.final.at[unit, place], dst_ref=self.final.at[unit, place],
            send_sem=self.gsend.at[unit, step], recv_sem=self.grecv.at[unit, step],
            device_id=(flip(self.me, self.orders[unit][step]), self.core), device_id_type=MESH,
        )

    def share_copy(self, unit):
        keep, _, size = self.spans(unit)[BITS - 1]
        place = pl.ds(pl.multiple_of(keep, size), size)
        if self.scatters:
            return pltpu.make_async_copy(self.held.at[unit, place], self.out.at[unit], self.local.at[unit])
        return pltpu.make_async_copy(self.ins[0].at[unit], self.final.at[unit, place], self.local.at[unit, 0])

    def outs(self, unit):
        return [
            pltpu.make_async_copy(
                self.final.at[unit, pl.ds(side * (D // 2), D // 2)],
                self.window(self.out, unit, side),
                self.local.at[unit, side],
            )
            for side in range(GROUP)
        ]

    def prefetch(self):
        if self.scatters:
            for unit in range(min(2, self.count)):
                start_all(self.loads(unit))
        else:
            for unit in range(self.count):
                self.share_copy(unit).start()

    def begin(self):
        if not self.scatters:
            for unit in range(self.count):
                self.share_copy(unit).wait()
                self.gather_copy(unit, BITS - 1).start()
            return
        for unit in range(self.count):
            wait_all(self.loads(unit))
            add_rows(self.held.at[unit], self.held.at[unit], 0, self.stage.at[unit % 2], 0, UNIT)
            self.scatter_copy(unit, 0).start()
            if unit + 2 < self.count:
                start_all(self.loads(unit + 2))

    def stages(self):
        return BITS * (self.scatters + self.gathers)

    def advance(self, unit, stage):
        if self.scatters and stage < BITS:
            self.scatter_copy(unit, stage).wait()
            keep, _, size = self.spans(unit)[stage]
            landing = UNIT - 2 * size
            target = self.final if self.gathers and stage == BITS - 1 else self.held
            add_rows(target.at[unit], self.held.at[unit], keep, self.arrived.at[unit], landing, size)
            if stage < BITS - 1:
                self.scatter_copy(unit, stage + 1).start()
            elif self.gathers:
                self.gather_copy(unit, BITS - 1).start()
            else:
                self.share_copy(unit).start()
            return
        step = BITS - 1 - (stage - BITS * self.scatters)
        self.gather_copy(unit, step).wait()
        if step:
            self.gather_copy(unit, step - 1).start()
        else:
            start_all(self.outs(unit))

    def finish(self):
        for unit in range(self.count):
            if self.gathers:
                wait_all(self.outs(unit))
            else:
                self.share_copy(unit).wait()


def bind_sums(sums, ins, outs, scratch):
    ins, outs, scratch = list(ins), list(outs), list(scratch)
    for one in sums:
        a, b, c = one.inputs(), 1, len(one.scratch())
        one.bind(ins[:a], outs[:b], scratch[:c])
        ins, outs, scratch = ins[a:], outs[b:], scratch[c:]


def run_steps(sums, steps):
    owners = [(one, unit) for one in sums for unit in range(one.count)]
    for unit, stage in steps:
        one, own = owners[unit]
        one.advance(own, stage)


class Pull:
    def __init__(self, shapes):
        self.chunks = [
            (which, down, across)
            for which, (downs, acrosses) in enumerate(shapes)
            for down in range(downs)
            for across in range(acrosses)
        ]
        self.shapes = shapes

    def scratch(self):
        n = len(self.chunks)
        return [
            pltpu.VMEM((3, D // 2, D), F32),
            pltpu.SemaphoreType.DMA((n,)),
            pltpu.SemaphoreType.DMA((n,)),
            pltpu.SemaphoreType.DMA((n,)),
        ]

    def bind(self, layer, sources, targets, scratch):
        self.layer, self.sources, self.targets = layer, sources, targets
        self.stage, self.loads, self.sends, self.recvs = scratch
        self.me, self.core = lax.axis_index("dp"), lax.axis_index("fsdp")

    def load(self, i):
        which, down, across = self.chunks[i]
        layer = self.layer[which]
        return pltpu.make_async_copy(
            self.sources[which].at[layer, pl.ds(down * (D // 2), D // 2), pl.ds(across * D, D)],
            self.stage.at[i % 3],
            self.loads.at[i],
        )

    def place(self, i):
        which, down, across = self.chunks[i]
        half = D // 2
        first = pl.multiple_of(self.core * (self.shapes[which][0] * half) + down * half, half)
        return pl.ds(first, half), pl.ds(across * D, D)

    def push(self, i):
        place = self.targets[self.chunks[i][0]].at[self.place(i)]
        return pltpu.make_async_remote_copy(
            src_ref=place, dst_ref=place, send_sem=self.sends.at[i], recv_sem=self.recvs.at[i],
            device_id=(self.me, 1 - self.core), device_id_type=MESH,
        )

    def begin(self):
        for i in range(min(3, len(self.chunks))):
            self.load(i).start()

    def turn(self, i):
        self.load(i).wait()
        self.targets[self.chunks[i][0]][self.place(i)] = self.stage[i % 3].astype(BF)
        self.push(i).start()
        if i + 3 < len(self.chunks):
            self.load(i + 3).start()

    def of(self, which):
        return [i for i, chunk in enumerate(self.chunks) if chunk[0] == which]

    def arrive(self, which):
        for i in self.of(which):
            self.push(i).wait()


def qkv_kernel(pull, h_ref, gain_ref, mean_ref, source, *refs):
    normed_ref, q_ref, k_ref, v_ref, scale_q_ref, scale_k_ref, full_ref = refs[:7]
    weight, sem = refs[7:9]
    step = pl.program_id(0)
    keep = pltpu.make_async_copy(weight, full_ref, sem)
    load = pltpu.make_async_copy(source, weight, sem)
    if pull:
        pull.bind([0], [source], [weight], refs[9:])

    @pl.when(step == 0)
    def _():
        if pull:
            pull.begin()
            meet(0)
            for i in range(len(pull.chunks)):
                pull.turn(i)
        else:
            load.start()

    unit, _ = normalise(h_ref[...].astype(F32))
    normed = (unit * gain_ref[0:1, :]).astype(BF)
    normed_ref[...] = normed

    @pl.when(step == 0)
    def _():
        if pull:
            pull.arrive(0)
            keep.start()
        else:
            load.wait()

    v_ref[...] = dot(normed, weight[:, 2 * D :]).astype(BF)
    for part, out_ref, scale_ref in ((0, q_ref, scale_q_ref), (1, k_ref, scale_k_ref)):
        raw = dot(normed, weight[:, part * D : (part + 1) * D])
        centred = raw - head_mean(raw, mean_ref[...], exact=True)
        scale = lax.rsqrt(head_mean(centred * centred, mean_ref[...]) + norm_eps)
        out_ref[...] = (centred * scale * gain_ref[2 + part : 3 + part, :]).astype(BF)
        scale_ref[...] = scale.astype(BF)

    if pull:

        @pl.when(step == pl.num_programs(0) - 1)
        def _():
            keep.wait()


def qkv_forward(h, gains, mean_mat, source, fresh, collective_id):
    rows = h.shape[0]
    block = min(512, rows)
    row = lambda width: pl.BlockSpec((block, width), lambda i: (i, 0))
    pull = Pull([(1, 3)]) if fresh else None
    full = [jax.ShapeDtypeStruct((D, 3 * D), BF)]
    results = pl.pallas_call(
        functools.partial(qkv_kernel, pull) if fresh else functools.partial(qkv_plain_kernel),
        name="qkv_forward",
        grid=(rows // block,),
        in_specs=[row(D), whole(gains.shape), whole(mean_mat.shape), ANY],
        out_specs=[row(D)] * 6 + [ANY] * fresh,
        out_shape=[jax.ShapeDtypeStruct((rows, D), BF)] * 6 + full * fresh,
        scratch_shapes=[pltpu.VMEM((D, 3 * D), BF), pltpu.SemaphoreType.DMA]
        + (pull.scratch() if fresh else []),
        compiler_params=remote_params(fresh, collective_id),
    )(h, gains, mean_mat, source)
    return results if fresh else [*results, source]


def qkv_plain_kernel(h_ref, gain_ref, mean_ref, source, *refs):
    qkv_kernel(None, h_ref, gain_ref, mean_ref, source, *refs[:6], source, *refs[6:])


def window_at(block, count):
    return block - 1 + (count - 1 - block) // (count - 1) - block // (count - 1)


def pair_stack(x, low_lanes):
    zero = jnp.zeros_like(x)
    return jnp.concatenate([jnp.where(low_lanes, x, zero), jnp.where(low_lanes, zero, x)], axis=0)


def mix_kernel(
    tile, reach, pull, layer, follow, n_source,
    h_ref, q_ref, k_ref, v_ref, seg_ref, code_ref, gain_ref, *refs,
):
    sources, outs, follows, scratch, pull_scratch = carve(
        refs, n_source, 4 + (3 if pull else 0), int(follow), 4 + int(follow), len(refs)
    )
    attended_ref, middle_ref, before_ref, out_ref = outs[:4]
    proj, up, down, sems = scratch[:4]
    weights = (proj, up, down)
    if pull:
        targets = list(weights) + ([scratch[4]] if follow else [])
        pull.bind([layer] * 3 + [layer + 1] * follow, sources, targets, pull_scratch)
        keeps = [
            pltpu.make_async_copy(weight, full, sems.at[i])
            for i, (weight, full) in enumerate(zip(targets, outs[4:] + follows))
        ]
    else:
        loads = [
            pltpu.make_async_copy(source, weight, sems.at[i])
            for i, (source, weight) in enumerate(zip(sources, weights))
        ]
    step = pl.program_id(0)
    count = k_ref.shape[0] // tile
    keys = reach * tile
    factor = LOG2E * HEAD_DIM ** (-0.5)
    low_lanes = lax.broadcasted_iota(jnp.int32, (tile, 128), 1) < HEAD_DIM

    @pl.when(step == 0)
    def _():
        if pull:
            pull.begin()
            meet(0)
        else:
            start_all(loads)

    @pl.when(step < count)
    def _():
        first = pl.multiple_of(window_at(step, count) * tile if count > reach else 0, tile)
        window = pl.ds(first, keys)
        here = pl.ds(pl.multiple_of(step * tile, tile), tile)
        seg = seg_ref[here, :]
        code = code_ref[:, window]
        query_at = step * tile + lax.broadcasted_iota(jnp.int32, (tile, keys), 0)
        key_at = first + lax.broadcasted_iota(jnp.int32, (tile, keys), 1)
        bias = jnp.where((seg == code) | (query_at == key_at), 0.0, MASKED)
        bias = jnp.concatenate([bias, bias], axis=0)

        def front(pair):
            lanes = slice(pair * 128, (pair + 1) * 128)
            return dot_nt(pair_stack(q_ref[here, lanes], low_lanes), k_ref[window, lanes])

        following = front(0)
        for pair in range(HEADS // 2):
            lanes = slice(pair * 128, (pair + 1) * 128)
            scores = following
            if pair + 1 < HEADS // 2:
                following = front(pair + 1)
            expo = jnp.exp2(scores * factor + bias)
            total = jnp.sum(expo, axis=-1, keepdims=True)
            mixed = dot(expo.astype(BF), v_ref[window, lanes]) * (1.0 / total)
            attended_ref[here, lanes] = jnp.where(low_lanes, mixed[:tile], mixed[tile:]).astype(BF)

    if pull:
        per_step = -(-len(pull.chunks) // count)
        for turn in range(count):
            mine = range(turn * per_step, min((turn + 1) * per_step, len(pull.chunks)))
            if mine:

                @pl.when(step == turn)
                def _():
                    for i in mine:
                        pull.turn(i)

    @pl.when(step == count)
    def _():
        if pull:
            for which in range(3):
                pull.arrive(which)
                keeps[which].start()
        else:
            wait_all(loads)

    @pl.when(step >= count)
    def _():
        rows = h_ref.shape[0]
        here = pl.ds(pl.multiple_of((step - count) * rows, rows), rows)
        middle = h_ref[...].astype(F32) + dot(attended_ref[here, :], proj[...])
        middle_ref[...] = middle
        unit, _ = normalise(middle)
        normed = (unit * gain_ref[1:2, :]).astype(BF)
        result = middle
        for part in range(up.shape[1] // D):
            lanes = slice(part * D, (part + 1) * D)
            before = dot(normed, up[:, lanes])
            before_ref[:, lanes] = before.astype(BF)
            active = jax.nn.gelu(before, approximate=True).astype(BF)
            result = result + dot(active, down[lanes, :])
        out_ref[...] = result.astype(out_ref.dtype)

    if pull:

        @pl.when(step == pl.num_programs(0) - 1)
        def _():
            if follow:
                pull.arrive(3)
                keeps[3].start()
            wait_all(keeps)


def mix_forward(h, q, k, v, seg, code, gains, sources, out_type, layer, paired, collective_id):
    rows = h.shape[0]
    block = min(512, rows)
    tile = min(128, rows)
    reach = min(3, rows // tile)
    count = rows // tile
    width = sources[1].shape[-1]
    follow = len(sources) > 3
    shapes = [(1, 1), (1, width // D), (width // D, 1)] + [(1, 3)] * follow
    pull = Pull(shapes) if paired else None
    row = lambda w: pl.BlockSpec((block, w), lambda i: (jnp.maximum(i - count, 0), 0))
    outs = [(D, F32), (width, BF), (D, out_type)]
    fulls = [(D, D), (D, width), (width, D)]
    follows = [(D, 3 * D)] * follow
    results = pl.pallas_call(
        functools.partial(mix_kernel, tile, reach, pull, layer, follow, len(sources)),
        name="mix_forward",
        grid=(count + rows // block,),
        in_specs=[row(D)] + [whole(x.shape) for x in (q, k, v, seg, code, gains)] + [ANY] * len(sources),
        out_specs=[pl.BlockSpec((rows, D), lambda i: (0, 0), pipeline_mode=pl.Buffered(1))]
        + [row(w) for w, _ in outs]
        + [ANY] * (len(fulls + follows) if paired else 0),
        out_shape=[jax.ShapeDtypeStruct((rows, D), BF)]
        + [jax.ShapeDtypeStruct((rows, w), t) for w, t in outs]
        + [jax.ShapeDtypeStruct(x, BF) for x in (fulls + follows if paired else [])],
        scratch_shapes=[pltpu.VMEM(x, BF) for x in fulls]
        + [pltpu.SemaphoreType.DMA((4,))]
        + [pltpu.VMEM(x, BF) for x in follows]
        + (pull.scratch() if paired else []),
        compiler_params=remote_params(paired, collective_id),
    )(h, q, k, v, seg, code, gains, *sources)
    return results if paired else [*results, *sources]


class Blocks:
    def __init__(self, count, paired):
        self.count, self.paired = count, paired

    def out_shapes(self):
        rows = D // 2 if self.paired else D
        return [jax.ShapeDtypeStruct((self.count, rows, D), BF)] * (1 + self.paired)

    def scratch(self):
        return [pltpu.SemaphoreType.DMA((self.count,))] * (1 + 2 * self.paired)

    def bind(self, outs, sems):
        self.outs, self.sems = outs, sems

    def copies(self, block, lanes, ref, first_row):
        if not self.paired:
            return [
                pltpu.make_async_copy(
                    ref.at[pl.ds(first_row, D), lanes], self.outs[0].at[block], self.sems[0].at[block]
                )
            ]
        core = lax.axis_index("fsdp")
        half = D // 2
        mine = pl.multiple_of(first_row + core * half, half)
        theirs = pl.multiple_of(first_row + (1 - core) * half, half)
        return [
            pltpu.make_async_copy(
                ref.at[pl.ds(mine, half), lanes], self.outs[0].at[block], self.sems[0].at[block]
            ),
            pltpu.make_async_remote_copy(
                src_ref=ref.at[pl.ds(theirs, half), lanes], dst_ref=self.outs[1].at[block],
                send_sem=self.sems[1].at[block], recv_sem=self.sems[2].at[block],
                device_id=(lax.axis_index("dp"), 1 - core), device_id_type=MESH,
            ),
        ]


def carve(refs, *sizes):
    found, at = [], 0
    for size in sizes:
        found.append(refs[at : at + size])
        at += size
    return found


def sums_in(sums):
    return sum(one.inputs() for one in sums)


def sums_scratch(sums):
    return [shape for one in sums for shape in one.scratch()]


def sums_outs(sums):
    return [shape for one in sums for shape in one.out_shapes()]


def remote_params(paired, collective_id):
    if not paired:
        return params()
    return pltpu.CompilerParams(
        dimension_semantics=("arbitrary",), vmem_limit_bytes=VMEM_LIMIT,
        collective_id=collective_id, has_side_effects=True,
    )


def ffn_back_kernel(blocks, store, sums, plan, dh_ref, before_ref, middle_ref, gain_ref, *refs):
    weights, ins, outs, store_outs, sum_outs, own_scratch, store_sems, sum_scratch = carve(
        refs, 2, sums_in(sums), 2, 1 + store.paired, len(sums), 7, 1 + 2 * store.paired,
        len(sums_scratch(sums)),
    )
    dmid_ref, dgain_ref = outs
    up, down, active, dbefore, dbranch, normed, sems = own_scratch
    store.bind(store_outs, store_sems)
    bind_sums(sums, ins, sum_outs, sum_scratch)
    step = pl.program_id(0)
    copies = [
        pltpu.make_async_copy(source, target, sems.at[i])
        for i, (source, target) in enumerate(zip(weights, (up, down)))
    ]
    parts = up.shape[1] // D
    rows = dh_ref.shape[0]

    @pl.when(step == 0)
    def _():
        start_all(copies)
        dgain_ref[...] = jnp.zeros_like(dgain_ref)
        for one in sums:
            one.prefetch()
        if store.paired:
            meet(BITS if sums else 0)
        for one in sums:
            one.begin()

    @pl.when(step < blocks)
    def _():
        here = pl.ds(pl.multiple_of(step * rows, rows), rows)
        dh = dh_ref[...].astype(F32)
        branch = dh.astype(BF)
        dbranch[here, :] = branch
        gain = gain_ref[1:2, :]
        unit, scale = normalise(middle_ref[...])
        normed[here, :] = (unit * gain).astype(BF)

        @pl.when(step == 0)
        def _():
            wait_all(copies)

        def front(part):
            return dot_nt(branch, down[part * D : (part + 1) * D, :])

        dnormed = jnp.zeros((rows, D), F32)
        early = not sums
        following = front(0) if early else None
        for part in range(parts):
            lanes = slice(part * D, (part + 1) * D)
            dactive = following if early else front(part)
            if early and part + 1 < parts:
                following = front(part + 1)
            value = before_ref[:, lanes].astype(F32)
            root = math.sqrt(2.0 / math.pi)
            square = value * value
            curve = jnp.tanh(value * (root + (root * 0.044715) * square))
            half = 0.5 * (1.0 + curve)
            active[here, lanes] = (value * half).astype(BF)
            slope = half + (0.5 * value) * (1.0 - curve * curve) * (
                root + (3.0 * 0.044715 * root) * square
            )
            dpart = (dactive * slope).astype(BF)
            dbefore[here, lanes] = dpart
            dnormed = dnormed + dot_nt(dpart, up[:, lanes])
            for block in range(blocks):
                if block * parts + part in plan:

                    @pl.when(step == block)
                    def _():
                        run_steps(sums, plan[block * parts + part])

        dmid_ref[...] = dh + norm_back(dnormed, gain, unit, scale)
        dgain_ref[...] += column_sum(dnormed * unit)

    late = blocks * parts - blocks
    for tick in sorted(plan):
        if tick >= blocks * parts:

            @pl.when(step == tick - late)
            def _():
                run_steps(sums, plan[tick])

    every = slice(0, D)

    @pl.when((step >= blocks) & (step < blocks + parts))
    def _():
        part = step - blocks
        lanes = pl.ds(pl.multiple_of(part * D, D), D)
        up[:, lanes] = dot_tn(normed[...], dbefore[:, lanes]).astype(BF)
        start_all(store.copies(part, lanes, up, 0))

    @pl.when(step >= blocks + parts)
    def _():
        part = step - blocks - parts
        half = D // 2
        base = down.shape[0] // 2
        first_row = pl.multiple_of(part * D, D)
        for side in range(2):
            lanes = pl.ds(pl.multiple_of(side * base + part * half, half), half)
            here = pl.ds(pl.multiple_of(first_row + side * half, half), half)
            down[here, :] = dot_tn(active[:, lanes], dbranch[...]).astype(BF)
        start_all(store.copies(parts + part, every, down, first_row))

    @pl.when(step == blocks + 2 * parts - 1)
    def _():
        for part in range(parts):
            wait_all(store.copies(part, slice(part * D, (part + 1) * D), up, 0))
        for part in range(parts):
            wait_all(store.copies(parts + part, every, down, part * D))
        for one in sums:
            one.finish()


def ffn_backward(dh, before, middle, gains, shards, paired, sums, plan, sum_ins, collective_id):
    rows, width = before.shape
    block = min(512, rows)
    blocks = rows // block
    parts = width // D
    store = Blocks(2 * parts, paired)
    row = lambda w, **mode: pl.BlockSpec((block, w), lambda i: (jnp.minimum(i, blocks - 1), 0), **mode)
    once = {"pipeline_mode": pl.Buffered(1)} if sums else {}
    outs = store.out_shapes() + sums_outs(sums)
    return pl.pallas_call(
        functools.partial(ffn_back_kernel, blocks, store, sums, plan),
        name="ffn_backward",
        grid=(blocks + 2 * parts,),
        in_specs=[row(D, **once), row(width), row(D, **once), whole(gains.shape)] + [ANY] * (2 + len(sum_ins)),
        out_specs=[row(D), pl.BlockSpec((8, D), lambda i: (0, 0))] + [ANY] * len(outs),
        out_shape=[jax.ShapeDtypeStruct((rows, D), F32), jax.ShapeDtypeStruct((8, D), F32)] + outs,
        scratch_shapes=[
            pltpu.VMEM((D, width), BF),
            pltpu.VMEM((width, D), BF),
            pltpu.VMEM((rows, width), BF),
            pltpu.VMEM((rows, width), BF),
            pltpu.VMEM((rows, D), BF),
            pltpu.VMEM((rows, D), BF),
            pltpu.SemaphoreType.DMA((2,)),
        ]
        + store.scratch()
        + sums_scratch(sums),
        compiler_params=remote_params(paired, collective_id),
    )(dh, before, middle, gains, *shards, *sum_ins)


def attn_back_kernel(
    tile, reach, rows, store, sums, plan,
    seg_ref, code_ref, gain_ref, heads_ref, mean_ref, *refs,
):
    sources, refs = refs[:8], refs[8:]
    weights, ins, outs, store_outs, sum_outs, own_scratch, store_sems, sum_scratch = carve(
        refs, 3, sums_in(sums), 2, 1 + store.paired, len(sums), 18, 1 + 2 * store.paired,
        len(sums_scratch(sums)),
    )
    normed_ref, qkv_ref, proj_ref = weights
    dh_ref, dgain_ref = outs
    qkv, proj, dattended, inner, dk, dv, dmixed, sems, normed_sem = own_scratch[:9]
    held = own_scratch[9:17]
    dmid_ref, attended_ref, q_ref, k_ref, v_ref, scale_q_ref, scale_k_ref, h_ref = held
    loads = [
        pltpu.make_async_copy(source, target, own_scratch[17].at[i])
        for i, (source, target) in enumerate(zip(sources, held))
    ]
    store.bind(store_outs, store_sems)
    bind_sums(sums, ins, sum_outs, sum_scratch)
    step = pl.program_id(0)
    total_rows = k_ref.shape[0]
    count = total_rows // tile
    keys = reach * tile
    blocks = total_rows // rows
    proj_copy = pltpu.make_async_copy(proj_ref, proj, sems.at[0])
    qkv_copy = pltpu.make_async_copy(qkv_ref, qkv, sems.at[1])
    normed_copy = pltpu.make_async_copy(normed_ref, dattended, normed_sem)
    root = HEAD_DIM ** (-0.5)

    def head_norm_back(grad, gain, unit, scale):
        scaled = grad * gain
        first = head_mean(scaled, mean_ref[...])
        second = head_mean(scaled * unit, mean_ref[...])
        return scale.astype(F32) * (scaled - first - unit * second)

    @pl.when(step == 0)
    def _():
        proj_copy.start()
        start_all(loads)
        qkv_copy.start()
        dgain_ref[...] = jnp.zeros_like(dgain_ref)
        dk[...] = jnp.zeros_like(dk)
        dv[...] = jnp.zeros_like(dv)
        for one in sums:
            one.prefetch()
        if store.paired:
            meet(BITS if sums else 0)
        for one in sums:
            one.begin()
        proj_copy.wait()
        wait_all(loads[:2])
        for block in range(blocks):
            here = slice(block * rows, (block + 1) * rows)
            back = dot_nt(dmid_ref[here, :].astype(BF), proj[...]).astype(BF)
            dattended[here, :] = back
            product = back.astype(F32) * attended_ref[here, :].astype(F32)
            high = product.astype(BF)
            low = (product - high.astype(F32)).astype(BF)
            turn = (((0,), (1,)), ((), ()))
            inner[:, here] = lax.dot_general(
                heads_ref[...], high, turn, preferred_element_type=F32
            ) + lax.dot_general(heads_ref[...], low, turn, preferred_element_type=F32)

        wait_all(loads[2:6])

    for tick in sorted(plan):

        @pl.when(step == tick)
        def _():
            run_steps(sums, plan[tick])

    @pl.when(step < count)
    def _():
        first = pl.multiple_of(window_at(step, count) * tile if count > reach else 0, tile)
        window = pl.ds(first, keys)
        here = pl.ds(pl.multiple_of(step * tile, tile), tile)
        low_lanes = lax.broadcasted_iota(jnp.int32, (tile, 128), 1) < HEAD_DIM
        seg = seg_ref[:, here]
        code = code_ref[window, :]
        key_at = first + lax.broadcasted_iota(jnp.int32, (keys, tile), 0)
        query_at = step * tile + lax.broadcasted_iota(jnp.int32, (keys, tile), 1)
        bias = jnp.where((seg == code) | (query_at == key_at), 0.0, MASKED)
        bias = jnp.concatenate([bias, bias], axis=1)
        dq_parts = []

        def front(pair):
            lanes = slice(pair * 128, (pair + 1) * 128)
            queries = pair_stack(q_ref[here, lanes], low_lanes)
            grads = pair_stack(dattended[here, lanes], low_lanes)
            keys_part = k_ref[window, lanes]
            scores = dot_nt(keys_part, queries)
            return queries, grads, keys_part, scores, dot_nt(v_ref[window, lanes], grads)

        following = front(0)
        for pair in range(HEADS // 2):
            lanes = slice(pair * 128, (pair + 1) * 128)
            queries, grads, keys_part, scores, dprobs = following
            if pair + 1 < HEADS // 2:
                following = front(pair + 1)
            expo = jnp.exp2(scores * (LOG2E * root) + bias)
            probs = expo * (1.0 / jnp.sum(expo, axis=0, keepdims=True))
            less = jnp.concatenate(
                [inner[2 * pair : 2 * pair + 1, here], inner[2 * pair + 1 : 2 * pair + 2, here]],
                axis=1,
            )
            dscores = (probs * (dprobs - less)).astype(BF)
            dv[window, lanes] += dot(probs.astype(BF), grads)
            dk[window, lanes] += dot(dscores, queries)
            dq = dot_tn(dscores, keys_part)
            dq_parts.append(jnp.where(low_lanes, dq[:tile], dq[tile:]))
        dq = jnp.concatenate(dq_parts, axis=1) * root
        gain = gain_ref[2:3, :]
        unit = q_ref[here, :].astype(F32) * (1.0 / gain)
        dmixed[here, 0:D] = head_norm_back(dq, gain, unit, scale_q_ref[here, :]).astype(BF)
        dgain_ref[8:16, :] += column_sum(dq * unit)

    @pl.when(step == count)
    def _():
        normed_copy.start()
        qkv_copy.wait()
        wait_all(loads[6:])

    @pl.when((step >= count) & (step < count + blocks))
    def _():
        here = pl.ds(pl.multiple_of((step - count) * rows, rows), rows)
        grad = dk[here, :] * root
        gain = gain_ref[3:4, :]
        unit = k_ref[here, :].astype(F32) * (1.0 / gain)
        dmixed[here, D : 2 * D] = head_norm_back(grad, gain, unit, scale_k_ref[here, :]).astype(BF)
        dgain_ref[16:24, :] += column_sum(grad * unit)
        dmixed[here, 2 * D :] = dv[here, :].astype(BF)
        dnormed = dot_nt(dmixed[here, :], qkv[...])
        unit, scale = normalise(h_ref[here, :].astype(F32))
        dh_ref[...] = dmid_ref[here, :] + norm_back(dnormed, gain_ref[0:1, :], unit, scale)
        dgain_ref[0:8, :] += column_sum(dnormed * unit)

    @pl.when(step == count + blocks)
    def _():
        normed_copy.wait()

    @pl.when((step >= count + blocks) & (step < count + blocks + 3))
    def _():
        part = step - count - blocks
        lanes = pl.ds(pl.multiple_of(part * D, D), D)
        qkv[:, lanes] = dot_tn(dattended[...], dmixed[:, lanes]).astype(BF)
        start_all(store.copies(part, lanes, qkv, 0))

    every = slice(0, D)

    @pl.when(step == count + blocks + 3)
    def _():
        proj[...] = dot_tn(attended_ref[...], dmid_ref[...].astype(BF)).astype(BF)
        start_all(store.copies(3, every, proj, 0))
        for part in range(3):
            wait_all(store.copies(part, slice(part * D, (part + 1) * D), qkv, 0))
        wait_all(store.copies(3, every, proj, 0))
        for one in sums:
            one.finish()


def attn_backward(
    dmid, h, saved, attended, segs, gains, heads, mean_mat, shards, paired, sums, plan, sum_ins, collective_id
):
    total = h.shape[0]
    rows = min(512, total)
    tile = min(128, total)
    reach = min(3, total // tile)
    count, blocks = total // tile, total // rows
    normed, q, k, v, scale_q, scale_k = saved
    ins = [*segs, gains, heads, mean_mat]
    large = [dmid, attended, q, k, v, scale_q, scale_k, h]
    store = Blocks(4, paired)
    outs = store.out_shapes() + sums_outs(sums)
    return pl.pallas_call(
        functools.partial(attn_back_kernel, tile, reach, rows, store, sums, plan),
        name="attn_backward",
        grid=(count + blocks + 4,),
        in_specs=[whole(x.shape) for x in ins] + [ANY] * (len(large) + 3 + len(sum_ins)),
        out_specs=[
            pl.BlockSpec((rows, D), lambda i: (jnp.clip(i - count, 0, blocks - 1), 0)),
            pl.BlockSpec((24, D), lambda i: (0, 0)),
        ]
        + [ANY] * len(outs),
        out_shape=[jax.ShapeDtypeStruct((total, D), F32), jax.ShapeDtypeStruct((24, D), F32)] + outs,
        scratch_shapes=[
            pltpu.VMEM((D, 3 * D), BF),
            pltpu.VMEM((D, D), BF),
            pltpu.VMEM((total, D), BF),
            pltpu.VMEM((128, total), F32),
            pltpu.VMEM((total, D), F32),
            pltpu.VMEM((total, D), F32),
            pltpu.VMEM((total, 3 * D), BF),
            pltpu.SemaphoreType.DMA((2,)),
            pltpu.SemaphoreType.DMA,
        ]
        + [pltpu.VMEM(x.shape, x.dtype) for x in large]
        + [pltpu.SemaphoreType.DMA((len(large),))]
        + store.scratch()
        + sums_scratch(sums),
        compiler_params=remote_params(paired, collective_id),
    )(*ins, *large, normed, *shards, *sum_ins)


def last_sums_kernel(sums, steps, counts, *refs):
    n_in, n_out = counts
    small, ins = refs[0], refs[1 : 1 + n_in]
    small_total, outs = refs[1 + n_in], refs[2 + n_in : 2 + n_in + n_out]
    small_held, small_arrived, small_send, small_recv = refs[2 + n_in + n_out : 6 + n_in + n_out]
    bind_sums(sums, ins, outs, refs[6 + n_in + n_out :])
    me, core = lax.axis_index("dp"), lax.axis_index("fsdp")
    for one in sums:
        one.prefetch()
    meet(BITS)

    def small_copy(step):
        to = (me, 1 - core) if step == 0 else (flip(me, step - 1), core)
        return pltpu.make_async_remote_copy(
            src_ref=small_held.at[step], dst_ref=small_arrived.at[step],
            send_sem=small_send.at[step], recv_sem=small_recv.at[step],
            device_id=to, device_id_type=MESH,
        )

    small_held[0] = small[...]
    small_copy(0).start()
    for one in sums:
        one.begin()
    each = -(-len(steps) // (BITS + 1))
    for stage in range(BITS + 1):
        run_steps(sums, steps[stage * each : (stage + 1) * each])
        small_copy(stage).wait()
        value = small_held[stage] + small_arrived[stage]
        if stage < BITS:
            small_held[stage + 1] = value
            small_copy(stage + 1).start()
        else:
            small_total[...] = value
    for one in sums:
        one.finish()


def last_sums(sums, steps, small, ins, collective_id):
    vmem = pl.BlockSpec(memory_space=pltpu.VMEM)
    outs = [shape for one in sums for shape in one.out_shapes()]
    return pl.pallas_call(
        functools.partial(last_sums_kernel, sums, steps, (len(ins), len(outs))),
        name="last_sums",
        in_specs=[vmem] + [ANY] * len(ins),
        out_specs=[vmem] + [ANY] * len(outs),
        out_shape=[jax.ShapeDtypeStruct(small.shape, F32)] + outs,
        scratch_shapes=[
            pltpu.VMEM((BITS + 1, *small.shape), F32),
            pltpu.VMEM((BITS + 1, *small.shape), F32),
            pltpu.SemaphoreType.DMA((BITS + 1,)),
            pltpu.SemaphoreType.DMA((BITS + 1,)),
        ]
        + [shape for one in sums for shape in one.scratch()],
        compiler_params=pltpu.CompilerParams(
            collective_id=collective_id, has_side_effects=True, vmem_limit_bytes=VMEM_LIMIT
        ),
    )(small, *ins)


CORRECTION = 1.0 - 0.5**STEP


def adam(weight, first, second, grad, rate, decay):
    first = 0.5 * first + 0.5 * grad
    second = 0.5 * second + 0.5 * grad * grad
    step = first / CORRECTION / (jnp.sqrt(second / CORRECTION) + adam_eps)
    return weight - rate * (step + decay * weight), first, second


def adam_kernel(down, weight_ref, first_ref, second_ref, *refs):
    grad_refs, outs = refs[:-3], refs[-3:]
    half = D // 2
    for layer, grad_ref in enumerate(grad_refs):

        @pl.when(pl.program_id(0) == layer)
        def _():
            for i in range(grad_ref.shape[0]):
                rows = slice(i * half, (i + 1) * half) if down else slice(0, half)
                lanes = slice(0, D) if down else slice(i * D, (i + 1) * D)
                results = adam(
                    weight_ref[0, rows, lanes], first_ref[0, rows, lanes], second_ref[0, rows, lanes],
                    grad_ref[i].astype(F32), D ** (-0.5), 0.1,
                )
                for out, result in zip(outs, results):
                    out[0, rows, lanes] = result


def adam_step(weight, first, second, totals, base):
    layers, rows, width = weight.shape
    half = D // 2
    down = width == D
    blocks = rows * width // (half * D)
    each = 2 if blocks % 2 == 0 and base % 2 == 0 else 1
    steps = blocks // each
    shape = (1, each * half, D) if down else (1, half, each * D)
    part = pl.BlockSpec(shape, (lambda l, i: (l, i, 0)) if down else (lambda l, i: (l, 0, i)))

    def grad_spec(layer):
        def at(l, i):
            inside = jnp.where(l < layer, 0, steps - 1)
            return (base // each + jnp.where(l == layer, i, inside), 0, 0)

        return pl.BlockSpec((each, half, D), at)

    return pl.pallas_call(
        functools.partial(adam_kernel, down),
        name="adam_step",
        grid=(layers, steps),
        in_specs=[part] * 3 + [grad_spec(layer) for layer in range(layers)],
        out_specs=[part] * 3,
        out_shape=[jax.ShapeDtypeStruct(weight.shape, F32)] * 3,
        compiler_params=params(2),
    )(weight, first, second, *totals)


def per_device(dp, fsdp, *args):
    tokens, cotangent, segments, keep_mask = args[:4]
    masters, firsts, seconds = args[4::3], args[5::3], args[6::3]
    packs, length, width = tokens.shape
    layers = masters[0].shape[0]
    paired = (dp, fsdp) == (1 << BITS, 2)
    me = lax.axis_index("fsdp")

    def gather(shard):
        return lax.all_gather(shard.astype(BF), "fsdp", axis=0, tiled=True)

    gains_all = lax.all_gather(masters[4].astype(BF), "fsdp", axis=1, tiled=True).astype(F32)
    gains_all = jnp.pad(gains_all.transpose(0, 2, 1), ((0, 0), (0, 4), (0, 0)))
    channel = np.arange(D) // HEAD_DIM
    heads = (channel[:, None] == np.arange(128)[None, :]).astype(BF)
    mean_mat = ((channel[:256, None] == channel[None, :256]) / HEAD_DIM).astype(BF)
    seg = segments[0]
    code = jnp.where(keep_mask[0] == 1, seg, -1)

    hidden = tokens[0]
    stored, held = [], []
    qkv = masters[0] if paired else gather(masters[0][0])
    for layer in range(layers):
        gains = gains_all[layer]
        last = layer == layers - 1
        fresh = paired and layer == 0
        *saved, qkv = qkv_forward(hidden, gains, mean_mat, qkv, fresh, 2 * layers + 1)
        q, k, v = saved[1:4]
        if paired:
            sources = [masters[kind] for kind in (1, 2, 3)] + ([] if last else [masters[0]])
        else:
            sources = [gather(masters[kind][layer]) for kind in (1, 2, 3)]
        attended, middle, before, result, proj, up, down, *following = mix_forward(
            hidden, q, k, v, seg[:, None], code[None, :], gains, sources, BF if last else F32,
            layer, paired, 2 * layers + 2 + layer,
        )
        stored.append((hidden, saved, attended, middle, before))
        held.append((qkv, proj, up, down))
        hidden = result
        if not last:
            qkv = following[0] if paired else gather(masters[0][layer + 1])
    output = hidden.reshape(tokens.shape)

    made, shared = None, None
    totals = []
    d_hidden = cotangent[0]
    small = [None] * layers
    leaves = [None] * (2 * layers)
    for order, (layer, kind) in enumerate(
        (layer, kind) for layer in reversed(range(layers)) for kind in ("ffn", "attn")
    ):
        qkv, proj, up, down = held[layer]
        gains = gains_all[layer]
        h, saved, attended, middle, before = stored[layer]
        sums, sum_ins = [], []
        if paired and shared is not None:
            sums.append(Sum("gather", shared[1]))
            sum_ins.append(shared[0])
        if paired and made is not None:
            sums.append(Sum("scatter", made[1]))
            sum_ins += made[0]
        plan = PLANS[order - 1] if sums else {}
        if kind == "ffn":
            results = ffn_backward(
                d_hidden, before, middle, gains, (up, down), paired, sums, plan, sum_ins, order
            )
            d_middle, gain_two = results[:2]
        else:
            results = attn_backward(
                d_middle, h, saved, attended, (seg[None, :], code[:, None]), gains, heads, mean_mat,
                (qkv, proj), paired, sums, plan, sum_ins, order,
            )
            d_hidden, gain_rest = results[:2]
            gain_rest = gain_rest.reshape(3, 8, D).sum(1)
            small[layer] = jnp.stack([gain_rest[0], gain_two.sum(0), gain_rest[1], gain_rest[2]])
        results = results[2:]
        leaves[order] = results[0]
        if paired:
            made, results = (results[:2], ORDERS[order]), results[2:]
            if shared is not None:
                totals.append(results[0])
                results = results[1:]
            shared = (results[0], sums[-1].orders) if results else None
    small = jnp.concatenate(small)
    input_grad = d_hidden.reshape(tokens.shape)

    updated = []
    wide = masters[2].shape[2] // D
    if paired:
        sums = [Sum("gather", shared[1]), Sum("both", made[1])]
        small, *rest = last_sums(sums, LAST_STEPS, small, [shared[0], *made[0]], 2 * layers)
        totals += rest
        totals = list(reversed(totals))
        for kind, (which, base) in enumerate(((0, 0), (0, 3), (1, 0), (1, wide))):
            updated.append(
                adam_step(masters[kind], firsts[kind], seconds[kind], totals[which::2], base)
            )
    else:
        small = lax.psum(small, ("dp", "fsdp"))
        leaves = list(reversed(leaves))
        attn, ffn = jnp.stack(leaves[0::2]), jnp.stack(leaves[1::2])
        across = lambda x: x.transpose(0, 2, 1, 3).reshape(layers, D, -1)
        full = (
            across(attn[:, :3]),
            attn[:, 3],
            across(ffn[:, :wide]),
            ffn[:, wide:].reshape(layers, wide, 2, D // 2, D).transpose(0, 2, 1, 3, 4)
            .reshape(layers, wide * D, D),
        )
        for kind in range(4):
            grad = lax.psum_scatter(full[kind], "fsdp", scatter_dimension=1, tiled=True)
            grad = lax.psum(grad, "dp").astype(F32)
            updated.append(adam(masters[kind], firsts[kind], seconds[kind], grad, D ** (-0.5), 0.1))
    small = small.reshape(layers, 4, D).transpose(0, 2, 1)
    share = masters[4].shape[1]
    small = lax.dynamic_slice_in_dim(small, me * share, share, 1)
    updated.append(adam(masters[4], firsts[4], seconds[4], small, 0.5, 0.0))
    return (output, input_grad, *[x for group in updated for x in group])


ORDERS = (
    (XYZ, XZY, YXZ, YXZ, ZXY, ZYX),
    (XZY, YZX, XYZ),
    (XYZ, ZYX, YXZ, YZX, XZY, ZXY),
    (YXZ, XYZ, ZXY),
)
PLANS = (
    {
        4: ((0, 0), (1, 0), (2, 0), (3, 0),),
        5: ((4, 0), (5, 0),),
        6: ((0, 1), (1, 1),),
        8: ((5, 1), (0, 2), (1, 2), (2, 1), (3, 1), (4, 1),),
        9: ((5, 2), (0, 3), (4, 2), (1, 3),),
        10: ((2, 2), (3, 2),),
        11: ((5, 3),),
        12: ((4, 3),),
        13: ((2, 3), (3, 3),),
    },
    {
        2: ((0, 0), (1, 0), (2, 0), (7, 0), (3, 0), (4, 0), (5, 0),),
        3: ((1, 1),),
        4: ((4, 1), (6, 0), (0, 1), (5, 1), (8, 0), (2, 1),),
        5: ((3, 1),),
        6: ((7, 1), (4, 2),),
        7: ((1, 2), (6, 1),),
        8: ((2, 2), (0, 2), (5, 2), (8, 1),),
        9: ((7, 2), (6, 2), (3, 2),),
        13: ((7, 3), (6, 3), (4, 3), (8, 2),),
        15: ((2, 3), (8, 3), (1, 3), (0, 3), (5, 3), (3, 3),),
    },
    {
        0: ((0, 0), (1, 0), (2, 0),),
        3: ((3, 0), (1, 1), (0, 1), (2, 1),),
        4: ((7, 0), (5, 0),),
        5: ((4, 0), (6, 0),),
        6: ((8, 0), (5, 1),),
        7: ((3, 1), (2, 2),),
        8: ((4, 1), (8, 1),),
        9: ((1, 2), (0, 2), (5, 2), (8, 2), (7, 1), (3, 2), (4, 2), (6, 1),),
        10: ((2, 3),),
        12: ((7, 2), (5, 3), (6, 2), (8, 3),),
        13: ((3, 3), (4, 3), (1, 3), (0, 3), (7, 3), (6, 3),),
    },
)
LAST_STEPS = ((0, 0), (1, 0), (6, 0), (2, 0), (7, 0), (3, 0), (4, 0), (5, 0), (0, 1), (1, 1), (2, 1), (3, 1), (6, 1), (4, 1), (5, 1), (2, 2), (7, 1), (8, 0), (5, 2), (6, 2), (0, 2), (1, 2), (8, 1), (3, 2), (7, 2), (6, 3), (8, 2), (4, 2), (0, 3), (2, 3), (7, 3), (6, 4), (8, 3), (3, 3), (7, 4), (4, 3), (8, 4), (6, 5), (8, 5), (7, 5), (5, 3), (1, 3), (6, 6), (7, 6), (8, 6), (6, 7), (7, 7), (8, 7))


def solution(mesh):
    rows = P(("dp", "fsdp"), None, None)
    weight = P(None, "fsdp", None)
    flat = P(("dp", "fsdp"), None)
    return jax.shard_map(
        functools.partial(per_device, mesh.shape["dp"], mesh.shape["fsdp"]),
        mesh=mesh,
        in_specs=(rows, rows, flat, flat) + (weight,) * 15,
        out_specs=(rows, rows) + (weight,) * 15,
        check_vma=False,
    )
```
